32 devices in a mesh: fsdp: 16 (over z, y, core), dp: 2 (over x).
Axes of the slice: x: 2, y: 2, z: 4, core: 2. Of those that a mesh axis runs over, the one named last changes fastest.
Arguments:
- tokens: bfloat16 [32768, 1024], P(('fsdp', 'dp')), may hold values from -6 to 6
- item_start: int32 [32768], P(('fsdp', 'dp')), may hold values from 0 to 896, as said below
- out_grad: bfloat16 [32768, 1024], P(('fsdp', 'dp')), may hold values from -6 to 6
- norm_gains: float32 [2, 1024], replicated, may hold values from 0.5 to 1.5
- norm_shifts: float32 [2, 1024], replicated, may hold values from -1.25 to 1.25
- w_qkv: bfloat16 [1024, 3072], P('fsdp'), may hold values from -0.1875 to 0.1875
- bias_qkv: float32 [3072], replicated, may hold values from -1.25 to 1.25
- w_out: bfloat16 [1024, 1024], P('fsdp'), may hold values from -0.5 to 0.5
- w_fc: bfloat16 [1024, 4096], P('fsdp'), may hold values from -0.1875 to 0.1875
- bias_fc: float32 [4096], replicated, may hold values from -1.75 to 1.75
- w_proj: bfloat16 [4096, 1024], P('fsdp'), may hold values from -0.09375 to 0.09375
- out_biases: float32 [2, 1024], replicated, may hold values from -1.25 to 1.25
- adapters: float32 [4, 1024, 4], replicated, may hold values from -0.3125 to 0.3125
- momentum: float32 [4, 1024, 4], replicated, may hold values from -1280 to 1280
- average: float32 [4, 1024, 4], replicated, may hold values from -0.3125 to 0.3125
Outputs:
- block_out: bfloat16 [32768, 1024], P(('fsdp', 'dp'))
- in_grad: float32 [32768, 1024], P(('fsdp', 'dp'))
- adapter_grad: float32 [4, 1024, 4], replicated
- new_momentum: float32 [4, 1024, 4], replicated
- new_adapters: float32 [4, 1024, 4], replicated
- new_average: float32 [4, 1024, 4], replicated
- adapter_copy: bfloat16 [4, 1024, 4], replicated
The draws below stay inside these ranges and needn't reach their ends.
Inputs may be any that keep to these rules, and one draw needn't show every extreme that they name: `item_start`: each device's 1024 rows are cut into aligned runs of 1024 rows, and each run into items of 1024, 512, 256 or 128 rows at aligned places; every row holds the first row of its item, counted within its device. Every draw has an item of 1024 rows and one of 128 rows.
All inputs are finite; a program needn't handle non-finite values.
Results may differ from the reference program's by a relative error of at most 0.014.
The reference program's roundings to bfloat16 on the way count: a program that leaves them out, or rounds other values in their place, can miss the bound.
Values may be sent and summed in bfloat16 or wider, within the bound.
A program may use at most 256 MiB of HBM per device.

```python
import jax
import jax.numpy as jnp
from jax import lax

MODEL_DIM = 1024
HEADS = 16
FF = 4096
RANK = 4
ITEM_MAX = 1024
TOK_DEV = 1024
TOKENS = 32768


def draw_item_start(key, part):
    keys = jax.random.split(key, 3)
    blocks = TOKENS // ITEM_MAX
    split_whole = jax.random.randint(keys[0], (blocks,), 0, 2)
    split_half = jax.random.randint(keys[1], (blocks, 2), 0, 2)
    split_quarter = jax.random.randint(keys[2], (blocks, 4), 0, 2)
    split_whole = split_whole.at[0].set(0).at[blocks - 1].set(1)
    split_half = split_half.at[blocks - 1, 1].set(1)
    split_quarter = split_quarter.at[blocks - 1, 3].set(1)
    places = jnp.arange(TOKENS, dtype=jnp.int32)
    owner = places // ITEM_MAX
    inside = places % ITEM_MAX
    eighth = inside // (ITEM_MAX // 8)
    extent = jnp.where(split_whole[owner] == 0, ITEM_MAX, jnp.where(split_half[owner, eighth // 4] == 0, ITEM_MAX // 2, jnp.where(split_quarter[owner, eighth // 2] == 0, ITEM_MAX // 4, ITEM_MAX // 8)))
    return (places % TOK_DEV - inside + inside // extent * extent).astype(jnp.int32)


def shard_levels(key, shape, cuts, smallest, top_value):
    factor_of = 1.0
    for position, parts in cuts:
        draws = jax.random.uniform(jax.random.fold_in(jax.random.fold_in(key, 6), position), (parts,), jnp.float32, smallest / len(cuts), top_value / len(cuts))
        factor_of = factor_of * jnp.repeat(jnp.exp(draws), shape[position] // parts).reshape((-1,) + (1,) * (len(shape) - 1 - position))
    return factor_of


def bell_draw(own_key, shape, scale, bound, cuts=(), kind=jnp.bfloat16):
    level = shard_levels(own_key, shape, cuts, -0.22, 0.18) if cuts else 1.0
    entries = jax.random.normal(own_key, shape, jnp.float32) * scale * level
    return jnp.minimum(jnp.maximum(entries, -bound), bound).astype(kind)


def setup_inputs(seed: int = 0) -> dict:
    key_of = jax.random.split(jax.random.key(seed), 16)
    return {
        "tokens": bell_draw(key_of[0], (TOKENS, MODEL_DIM), 1.0, 6.0, ((0, 32),)),
        "item_start": draw_item_start(jax.random.fold_in(key_of[15], 71), 0),
        "out_grad": bell_draw(key_of[2], (TOKENS, MODEL_DIM), 1.0, 6.0, ((0, 32),)),
        "norm_gains": jnp.clip(1.0 + 0.1 * jax.random.normal(key_of[3], (2, MODEL_DIM), jnp.float32), 0.5, 1.5),
        "norm_shifts": bell_draw(key_of[4], (2, MODEL_DIM), 0.2, 1.25, (), jnp.float32),
        "w_qkv": bell_draw(key_of[5], (MODEL_DIM, 3 * MODEL_DIM), MODEL_DIM ** -0.5, 0.1875, ((0, 16),)),
        "bias_qkv": bell_draw(key_of[6], (3 * MODEL_DIM,), 0.2, 1.25, (), jnp.float32),
        "w_out": bell_draw(key_of[7], (MODEL_DIM, MODEL_DIM), (MODEL_DIM // 8) ** -0.5, 0.5, ((0, 16),)),
        "w_fc": bell_draw(key_of[8], (MODEL_DIM, FF), MODEL_DIM ** -0.5, 0.1875, ((0, 16),)),
        "bias_fc": bell_draw(key_of[9], (FF,), 0.3, 1.75, (), jnp.float32),
        "w_proj": bell_draw(key_of[10], (FF, MODEL_DIM), FF ** -0.5, 0.09375, ((0, 16),)),
        "out_biases": bell_draw(key_of[11], (2, MODEL_DIM), 0.2, 1.25, (), jnp.float32),
        "adapters": bell_draw(key_of[12], (4, MODEL_DIM, RANK), 0.05, 0.3125, (), jnp.float32),
        "momentum": bell_draw(key_of[13], (4, MODEL_DIM, RANK), (1.3 * TOKENS ** 0.5), 1280.0, (), jnp.float32),
        "average": bell_draw(key_of[14], (4, MODEL_DIM, RANK), 0.05, 0.3125, (), jnp.float32),
    }


@jax.custom_vjp
def reduced_rows(v):
    return lax.optimization_barrier(v.astype(jnp.bfloat16)).astype(jnp.float32)

@jax.custom_vjp
def reduced_gradient(v):
    return v

def low_keep(v):
    return (reduced_rows(v), None)

def low_pass(kept, grad):
    return (grad,)

def back_keep(v):
    return (v, None)

def back_low(kept, grad):
    return (reduced_rows(grad),)
reduced_rows.defvjp(low_keep, low_pass)
reduced_gradient.defvjp(back_keep, back_low)
query_span = 512
adapter_scale = 8.0
score_scale = 0.125

def matrix_product(left, right):
    return jnp.dot(left, right, precision=lax.Precision.HIGHEST, preferred_element_type=jnp.float32)

def layer_norm(values, gain, shift):
    center = values - lax.optimization_barrier(jnp.mean(values, axis=-1, keepdims=True))
    spread = lax.optimization_barrier(jnp.mean(center * center, axis=-1, keepdims=True))
    return center * lax.rsqrt(spread + 1e-05) * gain + shift

def gelu_tanh(values):
    return 0.5 * values * (1.0 + jnp.tanh(0.7978845608 * (values + 0.044715 * values * values * values)))

def attention(query_rows, keys_all, value_rows_full, starts):
    row_count = query_rows.shape[0]
    head_size = MODEL_DIM // HEADS
    span_rows = min(query_span, row_count)
    blocks = row_count // span_rows
    query_heads = query_rows.reshape(blocks, span_rows, HEADS, head_size)
    key_heads = keys_all.reshape(row_count, HEADS, head_size)
    value_heads = value_rows_full.reshape(row_count, HEADS, head_size)
    columns = jnp.arange(row_count, dtype=jnp.int32)

    @jax.checkpoint
    def one_block(pieces):
        query_block, start_block, row_ids = pieces
        scores = jnp.einsum('qhe,khe->hqk', query_block, key_heads, precision=lax.Precision.HIGHEST) * score_scale
        scores = reduced_gradient(scores)
        visible = (start_block[:, None] <= columns[None, :]) & (columns[None, :] <= row_ids[:, None])
        scores = jnp.where(visible[None], scores, jnp.float32(-1e+30))
        highest = lax.optimization_barrier(jnp.max(scores, axis=-1, keepdims=True))
        raised = jnp.exp(scores - highest)
        probs = raised / lax.optimization_barrier(jnp.sum(raised, axis=-1, keepdims=True))
        return jnp.einsum('hqk,khe->qhe', reduced_rows(probs), value_heads, precision=lax.Precision.HIGHEST)
    row_ids = columns.reshape(blocks, span_rows)
    outputs = lax.map(one_block, (query_heads, starts.reshape(blocks, span_rows), row_ids))
    return outputs.reshape(row_count, MODEL_DIM)

def forward(rows_in, starts, adapt, frozen):
    gains, shifts, wqkv, bqkv, wout, wfc, bfc, wproj, obias = frozen
    normed_one = reduced_rows(layer_norm(rows_in, gains[0], shifts[0]))
    reduced_adapter_pass = reduced_rows(adapt)
    mixed_tokens_full = matrix_product(normed_one, wqkv) + bqkv
    query_down_matrix = reduced_rows(reduced_gradient(matrix_product(normed_one, reduced_adapter_pass[0])))
    value_down_matrix = reduced_rows(reduced_gradient(matrix_product(normed_one, reduced_adapter_pass[2])))
    query_rows = reduced_rows(reduced_gradient(mixed_tokens_full[:, :MODEL_DIM] + adapter_scale * matrix_product(query_down_matrix, reduced_adapter_pass[1].T)))
    keys_all = reduced_rows(reduced_gradient(mixed_tokens_full[:, MODEL_DIM:2 * MODEL_DIM]))
    value_rows_full = reduced_rows(reduced_gradient(mixed_tokens_full[:, 2 * MODEL_DIM:] + adapter_scale * matrix_product(value_down_matrix, reduced_adapter_pass[3].T)))
    attended = reduced_rows(reduced_gradient(attention(query_rows, keys_all, value_rows_full, starts)))
    branch = reduced_gradient(matrix_product(attended, wout) + obias[0])
    middle = rows_in + branch
    normed_two = reduced_rows(layer_norm(middle, gains[1], shifts[1]))
    pre_act = reduced_gradient(matrix_product(normed_two, wfc) + bfc)
    activation = reduced_rows(gelu_tanh(pre_act))
    return middle + matrix_product(activation, wproj) + obias[1]

def reference(tokens, item_start, out_grad, norm_gains, norm_shifts, w_qkv, bias_qkv, w_out, w_fc, bias_fc, w_proj, out_biases, adapters, momentum, average):
    frozen = (norm_gains, norm_shifts, w_qkv.astype(jnp.float32), bias_qkv, w_out.astype(jnp.float32), w_fc.astype(jnp.float32), bias_fc, w_proj.astype(jnp.float32), out_biases)
    groups = TOKENS // TOK_DEV
    inputs_grouped = tokens.astype(jnp.float32).reshape(groups, TOK_DEV, MODEL_DIM)
    cotangents = out_grad.astype(jnp.float32).reshape(groups, TOK_DEV, MODEL_DIM)
    starts_grouped = item_start.astype(jnp.int32).reshape(groups, TOK_DEV)

    def one_group(pieces):
        rows_in, starts, cotangent = pieces

        def local_forward(values_in, adapt):
            return forward(values_in, starts, adapt, frozen)
        result, backward = jax.vjp(local_forward, rows_in, adapters)
        grad_in, grad_adapt = backward(cotangent)
        return (result.astype(jnp.bfloat16), grad_in, grad_adapt)
    outputs, grads_in, grads_adapt = lax.map(one_group, (inputs_grouped, starts_grouped, cotangents))
    adapter_grad = lax.optimization_barrier(jnp.sum(grads_adapt, axis=0))
    new_momentum = 0.9 * momentum + adapter_grad
    step_rate = 0.01 / jnp.sqrt(jnp.float32(TOKENS))
    new_adapters = adapters - step_rate * (adapter_grad + 0.9 * new_momentum)
    new_average = 0.9 * average + 0.1 * new_adapters
    return (outputs.reshape(TOKENS, MODEL_DIM), grads_in.reshape(TOKENS, MODEL_DIM), adapter_grad, new_momentum, new_adapters, new_average, new_adapters.astype(jnp.bfloat16))
```

```python
import functools
import jax, jax.numpy as jnp
from jax import lax
from jax.experimental import pallas as pl
from jax.experimental.pallas import tpu as pltpu
from jax.sharding import PartitionSpec as P
F32=jnp.float32; BF=jnp.bfloat16
T=1024; D=1024; H=16; G=4; GW=256
NEG=-1e30
def nn(a,b): return lax.dot_general(a,b,(((1,),(0,)),((),())),preferred_element_type=F32)
def nt(a,b): return lax.dot_general(a,b,(((1,),(1,)),((),())),preferred_element_type=F32)
def tn(a,b): return lax.dot_general(a,b,(((0,),(0,)),((),())),preferred_element_type=F32)
def lane(shape): return lax.broadcasted_iota(jnp.int32,shape,1)
def row(shape): return lax.broadcasted_iota(jnp.int32,shape,0)
def stats(v):
    mu=jnp.mean(v,axis=-1,keepdims=True); c=v-mu
    rs=lax.rsqrt(jnp.mean(c*c,axis=-1,keepdims=True)+1e-5)
    return c,rs
def parts(x):
    hi=x.astype(BF); r1=x-hi.astype(F32); mid=r1.astype(BF); lo=(r1-mid.astype(F32)).astype(BF)
    return hi.astype(F32),mid.astype(F32),lo.astype(F32)
def key_lanes(starts_row):
    l=lane((T,128)); r=row((T,128))
    return jnp.where(l<8, jnp.where(r>=starts_row,0.0,NEG), jnp.where(l<11,-1.0,0.0)).astype(BF)
def query_lanes(cols):
    l=lane((T,128)); r=row((T,128))
    base=jnp.where(l==lax.shift_right_logical(r,7),1.0,0.0)
    if cols is not None:
        hi,mid,lo=cols
        base=jnp.where(l==8,hi,jnp.where(l==9,mid,jnp.where(l==10,lo,base)))
    return base.astype(BF)
QB=256
def attn_fwd_pair(q,k,v,klanes,qlanes):
    l=lane((T,128))
    q8=q*jnp.asarray(0.125,BF)
    ka=jnp.concatenate([k,klanes],axis=1)
    outs=[];lses=[]
    tri=lane((QB,QB))<=row((QB,QB))
    for h in range(2):
        hm=(l<64) if h==0 else (l>=64)
        qa=jnp.concatenate([jnp.where(hm,q8,jnp.zeros_like(q8)),qlanes],axis=1)
        ob=[];lb=[]
        for i in range(T//QB):
            n=(i+1)*QB
            s=nt(qa[i*QB:(i+1)*QB],ka[:n])
            sd=jnp.where(tri,s[:,n-QB:],NEG)
            s=jnp.concatenate([s[:,:n-QB],sd],axis=1) if i else sd
            m=jnp.max(s,axis=1,keepdims=True)
            e=jnp.exp(s-m)
            tot=jnp.sum(e,axis=1,keepdims=True)
            o=nn(e.astype(BF),v[:n])*(1.0/tot)
            ob.append(o); lb.append(m+jnp.log(tot))
        outs.append(ob); lses.append(lb)
    return outs,lses
def fwd_kernel(x_ref,gain_ref,shift_ref,st_ref,w_ref,b_ref,at_ref,uq_ref,uv_ref,q_ref,k_ref,v_ref,o_ref,lse_ref,r_ref,h1_ref,kl_ref,ql_ref):
    g=pl.program_id(0)
    @pl.when(g==0)
    def _():
        def blk(i,_):
            sl=pl.ds(pl.multiple_of(i*256,256),256)
            c,rs=stats(x_ref[sl,:].astype(F32))
            h1_ref[sl,:]=(c*rs*gain_ref[0:1,:]+shift_ref[0:1,:]).astype(BF)
            r_ref[sl,:]=nt(h1_ref[sl,:],at_ref[...]).astype(BF)
            return 0
        lax.fori_loop(0,4,blk,0)
        kl_ref[...]=key_lanes(st_ref[...])
        ql_ref[...]=query_lanes(None)
        lse_ref[...]=jnp.zeros((T,128),F32)
    for i in range(4):
        sl=pl.ds(i*256,256)
        m=nn(h1_ref[sl,:],w_ref[0])+b_ref[0]
        q_ref[sl,:]=(m[:,:256]+nn(r_ref[sl,:],uq_ref[...])).astype(BF)
        k_ref[sl,:]=m[:,256:512].astype(BF)
        v_ref[sl,:]=(m[:,512:]+nn(r_ref[sl,:],uv_ref[...])).astype(BF)
    for p in range(2):
        cs=slice(p*128,p*128+128)
        outs,lses=attn_fwd_pair(q_ref[:,cs],k_ref[:,cs],v_ref[:,cs],kl_ref[...],ql_ref[...])
        lq=lane((QB,128))
        for i in range(T//QB):
            sl=slice(i*QB,(i+1)*QB)
            o_ref[sl,cs]=jnp.where(lq<64,outs[0][i],outs[1][i]).astype(BF)
            hd=g*4+p*2
            lse_ref[sl,:]=jnp.where(lq==hd,lses[0][i],jnp.where(lq==hd+1,lses[1][i],lse_ref[sl,:]))
VM=pl.BlockSpec(memory_space=pltpu.VMEM)
def fwd_call(x,gain,shift,st,w4,b4,at,uq,uv):
    cb=pl.BlockSpec((T,GW),lambda g:(0,g))
    ub=pl.BlockSpec((16,GW),lambda g:(0,g))
    return pl.pallas_call(fwd_kernel,grid=(G,),
      in_specs=[VM,VM,VM,VM,pl.BlockSpec((1,D,3*GW),lambda g:(g,0,0)),pl.BlockSpec((1,1,3*GW),lambda g:(g,0,0)),VM,ub,ub],
      out_specs=[cb,cb,cb,cb,pl.BlockSpec((T,128),lambda g:(0,0)),pl.BlockSpec((T,16),lambda g:(0,0))],
      out_shape=[jax.ShapeDtypeStruct((T,D),BF)]*4+[jax.ShapeDtypeStruct((T,128),F32),jax.ShapeDtypeStruct((T,16),BF)],
      scratch_shapes=[pltpu.VMEM((T,D),BF),pltpu.VMEM((T,128),BF),pltpu.VMEM((T,128),BF)],
      compiler_params=pltpu.CompilerParams(vmem_limit_bytes=58*2**20),name="attend")(x,gain,shift,st,w4,b4,at,uq,uv)

C0=0.7978845608; C1=0.044715
def mid_kernel(x_ref,o_ref,og_ref,gain_ref,shift_ref,ob_ref,wo_ref,wf_ref,bf_ref,wp_ref,bo_ref,dx2_ref,do_ref,x2_ref,h2_ref,dh_ref):
    j=pl.program_id(0); nj=pl.num_programs(0)
    y_ref=dx2_ref
    RB=256
    @pl.when(j==0)
    def _():
        def blk(i,_):
            sl=pl.ds(pl.multiple_of(i*RB,RB),RB)
            x2=x_ref[sl,:].astype(F32)+nn(o_ref[sl,:],wo_ref[...])+ob_ref[0:1,:]
            x2_ref[sl,:]=x2
            c,rs=stats(x2)
            h2_ref[sl,:]=(c*rs*gain_ref[1:2,:]+shift_ref[1:2,:]).astype(BF)
            y_ref[sl,:]=x2+ob_ref[1:2,:]
            dh_ref[sl,:]=jnp.zeros((RB,D),F32)
            return 0
        lax.fori_loop(0,T//RB,blk,0)
    def blk(i,_):
        sl=pl.ds(pl.multiple_of(i*RB,RB),RB)
        f=nn(h2_ref[sl,:],wf_ref[0])+bf_ref[...]
        f2=f*f
        t=jnp.tanh(C0*(f+C1*(f2*f)))
        hp=0.5*(1.0+t)
        g=(f*hp).astype(BF)
        gp=hp+(0.5*C0)*f*(1.0-t*t)*(1.0+(3*C1)*f2)
        y_ref[sl,:]+=nn(g,wp_ref[...])
        dg=nt(og_ref[sl,:],wp_ref[...])
        df=(dg*gp).astype(BF)
        dh_ref[sl,:]+=nt(df,wf_ref[0])
        return 0
    lax.fori_loop(0,T//RB,blk,0)
    @pl.when(j==nj-1)
    def _():
        def blk(i,_):
            sl=pl.ds(pl.multiple_of(i*RB,RB),RB)
            bo_ref[sl,:]=y_ref[sl,:].astype(BF)
            c,rs=stats(x2_ref[sl,:])
            xh=c*rs
            dy=dh_ref[sl,:]*gain_ref[1:2,:]
            dx2=og_ref[sl,:].astype(F32)+rs*(dy-jnp.mean(dy,axis=-1,keepdims=True)-xh*jnp.mean(dy*xh,axis=-1,keepdims=True))
            dx2_ref[sl,:]=dx2
            do_ref[sl,:]=nt(dx2.astype(BF),wo_ref[...]).astype(BF)
            return 0
        lax.fori_loop(0,T//RB,blk,0)
def mid_call(x,o,og,gain,shift,ob,wo,wf4,bfc,wp):
    nf,_,fw=wf4.shape
    return pl.pallas_call(mid_kernel,grid=(nf,),
      in_specs=[VM]*7+[pl.BlockSpec((1,D,fw),lambda j:(j,0,0)),pl.BlockSpec((1,fw),lambda j:(0,j)),pl.BlockSpec((fw,D),lambda j:(j,0))],
      out_specs=[VM,VM,VM],
      out_shape=[jax.ShapeDtypeStruct((T,D),BF),jax.ShapeDtypeStruct((T,D),F32),jax.ShapeDtypeStruct((T,D),BF)],
      scratch_shapes=[pltpu.VMEM((T,D),F32),pltpu.VMEM((T,D),BF),pltpu.VMEM((T,D),F32)],
      compiler_params=pltpu.CompilerParams(vmem_limit_bytes=60*2**20),name="middle")(x,o,og,gain,shift,ob,wo,wf4,bfc,wp)

def attn_bwd_pair(q,k,v,do,o,lcols,klanes,store,KB=256):
    l=lane((T,128))
    q8=q*jnp.asarray(0.125,BF)
    ka=jnp.concatenate([k,klanes],axis=1)
    vl=jnp.where((l>=8)&(l<11),-1.0,0.0).astype(BF)
    va=jnp.concatenate([v,vl],axis=1)
    prod=do.astype(F32)*o.astype(F32)
    causal=row((KB,KB))<=lane((KB,KB))
    res=[]
    for h in range(2):
        hm=(l<64) if h==0 else (l>=64)
        dcol=jnp.sum(jnp.where(hm,prod,0.0),axis=1,keepdims=True)
        qa=jnp.concatenate([jnp.where(hm,q8,jnp.zeros_like(q8)),query_lanes(parts(lcols[h]))],axis=1)
        hi,mid,lo=parts(dcol)
        dl=jnp.where(l==8,hi,jnp.where(l==9,mid,jnp.where(l==10,lo,0.0))).astype(BF)
        da=jnp.concatenate([jnp.where(hm,do,jnp.zeros_like(do)),dl],axis=1)
        dqs=[None]*(T//KB); dks=[];dvs=[]
        for j in range(T//KB):
            r0=j*KB
            t=nt(ka[r0:r0+KB],qa[r0:])
            td=jnp.where(causal,t[:,:KB],NEG)
            t=jnp.concatenate([td,t[:,KB:]],axis=1) if r0+KB<T else td
            p=jnp.exp(t)
            dvs.append(nn(p.astype(BF),do[r0:]))
            u=nt(va[r0:r0+KB],da[r0:])
            ds=(p*u).astype(BF)
            dks.append(nn(ds,q8[r0:]))
            dq=tn(ds,k[r0:r0+KB])
            for i in range(j,T//KB):
                piece=dq[(i-j)*KB:(i-j+1)*KB]
                dqs[i]=piece if dqs[i] is None else dqs[i]+piece
        res.append((dqs,dks,dvs))
    lk=lane((KB,128))<64
    for i in range(T//KB):
        sl=slice(i*KB,(i+1)*KB)
        store("q",sl,jnp.where(lk,res[0][0][i],res[1][0][i])*0.125)
        store("k",sl,jnp.where(lk,res[0][1][i],res[1][1][i]))
        store("v",sl,jnp.where(lk,res[0][2][i],res[1][2][i]))
def bwd_kernel(x_ref,gain_ref,shift_ref,st_ref,w_ref,at_ref,uq_ref,uv_ref,r_ref,lse_ref,q_ref,k_ref,v_ref,do_ref,o_ref,dx2_ref,ig_ref,ga_ref,kl_ref,dm_ref,dh_ref,dr_ref,gs_ref):
    g=pl.program_id(0)
    @pl.when(g==0)
    def _():
        kl_ref[...]=key_lanes(st_ref[...])
        dr_ref[...]=jnp.zeros((T,16),F32)
    l=lane((T,128))
    for p in range(2):
        cs=slice(p*128,p*128+128)
        hd=g*4+p*2
        lse=lse_ref[...]
        lc=[jnp.sum(jnp.where(l==hd+h,lse,0.0),axis=1,keepdims=True) for h in range(2)]
        def store(kind,sl,val):
            off={"q":0,"k":256,"v":512}[kind]+p*128
            dm_ref[sl,off:off+128]=val.astype(BF)
        attn_bwd_pair(q_ref[:,cs],k_ref[:,cs],v_ref[:,cs],do_ref[:,cs],o_ref[:,cs],lc,kl_ref[...],store)
    dq=dm_ref[:,:256]; dv=dm_ref[:,512:]
    dr_ref[...]+=nt(dq,uq_ref[...])+nt(dv,uv_ref[...])
    ra=row((16,256))
    gu=8.0*(jnp.where((ra>=4)&(ra<8),tn(r_ref[...],dq),0.0)+jnp.where(ra>=12,tn(r_ref[...],dv),0.0))
    gs_ref[:,pl.ds(pl.multiple_of(g*256,256),256)]=gu
    @pl.when(g==0)
    def _():
        for i in range(4):
            sl=slice(i*256,(i+1)*256)
            dh_ref[sl,:]=nt(dm_ref[sl,:],w_ref[0])
    @pl.when(g>0)
    def _():
        for i in range(4):
            sl=slice(i*256,(i+1)*256)
            dh_ref[sl,:]+=nt(dm_ref[sl,:],w_ref[0])
    @pl.when(g==G-1)
    def _():
        def blk(i,_):
            sl=pl.ds(pl.multiple_of(i*256,256),256)
            drb=dr_ref[sl,:].astype(BF)
            dh=dh_ref[sl,:]+nn(drb,at_ref[...])
            c,rs=stats(x_ref[sl,:].astype(F32))
            xh=c*rs
            h1=(xh*gain_ref[0:1,:]+shift_ref[0:1,:]).astype(BF)
            dy=dh*gain_ref[0:1,:]
            ig_ref[sl,:]=dx2_ref[sl,:]+rs*(dy-jnp.mean(dy,axis=-1,keepdims=True)-xh*jnp.mean(dy*xh,axis=-1,keepdims=True))
            gs_ref[...]+=tn(drb,h1)
            return 0
        lax.fori_loop(0,4,blk,0)
        for i in range(4):
            ga_ref[i]=gs_ref[4*i:4*i+4,:]
def bwd_call(x,gain,shift,st,w4,at,uq,uv,r,lse,q,k,v,do,o,dx2):
    cb=pl.BlockSpec((T,GW),lambda g:(0,g))
    ub=pl.BlockSpec((16,GW),lambda g:(0,g))
    return pl.pallas_call(bwd_kernel,grid=(G,),
      in_specs=[VM,VM,VM,VM,pl.BlockSpec((1,D,3*GW),lambda g:(g,0,0)),VM,ub,ub,VM,VM,cb,cb,cb,cb,cb,VM],
      out_specs=[VM,VM],
      out_shape=[jax.ShapeDtypeStruct((T,D),F32),jax.ShapeDtypeStruct((4,4,D),F32)],
      scratch_shapes=[pltpu.VMEM((T,128),BF),pltpu.VMEM((T,768),BF),pltpu.VMEM((T,D),F32),pltpu.VMEM((T,16),F32),pltpu.VMEM((16,D),F32)],
      compiler_params=pltpu.CompilerParams(vmem_limit_bytes=60*2**20),name="back")(x,gain,shift,st,w4,at,uq,uv,r,lse,q,k,v,do,o,dx2)
MESH=pl.DeviceIdType.MESH

def make_gather(A,B,chunks,offs=(0,2,3,5,6)):
    L1a = A>=B
    L1,L2 = (A,B) if L1a else (B,A)
    n=len(chunks)
    def setup():
        f = lax.axis_index("fsdp"); d = lax.axis_index("dp")
        c = lax.rem(f,2); h=lax.div(f,2); b = lax.rem(h,B); a = lax.div(h,B)
        par=lax.rem(d,2); xp = d+1-2*par
        return f,d,a,b,c,par,xp
    def dev(a_,b_,c_,d_):
        return {"fsdp": (a_*B+b_)*2+c_, "dp": d_}
    def run(w_refs,o_refs,S, tick=None):
        f,d,a,b,c,par,xp=setup()
        if L1a:
            l1=lambda k: (lax.rem(a+k,A),b); l2=lambda k:(a,lax.rem(b+k,B));
            l1m=lambda k: (lax.rem(a+A-k,A),b)
        else:
            l1=lambda k: (a,lax.rem(b+k,B)); l2=lambda k:(lax.rem(a+k,A),b)
            l1m=lambda k: (a,lax.rem(b+B-k,B))
        bar=pltpu.get_barrier_semaphore()
        peers=[dev(a,b,1-c,d),dev(a,b,c,xp)]+[dev(*l1(k),c,d) for k in range(1,L1)]+[dev(*l2(k),c,d) for k in range(1,L2)]
        for p in peers: pl.semaphore_signal(bar,inc=1,device_id=p,device_id_type=MESH)
        def view(g,aa,bb,cc,cols):
            ch=chunks[g]; o=o_refs[ch["out"]]
            idx=(ch["osel"],) if ch["osel"] is not None else ()
            return o.at[idx+(aa,bb,cc,pl.ds(ch["r0"],ch["rows"]),cols)]
        def width(g): return sum(w for _,w in chunks[g]["cols"])
        def carried(g):
            ch=chunks[g]; N=width(g); xc=ch["xc"]
            return pl.ds(pl.multiple_of(par*xc,128),N-xc)
        def xsend(g):
            ch=chunks[g]; N=width(g); xc=ch["xc"]
            return pl.ds(pl.multiple_of(par*(N-xc),128),xc)
        def xrecv(g):
            ch=chunks[g]; N=width(g); xc=ch["xc"]
            return pl.ds(pl.multiple_of((1-par)*(N-xc),128),xc)
        loc=[]
        for g in range(n):
            ch=chunks[g]; w=w_refs[ch["src"]]; off=0; lst=[]
            for i,(c0,wd) in enumerate(ch["cols"]):
                cp=pltpu.make_async_copy(w.at[pl.ds(ch["r0"],ch["rows"]),pl.ds(c0,wd)], view(g,a,b,c,pl.ds(off,wd)), S["loc"].at[g,i])
                cp.start(); lst.append(cp); off+=wd
            loc.append(lst)
        pl.semaphore_wait(bar,len(peers))
        def rc(src,dst,ss,rs,to):
            return pltpu.make_async_remote_copy(src_ref=src,dst_ref=dst,send_sem=ss,recv_sem=rs,device_id=to,device_id_type=MESH)
        pend=[]
        st={}
        def stage0(g):
            for cp in loc[g]: cp.wait()
            v=view(g,a,b,c,carried(g)); cps=[]
            for k in range(1,L1):
                cp=rc(v,v,S["zs"].at[g,k-1],S["zr"].at[g,k-1],dev(*l1(k),c,d)); cp.start(); cps.append(cp)
            st[g]=cps; pend.extend(cps)
        def stage1(g):
            for k,cp in enumerate(st[g]):
                cp.wait_recv()
            sl=carried(g)
            v = view(g,slice(None),b,c,sl) if L1a else view(g,a,slice(None),c,sl)
            cps=[]
            for k in range(1,L2):
                cp=rc(v,v,S["ys"].at[g,k-1],S["yr"].at[g,k-1],dev(*l2(k),c,d)); cp.start(); cps.append(cp)
            xs=[]
            for k in range(1,L1):
                aa,bb=l1(k); v=view(g,aa,bb,c,xsend(g))
                cp=rc(v,v,S["x1s"].at[g,k-1],S["x1r"].at[g,k-1],dev(a,b,c,xp)); cp.start(); xs.append(cp)
            st[g]=(cps,xs); pend.extend(cps); pend.extend(xs)
        def stage2(g):
            cps,xs=st[g]; ys=[]
            for k,cp in enumerate(cps,1):
                cp.wait_recv()
            for k,cp in enumerate(cps,1):
                aa,bb=l2(k)
                v = view(g,slice(None),bb,c,xsend(g)) if L1a else view(g,aa,slice(None),c,xsend(g))
                x=rc(v,v,S["x2s"].at[g,k-1],S["x2r"].at[g,k-1],dev(a,b,c,xp)); x.start(); ys.append(x)
            st[g]=(xs,ys); pend.extend(ys)
        def stage3(g):
            xs,ys=st[g]
            for cp in xs+ys: cp.wait_recv()
            v=view(g,slice(None),slice(None),c,pl.ds(0,width(g)))
            cp=rc(v,v,S["cs"].at[g],S["cr"].at[g],dev(a,b,1-c,d)); cp.start(); st[g]=cp; pend.append(cp)
        def stage4(g):
            st[g].wait_recv()
        stages=[stage0,stage1,stage2,stage3,stage4]
        for t in range(n+offs[-1]):
            for s in range(len(stages)):
                g=t-offs[s]
                if 0<=g<n: stages[s](g)
            if tick is not None: tick(t)
        for cp in pend: cp.wait_send()
    sems=dict(loc=(n,max(len(ch["cols"]) for ch in chunks)),zs=(n,L1-1),zr=(n,L1-1),ys=(n,L2-1),yr=(n,L2-1),x1s=(n,L1-1),x1r=(n,L1-1),x2s=(n,L2-1),x2r=(n,L2-1),cs=(n,),cr=(n,))
    return run,sems

def gather_chunks(R,RP,nf=4,qs=2,rs=2):
    ch=[]
    for j in range(G):
        for r in range(qs):
            ch.append(dict(src=0,out=0,osel=j,r0=R//qs*r,rows=R//qs,cols=[(D*p+GW*j,GW) for p in range(3)],xc=GW))
    for r in range(rs):
        ch.append(dict(src=1,out=1,osel=None,r0=R//rs*r,rows=R//rs,cols=[(0,D)],xc=384))
    w_=4*D//nf; r_=RP//nf
    for j in range(nf):
        for r in range(rs):
            ch.append(dict(src=2,out=2,osel=j,r0=R//rs*r,rows=R//rs,cols=[(w_*j,w_)],xc=384))
        for r in range(rs):
            ch.append(dict(src=3,out=3,osel=None,r0=r_*j+r_//rs*r,rows=r_//rs,cols=[(0,D)],xc=384))
    return ch
def gather_call(A,B,wq,wo,wf,wp):
    R=wq.shape[0]; RP=wp.shape[0]
    run,sems=make_gather(A,B,gather_chunks(R,RP),(0,2,3,4,5))
    names=list(sems)
    def body(*refs):
        run(refs[:4],refs[4:8],dict(zip(names,refs[8:])))
    outs=[(G,A,B,2,R,3*GW),(A,B,2,R,D),(4,A,B,2,R,D),(A,B,2,RP,D)]
    hbm=pl.BlockSpec(memory_space=pl.ANY)
    o=pl.pallas_call(body,in_specs=[VM]*4,out_specs=[hbm]*4,out_shape=[jax.ShapeDtypeStruct(s,BF) for s in outs],
      scratch_shapes=[pltpu.SemaphoreType.DMA(s) for s in sems.values()],
      compiler_params=pltpu.CompilerParams(collective_id=0,has_side_effects=True,vmem_limit_bytes=16*2**20),name="gather")(wq,wo,wf,wp)
    return o[0].reshape(G,D,3*GW),o[1].reshape(D,D),o[2].reshape(4,D,D),o[3].reshape(4*D,D)

def sum_kernel(F,DP,g_ref,o_ref,acc_ref,rcv_ref,ss,rs):
    f=lax.axis_index("fsdp"); d=lax.axis_index("dp")
    partners=[]
    for ax,size,me in (("fsdp",F,f),("dp",DP,d)):
        bit=1
        while bit<size:
            other=me+bit-2*bit*lax.rem(lax.div(me,bit),2)
            partners.append({"fsdp":other,"dp":d} if ax=="fsdp" else {"fsdp":f,"dp":other})
            bit*=2
    bar=pltpu.get_barrier_semaphore()
    for p in partners: pl.semaphore_signal(bar,inc=1,device_id=p,device_id_type=MESH)
    pl.semaphore_wait(bar,len(partners))
    acc_ref[0]=g_ref[...]
    cps=[]
    for s,p in enumerate(partners):
        cp=pltpu.make_async_remote_copy(src_ref=acc_ref.at[s],dst_ref=rcv_ref.at[s],send_sem=ss.at[s],recv_sem=rs.at[s],device_id=p,device_id_type=MESH)
        cp.start(); cps.append(cp)
        cp.wait_recv()
        tot=acc_ref[s]+rcv_ref[s]
        if s+1<len(partners): acc_ref[s+1]=tot
        else: o_ref[...]=tot
    for cp in cps: cp.wait_send()
def sum_call(F,DP,g):
    n=(F.bit_length()-1)+(DP.bit_length()-1)
    return pl.pallas_call(functools.partial(sum_kernel,F,DP),in_specs=[VM],out_specs=VM,out_shape=jax.ShapeDtypeStruct(g.shape,F32),
      scratch_shapes=[pltpu.VMEM((n,)+g.shape,F32),pltpu.VMEM((n,)+g.shape,F32),pltpu.SemaphoreType.DMA((n,)),pltpu.SemaphoreType.DMA((n,))],
      compiler_params=pltpu.CompilerParams(collective_id=1,has_side_effects=True),name="total")(g)

def adapters_prep(ad):
    a=ad.astype(BF).transpose(0,2,1)
    at=jnp.concatenate([a[0],a[0],a[2],a[2]],0)
    z=jnp.zeros((4,D),BF); u8=a*jnp.asarray(8,BF)
    uq=jnp.concatenate([u8[1],z,z,z],0); uv=jnp.concatenate([z,z,u8[3],z],0)
    return at,uq,uv
def solution(mesh):
    F=mesh.shape["fsdp"]; DP=mesh.shape["dp"]
    A,B=(F//4,2) if F<=16 else (2,F//4)
    def per_device(tokens,item_start,og,gains,shifts,wqkv,bqkv,wout,wfc,bfc,wproj,ob,adapters,momentum,average):
        b4=bqkv.reshape(3,4,256).transpose(1,0,2).reshape(4,1,768)
        at,uq,uv=adapters_prep(adapters)
        st=jnp.pad(item_start[::128],(0,120)).reshape(1,128)
        w4,wo,wf4,wp=gather_call(A,B,wqkv,wout,wfc,wproj)
        q,k,v,o,lse,r=fwd_call(tokens,gains,shifts,st,w4,b4,at,uq,uv)
        bo,dx2,do=mid_call(tokens,o,og,gains,shifts,ob,wo,wf4,bfc.reshape(1,-1),wp)
        ig,ga=bwd_call(tokens,gains,shifts,st,w4,at,uq,uv,r,lse,q,k,v,do,o,dx2)
        grad=sum_call(F,DP,ga).transpose(0,2,1)
        rate=0.01/jnp.sqrt(jnp.float32(tokens.shape[0]*F*DP))
        mom=0.9*momentum+grad
        new=adapters-rate*(grad+0.9*mom)
        avg=0.9*average+0.1*new
        return bo,ig,grad,mom,new,avg,new.astype(BF)
    rows=P(("fsdp","dp"),None); w=P("fsdp",None); n=P()
    return jax.shard_map(per_device,mesh=mesh,
      in_specs=(rows,P(("fsdp","dp")),rows,n,n,w,n,w,w,n,w,n,n,n,n),out_specs=(rows,rows,n,n,n,n,n),check_vma=False)
```

```python
import functools
import jax, jax.numpy as jnp
from jax import lax
from jax.experimental import pallas as pl
from jax.experimental.pallas import tpu as pltpu
from jax.sharding import PartitionSpec as P
F32=jnp.float32; BF=jnp.bfloat16
T=1024; D=1024; H=16; G=4; GW=256
NEG=-1e30
def nn(a,b): return lax.dot_general(a,b,(((1,),(0,)),((),())),preferred_element_type=F32)
def nt(a,b): return lax.dot_general(a,b,(((1,),(1,)),((),())),preferred_element_type=F32)
def tn(a,b): return lax.dot_general(a,b,(((0,),(0,)),((),())),preferred_element_type=F32)
def lane(shape): return lax.broadcasted_iota(jnp.int32,shape,1)
def row(shape): return lax.broadcasted_iota(jnp.int32,shape,0)
def stats(v):
    mu=jnp.mean(v,axis=-1,keepdims=True); c=v-mu
    rs=lax.rsqrt(jnp.mean(c*c,axis=-1,keepdims=True)+1e-5)
    return c,rs
def parts(x):
    hi=x.astype(BF); r1=x-hi.astype(F32); mid=r1.astype(BF); lo=(r1-mid.astype(F32)).astype(BF)
    return hi.astype(F32),mid.astype(F32),lo.astype(F32)
def key_lanes(starts_row):
    l=lane((T,128)); r=row((T,128))
    return jnp.where(l<8, jnp.where(r>=starts_row,0.0,NEG), jnp.where(l<11,-1.0,0.0)).astype(BF)
def query_lanes(cols):
    l=lane((T,128)); r=row((T,128))
    base=jnp.where(l==lax.shift_right_logical(r,7),1.0,0.0)
    if cols is not None:
        hi,mid,lo=cols
        base=jnp.where(l==8,hi,jnp.where(l==9,mid,jnp.where(l==10,lo,base)))
    return base.astype(BF)
QB=256
VM=pl.BlockSpec(memory_space=pltpu.VMEM)
C0=0.7978845608; C1=0.044715
def attn_bwd_pair(q,k,v,do,o,lcols,klanes,store,KB=256):
    l=lane((T,128))
    q8=q*jnp.asarray(0.125,BF)
    ka=jnp.concatenate([k,klanes],axis=1)
    vl=jnp.where((l>=8)&(l<11),-1.0,0.0).astype(BF)
    va=jnp.concatenate([v,vl],axis=1)
    prod=do.astype(F32)*o.astype(F32)
    causal=row((KB,KB))<=lane((KB,KB))
    res=[]
    for h in range(2):
        hm=(l<64) if h==0 else (l>=64)
        dcol=jnp.sum(jnp.where(hm,prod,0.0),axis=1,keepdims=True)
        qa=jnp.concatenate([jnp.where(hm,q8,jnp.zeros_like(q8)),query_lanes(parts(lcols[h]))],axis=1)
        hi,mid,lo=parts(dcol)
        dl=jnp.where(l==8,hi,jnp.where(l==9,mid,jnp.where(l==10,lo,0.0))).astype(BF)
        da=jnp.concatenate([jnp.where(hm,do,jnp.zeros_like(do)),dl],axis=1)
        dqs=[None]*(T//KB); dks=[];dvs=[]
        for j in range(T//KB):
            r0=j*KB
            t=nt(ka[r0:r0+KB],qa[r0:])
            td=jnp.where(causal,t[:,:KB],NEG)
            t=jnp.concatenate([td,t[:,KB:]],axis=1) if r0+KB<T else td
            p=jnp.exp(t)
            dvs.append(nn(p.astype(BF),do[r0:]))
            u=nt(va[r0:r0+KB],da[r0:])
            ds=(p*u).astype(BF)
            dks.append(nn(ds,q8[r0:]))
            dq=tn(ds,k[r0:r0+KB])
            for i in range(j,T//KB):
                piece=dq[(i-j)*KB:(i-j+1)*KB]
                dqs[i]=piece if dqs[i] is None else dqs[i]+piece
        res.append((dqs,dks,dvs))
    lk=lane((KB,128))<64
    for i in range(T//KB):
        sl=slice(i*KB,(i+1)*KB)
        store("q",sl,jnp.where(lk,res[0][0][i],res[1][0][i])*0.125)
        store("k",sl,jnp.where(lk,res[0][1][i],res[1][1][i]))
        store("v",sl,jnp.where(lk,res[0][2][i],res[1][2][i]))
MESH=pl.DeviceIdType.MESH

NU=12; NC=24; OFFS=(0,2,3,4,5); NT=NC+OFFS[-1]
class Gather:
    def __init__(self,A,B,l_ref,u_ref,S):
        self.A,self.B,self.l,self.u,self.S=A,B,l_ref,u_ref,S
        self.hr=u_ref.shape[4]//2
        f=lax.axis_index("fsdp"); d=lax.axis_index("dp")
        self.d=d; self.c=lax.rem(f,2); h=lax.div(f,2); self.b=lax.rem(h,B); self.a=lax.div(h,B)
        self.par=lax.rem(d,2); self.xp=d+1-2*self.par
        self.long_a=A>=B; self.L1,self.L2=(A,B) if A>=B else (B,A)
        self.xc=384
    def dev(self,a,b,c,d): return {"fsdp":(a*self.B+b)*2+c,"dp":d}
    def along_a(self,k): return lax.rem(self.a+k,self.A),self.b
    def along_b(self,k): return self.a,lax.rem(self.b+k,self.B)
    def l1(self,k): return self.along_a(k) if self.long_a else self.along_b(k)
    def l2(self,k): return self.along_b(k) if self.long_a else self.along_a(k)
    def peers(self):
        me=(self.a,self.b)
        return [self.dev(*me,1-self.c,self.d),self.dev(*me,self.c,self.xp)]+[self.dev(*self.l1(k),self.c,self.d) for k in range(1,self.L1)]+[self.dev(*self.l2(k),self.c,self.d) for k in range(1,self.L2)]
    def greet(self):
        self.bar=pltpu.get_barrier_semaphore()
        for p in self.peers(): pl.semaphore_signal(self.bar,inc=1,device_id=p,device_id_type=MESH)
    def greeted(self): pl.semaphore_wait(self.bar,len(self.peers()))
    def rows(self,g): return lax.div(g,2),pl.ds(pl.multiple_of(lax.rem(g,2)*self.hr,8),self.hr)
    def view(self,g,a,b,c,cols):
        u,r=self.rows(g)
        return self.u.at[u,a,b,c,r,cols]
    def carried(self): return pl.ds(pl.multiple_of(self.par*self.xc,128),D-self.xc)
    def crossed(self): return pl.ds(pl.multiple_of(self.par*(D-self.xc),128),self.xc)
    def own(self,g):
        u,r=self.rows(g)
        return pltpu.make_async_copy(self.l.at[u,r],self.view(g,self.a,self.b,self.c,slice(None)),self.S["loc"].at[g])
    def rc(self,src,dst,name,idx,to):
        return pltpu.make_async_remote_copy(src_ref=src,dst_ref=dst,send_sem=self.S[name+"s"].at[idx],recv_sem=self.S[name+"r"].at[idx],device_id=to,device_id_type=MESH)
    def zs(self,g):
        u,r=self.rows(g); s=self.l.at[u,r,self.carried()]; t=self.view(g,self.a,self.b,self.c,self.carried())
        return [self.rc(s,t,"z",(g,k-1),self.dev(*self.l1(k),self.c,self.d)) for k in range(1,self.L1)]
    def line(self,g,k,cols):
        a,b=self.l2(k) if k else (self.a,self.b)
        return self.view(g,slice(None),b,self.c,cols) if self.long_a else self.view(g,a,slice(None),self.c,cols)
    def ys(self,g):
        v=self.line(g,0,self.carried())
        return [self.rc(v,v,"y",(g,k-1),self.dev(*self.l2(k),self.c,self.d)) for k in range(1,self.L2)]
    def xs(self,g):
        to=self.dev(self.a,self.b,self.c,self.xp); out=[]
        for k in range(1,self.L1):
            v=self.view(g,*self.l1(k),self.c,self.crossed()); out.append(self.rc(v,v,"x",(g,k-1),to))
        return out
    def ws(self,g):
        to=self.dev(self.a,self.b,self.c,self.xp); out=[]
        for k in range(1,self.L2):
            v=self.line(g,k,self.crossed()); out.append(self.rc(v,v,"w",(g,k-1),to))
        return out
    def cs(self,g):
        v=self.view(g,slice(None),slice(None),self.c,slice(None))
        return [self.rc(v,v,"c",(g,),self.dev(self.a,self.b,1-self.c,self.d))]
    def stage(self,s,g):
        if s==0:
            self.own(g).start()
            for cp in self.zs(g): cp.start()
        elif s==1:
            for cp in self.zs(g): cp.wait_recv()
            self.own(g).wait()
            for cp in self.ys(g)+self.xs(g): cp.start()
        elif s==2:
            for cp in self.ys(g): cp.wait_recv()
            for cp in self.ws(g): cp.start()
        elif s==3:
            for cp in self.xs(g)+self.ws(g): cp.wait_recv()
            for cp in self.cs(g): cp.start()
        else:
            for cp in self.cs(g): cp.wait_recv()
    def tick(self,t):
        for s,o in enumerate(OFFS):
            if isinstance(t,int):
                if 0<=t-o<NC: self.stage(s,jnp.int32(t-o))
            else:
                @pl.when((t-o>=0)&(t-o<NC))
                def _(s=s,o=o): self.stage(s,t-o)
    def finish(self):
        def done(g,_):
            for cp in self.zs(g)+self.ys(g)+self.xs(g)+self.ws(g)+self.cs(g): cp.wait_send()
            return 0
        lax.fori_loop(0,NC,done,0)
    @staticmethod
    def sems(A,B):
        L1,L2=max(A,B),min(A,B); s={"loc":(NC,)}
        for n,k in (("z",L1-1),("y",L2-1),("x",L1-1),("w",L2-1)):
            s[n+"s"]=(NC,k); s[n+"r"]=(NC,k)
        s["cs"]=(NC,); s["cr"]=(NC,)
        return {n:pltpu.SemaphoreType.DMA(v) for n,v in s.items()}

def attn_fwd_head(q8,k,v,klanes,qlanes,h,put):
    l=lane((T,128))
    hm=(l<64) if h==0 else (l>=64)
    qa=jnp.concatenate([jnp.where(hm,q8,jnp.zeros_like(q8)),qlanes],axis=1)
    ka=jnp.concatenate([k,klanes],axis=1)
    tri=lane((QB,QB))<=row((QB,QB))
    for i in range(T//QB):
        n=(i+1)*QB
        s=nt(qa[i*QB:(i+1)*QB],ka[:n])
        sd=jnp.where(tri,s[:,n-QB:],NEG)
        s=jnp.concatenate([s[:,:n-QB],sd],axis=1) if i else sd
        m=jnp.max(s,axis=1,keepdims=True)
        e=jnp.exp(s-m)
        tot=jnp.sum(e,axis=1,keepdims=True)
        put(i,nn(e.astype(BF),v[:n])*(1.0/tot),m+jnp.log(tot))

def forward_kernel(A,B,sem_names,x_ref,og_ref,st_ref,gain_ref,shift_ref,ob_ref,b3_ref,bf_ref,at_ref,uu_ref,wq_ref,wo_ref,wf_ref,wp_ref,
                   u_ref,qkv_out,o_out,lse_ref,r_ref,bo_out,dx2_out,do_out,
                   l_ref,h1_ref,qkv_ref,o_ref,x2_ref,h2_ref,y_ref,dh_ref,kl_ref,ql_ref,wb_ref,wout_ref,bo_ref,do_ref,wsem,osem,*sems):
    G_=Gather(A,B,l_ref,u_ref,dict(zip(sem_names,sems)))
    R=wq_ref.shape[0]
    G_.greet()
    for p in range(8):
        for i in range(3):
            c0=384*p+128*i
            l_ref[c0//1024,:,c0%1024:c0%1024+128]=wq_ref[:,1024*i+128*p:1024*i+128*p+128]
    G_.greeted()
    G_.tick(0); G_.tick(1)
    l_ref[3]=wo_ref[...]
    for j in range(4):
        l_ref[5+2*j]=wp_ref[R*j:R*j+R,:]
    fw=R; S_=D//fw
    half=lane((R,128))<64
    for j in range(4):
        for t in range(8):
            if R==64:
                p0=wf_ref[:,512*t+128*(j//2):512*t+128*(j//2)+128]; p1=wf_ref[:,512*t+256+128*(j//2):512*t+256+128*(j//2)+128]
                ps=[p0,p1]
                f=[x.astype(F32) for x in ps]
                if j%2==0: v=jnp.where(half,f[0],pltpu.roll(f[1],64,1))
                else: v=jnp.where(half,pltpu.roll(f[0],64,1),f[1])
            else:
                f=[wf_ref[:,512*t+128*i:512*t+128*i+128].astype(F32) for i in range(4)]
                ln=lane((R,128)); v=None
                for i in range(4):
                    sh=(32*i-32*j)%128
                    x=pltpu.roll(f[i],sh,1) if sh else f[i]
                    v=x if v is None else jnp.where((ln>=32*i)&(ln<32*i+32),x,v)
            l_ref[4+2*j,:,128*t:128*t+128]=v.astype(BF)
    G_.tick(2)
    def ln0(i,_):
        sl=pl.ds(pl.multiple_of(i*256,256),256)
        c,rs=stats(x_ref[sl,:].astype(F32))
        h1_ref[sl,:]=(c*rs*gain_ref[0:1,:]+shift_ref[0:1,:]).astype(BF)
        r_ref[sl,:]=nt(h1_ref[sl,:],at_ref[...]).astype(BF)
        return 0
    lax.fori_loop(0,2,ln0,0)
    G_.tick(3)
    lax.fori_loop(2,4,ln0,0)
    kl_ref[...]=key_lanes(st_ref[...])
    ql_ref[...]=query_lanes(None)
    lse_ref[...]=jnp.zeros((T,128),F32)
    for t in (4,5,6): G_.tick(t)
    def load(u,slot): return pltpu.make_async_copy(u_ref.at[u],wb_ref.at[slot],wsem.at[slot])
    def w(slot): return wb_ref[slot].reshape(D,D)
    def out(src,dst,k):
        cp=pltpu.make_async_copy(src,dst,osem.at[k]); cp.start(); return cp
    load(0,0).start()
    G_.tick(7)
    t=8
    pend=[]
    wo_cp=pltpu.make_async_copy(u_ref.at[3],wout_ref,wsem.at[4])
    first=(0,2,5,8)
    for u in range(3):
        load(u,u).wait()
        def mix(i,_,u=u):
            sl=pl.ds(pl.multiple_of(i*256,256),256)
            cs=slice(u*1024,u*1024+1024)
            qkv_ref[sl,cs]=(nn(h1_ref[sl,:],w(u))+(nn(r_ref[sl,:],uu_ref[:,cs])+b3_ref[:,cs])).astype(BF)
            return 0
        lax.fori_loop(0,4,mix,0)
        G_.tick(t); t+=1
        if u<2: load(u+1,u+1).start()
        else: wo_cp.start()
        base=t
        def pair(p,_,u=u,base=base):
            qs=pl.ds(pl.multiple_of(p*384,128),128); ks=pl.ds(pl.multiple_of(p*384+128,128),128); vs=pl.ds(pl.multiple_of(p*384+256,128),128)
            oc=pl.ds(pl.multiple_of(p*128,128),128)
            lq=lane((QB,128))
            for h in range(2):
                q8=qkv_ref[:,qs]*jnp.asarray(0.125,BF)
                def put(i,o,ls,h=h):
                    sl=slice(i*QB,(i+1)*QB)
                    if h==0: o_ref[sl,oc]=o.astype(BF)
                    else: o_ref[sl,oc]=jnp.where(lq<64,o_ref[sl,oc],o.astype(BF))
                    lse_ref[sl,:]=jnp.where(lq==2*p+h,ls,lse_ref[sl,:])
                attn_fwd_head(q8,qkv_ref[:,ks],qkv_ref[:,vs],kl_ref[...],ql_ref[...],h,put)
                if h==0 and u==0: G_.tick(base+p-first[u])
            if u>0: G_.tick(base+p-first[u])
            return 0
        lax.fori_loop(first[u],first[u+1],pair,0)
        t=base+first[u+1]-first[u]
    pend.append(out(qkv_ref,qkv_out,0)); pend.append(out(o_ref,o_out,1))
    load(4,0).start(); load(5,1).start()
    wo_cp.wait()
    RB=256
    def mid0(i,_):
        sl=pl.ds(pl.multiple_of(i*RB,RB),RB)
        x2=x_ref[sl,:].astype(F32)+nn(o_ref[sl,:],wout_ref[...].reshape(D,D))+ob_ref[0:1,:]
        x2_ref[sl,:]=x2
        c,rs=stats(x2)
        h2_ref[sl,:]=(c*rs*gain_ref[1:2,:]+shift_ref[1:2,:]).astype(BF)
        y_ref[sl,:]=x2+ob_ref[1:2,:]
        dh_ref[sl,:]=jnp.zeros((RB,D),F32)
        return 0
    lax.fori_loop(0,T//RB,mid0,0)
    G_.tick(t); t+=1
    base=t
    def chunk(j,_):
        s0=2*lax.rem(j,2); s1=s0+1
        load(4+2*j,s0).wait(); load(5+2*j,s1).wait()
        def blk(i,_):
            sl=pl.ds(pl.multiple_of(i*RB,RB),RB)
            wf=wb_ref[s0].reshape(D,D); wp=wb_ref[s1].reshape(D,D)
            f=nn(h2_ref[sl,:],wf)+bf_ref[pl.ds(j,1),:]
            f2=f*f
            th=jnp.tanh(C0*(f+C1*(f2*f)))
            hp=0.5*(1.0+th)
            g=(f*hp).astype(BF)
            gp=hp+(0.5*C0)*f*(1.0-th*th)*(1.0+(3*C1)*f2)
            y_ref[sl,:]+=nn(g,wp)
            dg=nt(og_ref[sl,:],wp)
            df=(dg*gp).astype(BF)
            dh_ref[sl,:]+=nt(df,wf)
            G_.tick(base+4*j+i)
            @pl.when((i==1)&(j<3))
            def _():
                load(6+2*j,2-s0).start(); load(7+2*j,3-s0).start()
            return 0
        lax.fori_loop(0,T//RB,blk,0)
        return 0
    lax.fori_loop(0,4,chunk,0)
    for i in range(T//RB):
        sl=slice(i*RB,(i+1)*RB)
        bo_ref[sl,:]=y_ref[sl,:].astype(BF)
        pend.append(out(bo_ref.at[sl],bo_out.at[sl],2+3*i))
        c,rs=stats(x2_ref[sl,:])
        xh=c*rs
        dy=dh_ref[sl,:]*gain_ref[1:2,:]
        dx2=og_ref[sl,:].astype(F32)+rs*(dy-jnp.mean(dy,axis=-1,keepdims=True)-xh*jnp.mean(dy*xh,axis=-1,keepdims=True))
        x2_ref[sl,:]=dx2
        pend.append(out(x2_ref.at[sl],dx2_out.at[sl],3+3*i))
        do_ref[sl,:]=nt(dx2.astype(BF),wout_ref[...].reshape(D,D)).astype(BF)
        pend.append(out(do_ref.at[sl],do_out.at[sl],4+3*i))
    for cp in pend: cp.wait()
    G_.finish()
def forward_call(A,B,x,og,st,gain,shift,ob,b3,bf4,at,uu,wq,wo,wf,wp):
    R=wq.shape[0]
    sems=Gather.sems(A,B)
    hbm=pl.BlockSpec(memory_space=pl.ANY)
    sd=jax.ShapeDtypeStruct
    return pl.pallas_call(functools.partial(forward_kernel,A,B,list(sems)),
      in_specs=[VM]*14,
      out_specs=[hbm,hbm,hbm,VM,VM,hbm,hbm,hbm],
      out_shape=[sd((NU,A,B,2,R,D),BF),sd((T,3*D),BF),sd((T,D),BF),sd((T,128),F32),sd((T,16),BF),sd((T,D),BF),sd((T,D),F32),sd((T,D),BF)],
      scratch_shapes=[pltpu.VMEM((NU,R,D),BF),pltpu.VMEM((T,D),BF),pltpu.VMEM((T,3*D),BF),pltpu.VMEM((T,D),BF),pltpu.VMEM((T,D),F32),pltpu.VMEM((T,D),BF),
        pltpu.VMEM((T,D),F32),pltpu.VMEM((T,D),F32),pltpu.VMEM((T,128),BF),pltpu.VMEM((T,128),BF),pltpu.VMEM((4,A,B,2,R,D),BF),pltpu.VMEM((A,B,2,R,D),BF),
        pltpu.VMEM((T,D),BF),pltpu.VMEM((T,D),BF),pltpu.SemaphoreType.DMA((5,)),pltpu.SemaphoreType.DMA((14,))]+list(sems.values()),
      compiler_params=pltpu.CompilerParams(collective_id=0,has_side_effects=True,vmem_limit_bytes=60*2**20),name="front")(x,og,st,gain,shift,ob,b3,bf4,at,uu,wq,wo,wf,wp)

def back_kernel(x_ref,gain_ref,shift_ref,st_ref,w_ref,at_ref,uu_ref,r_ref,lse_ref,qkv_ref,do_ref,o_ref,dx2_ref,bo_in,ig_ref,ga_ref,bo_ref,kl_ref,dm_ref):
    p=pl.program_id(0)
    bo_ref[...]=bo_in[...]
    @pl.when(p==0)
    def _():
        kl_ref[...]=key_lanes(st_ref[...])
    l=lane((T,128))
    lse=lse_ref[...]
    lc=[jnp.sum(jnp.where(l==2*p+h,lse,0.0),axis=1,keepdims=True) for h in range(2)]
    def store(kind,sl,val):
        dm_ref[sl,pl.ds(pl.multiple_of(p*384+{"q":0,"k":128,"v":256}[kind],128),128)]=val.astype(BF)
    attn_bwd_pair(qkv_ref[:,0:128],qkv_ref[:,128:256],qkv_ref[:,256:384],do_ref[...],o_ref[...],lc,kl_ref[...],store)
    @pl.when(p==7)
    def _():
        ga_ref[...]=jnp.zeros((4,4,D),F32)
        def blk(i,_):
            sl=pl.ds(pl.multiple_of(i*256,256),256)
            dm=dm_ref[sl,:]
            drb=nt(dm,uu_ref[...]).astype(BF)
            dh=nn(drb,at_ref[...])
            for u in range(3): dh=dh+nt(dm[:,u*1024:u*1024+1024],w_ref[u].reshape(D,D))
            c,rs=stats(x_ref[sl,:].astype(F32))
            xh=c*rs
            h1=(xh*gain_ref[0:1,:]+shift_ref[0:1,:]).astype(BF)
            dy=dh*gain_ref[0:1,:]
            ig_ref[sl,:]=dx2_ref[sl,:]+rs*(dy-jnp.mean(dy,axis=-1,keepdims=True)-xh*jnp.mean(dy*xh,axis=-1,keepdims=True))
            ga=tn(drb,h1)
            gu=tn(r_ref[sl,:],dm)*8.0
            ga_ref[0]+=ga[0:4]
            ga_ref[2]+=ga[8:12]
            for k in range(8):
                ga_ref[1,:,128*k:128*k+128]+=gu[4:8,384*k:384*k+128]
                ga_ref[3,:,128*k:128*k+128]+=gu[12:16,384*k+256:384*k+384]
            return 0
        lax.fori_loop(0,4,blk,0)
def back_call(x,gain,shift,st,u,at,uu,r,lse,qkv,do,o,dx2,bo):
    pb=lambda wd: pl.BlockSpec((T,wd),lambda p:(0,p))
    sd=jax.ShapeDtypeStruct
    ub=pl.BlockSpec((3,)+u.shape[1:],lambda p:(0,)*len(u.shape),pipeline_mode=pl.Buffered(1))
    return pl.pallas_call(back_kernel,grid=(8,),
      in_specs=[VM,VM,VM,VM,ub,VM,VM,VM,VM,pb(384),pb(128),pb(128),VM,pb(128)],
      out_specs=[VM,VM,pb(128)],
      out_shape=[sd((T,D),F32),sd((4,4,D),F32),sd((T,D),BF)],
      scratch_shapes=[pltpu.VMEM((T,128),BF),pltpu.VMEM((T,3*D),BF)],
      compiler_params=pltpu.CompilerParams(vmem_limit_bytes=60*2**20),name="back")(x,gain,shift,st,u,at,uu,r,lse,qkv,do,o,dx2,bo)

def sum_kernel(F,DP,g_ref,o_ref,acc_ref,rcv_ref,ss,rs):
    f=lax.axis_index("fsdp"); d=lax.axis_index("dp")
    partners=[]
    for ax,size,me in (("fsdp",F,f),("dp",DP,d)):
        bit=1
        while bit<size:
            other=me+bit-2*bit*lax.rem(lax.div(me,bit),2)
            partners.append({"fsdp":other,"dp":d} if ax=="fsdp" else {"fsdp":f,"dp":other})
            bit*=2
    bar=pltpu.get_barrier_semaphore()
    for p in partners: pl.semaphore_signal(bar,inc=1,device_id=p,device_id_type=MESH)
    pl.semaphore_wait(bar,len(partners))
    acc_ref[0]=g_ref[...]
    cps=[]
    for s,p in enumerate(partners):
        cp=pltpu.make_async_remote_copy(src_ref=acc_ref.at[s],dst_ref=rcv_ref.at[s],send_sem=ss.at[s],recv_sem=rs.at[s],device_id=p,device_id_type=MESH)
        cp.start(); cps.append(cp)
        cp.wait_recv()
        tot=acc_ref[s]+rcv_ref[s]
        if s+1<len(partners): acc_ref[s+1]=tot
        else: o_ref[...]=tot
    for cp in cps: cp.wait_send()
def sum_call(F,DP,g):
    n=(F.bit_length()-1)+(DP.bit_length()-1)
    return pl.pallas_call(functools.partial(sum_kernel,F,DP),in_specs=[VM],out_specs=VM,out_shape=jax.ShapeDtypeStruct(g.shape,F32),
      scratch_shapes=[pltpu.VMEM((n,)+g.shape,F32),pltpu.VMEM((n,)+g.shape,F32),pltpu.SemaphoreType.DMA((n,)),pltpu.SemaphoreType.DMA((n,))],
      compiler_params=pltpu.CompilerParams(collective_id=1,has_side_effects=True),name="total")(g)

def adapters_prep(ad):
    a=ad.astype(BF).transpose(0,2,1)
    at=jnp.concatenate([a[0],a[0],a[2],a[2]],0)
    u8=(a*jnp.asarray(8,BF)).reshape(4,4,8,1,128)
    z=jnp.zeros((4,8,1,128),BF)
    top=jnp.concatenate([u8[1],z,z],2); low=jnp.concatenate([z,z,u8[3]],2); none=jnp.concatenate([z,z,z],2)
    return at,jnp.concatenate([top,none,low,none],0).reshape(16,3*D)
def solution(mesh):
    F=mesh.shape["fsdp"]; DP=mesh.shape["dp"]
    A,B=(F//4,2) if F<=16 else (2,F//4)
    def per_device(tokens,item_start,og,gains,shifts,wqkv,bqkv,wout,wfc,bfc,wproj,ob,adapters,momentum,average):
        R=wqkv.shape[0]
        b3=bqkv.reshape(3,8,128).transpose(1,0,2).reshape(1,3*D)
        bf4=bfc.reshape(D//R,4,R).transpose(1,0,2).reshape(4,D)
        at,uu=adapters_prep(adapters)
        st=jnp.pad(item_start[::128],(0,120)).reshape(1,128)
        u,qkv,o,lse,r,bo,dx2,do=forward_call(A,B,tokens,og,st,gains,shifts,ob,b3,bf4,at,uu,wqkv,wout,wfc,wproj)
        ig,ga,bo=back_call(tokens,gains,shifts,st,u,at,uu,r,lse,qkv,do,o,dx2,bo)
        grad=sum_call(F,DP,ga).transpose(0,2,1)
        rate=0.01/jnp.sqrt(jnp.float32(tokens.shape[0]*F*DP))
        mom=0.9*momentum+grad
        new=adapters-rate*(grad+0.9*mom)
        avg=0.9*average+0.1*new
        return bo,ig,grad,mom,new,avg,new.astype(BF)
    rows=P(("fsdp","dp"),None); w=P("fsdp",None); n=P()
    return jax.shard_map(per_device,mesh=mesh,
      in_specs=(rows,P(("fsdp","dp")),rows,n,n,w,n,w,w,n,w,n,n,n,n),out_specs=(rows,rows,n,n,n,n,n),check_vma=False)
```

```python
import functools
import jax, jax.numpy as jnp
from jax import lax
from jax.experimental import pallas as pl
from jax.experimental.pallas import tpu as pltpu
from jax.sharding import PartitionSpec as P
F32=jnp.float32; BF=jnp.bfloat16
T=1024; D=1024; H=16; G=4; GW=256
NEG=-1e30
def nn(a,b): return lax.dot_general(a,b,(((1,),(0,)),((),())),preferred_element_type=F32)
def nt(a,b): return lax.dot_general(a,b,(((1,),(1,)),((),())),preferred_element_type=F32)
def tn(a,b): return lax.dot_general(a,b,(((0,),(0,)),((),())),preferred_element_type=F32)
def lane(shape): return lax.broadcasted_iota(jnp.int32,shape,1)
def row(shape): return lax.broadcasted_iota(jnp.int32,shape,0)
def stats(v):
    mu=jnp.mean(v,axis=-1,keepdims=True); c=v-mu
    rs=lax.rsqrt(jnp.mean(c*c,axis=-1,keepdims=True)+1e-5)
    return c,rs
def parts(x):
    hi=x.astype(BF); r1=x-hi.astype(F32); mid=r1.astype(BF); lo=(r1-mid.astype(F32)).astype(BF)
    return hi.astype(F32),mid.astype(F32),lo.astype(F32)
def key_lanes(starts_row):
    l=lane((T,128)); r=row((T,128))
    return jnp.where(l<8, jnp.where(r>=starts_row,0.0,NEG), jnp.where(l<11,-1.0,0.0)).astype(BF)
def query_lanes(cols):
    l=lane((T,128)); r=row((T,128))
    base=jnp.where(l==lax.shift_right_logical(r,7),1.0,0.0)
    if cols is not None:
        hi,mid,lo=cols
        base=jnp.where(l==8,hi,jnp.where(l==9,mid,jnp.where(l==10,lo,base)))
    return base.astype(BF)
QB=256
VM=pl.BlockSpec(memory_space=pltpu.VMEM)
C0=0.7978845608; C1=0.044715
def attn_bwd_pair(q,k,v,do,o,lcols,klanes,store,KB=256):
    l=lane((T,128))
    q8=q*jnp.asarray(0.125,BF)
    ka=jnp.concatenate([k,klanes],axis=1)
    vl=jnp.where((l>=8)&(l<11),-1.0,0.0).astype(BF)
    va=jnp.concatenate([v,vl],axis=1)
    prod=do.astype(F32)*o.astype(F32)
    causal=row((KB,KB))<=lane((KB,KB))
    res=[]
    for h in range(2):
        hm=(l<64) if h==0 else (l>=64)
        dcol=jnp.sum(jnp.where(hm,prod,0.0),axis=1,keepdims=True)
        qa=jnp.concatenate([jnp.where(hm,q8,jnp.zeros_like(q8)),query_lanes(parts(lcols[h]))],axis=1)
        hi,mid,lo=parts(dcol)
        dl=jnp.where(l==8,hi,jnp.where(l==9,mid,jnp.where(l==10,lo,0.0))).astype(BF)
        da=jnp.concatenate([jnp.where(hm,do,jnp.zeros_like(do)),dl],axis=1)
        dqs=[None]*(T//KB); dks=[];dvs=[]
        for j in range(T//KB):
            r0=j*KB
            t=nt(ka[r0:r0+KB],qa[r0:])
            td=jnp.where(causal,t[:,:KB],NEG)
            t=jnp.concatenate([td,t[:,KB:]],axis=1) if r0+KB<T else td
            p=jnp.exp(t)
            dvs.append(nn(p.astype(BF),do[r0:]))
            u=nt(va[r0:r0+KB],da[r0:])
            ds=(p*u).astype(BF)
            dks.append(nn(ds,q8[r0:]))
            dq=tn(ds,k[r0:r0+KB])
            for i in range(j,T//KB):
                piece=dq[(i-j)*KB:(i-j+1)*KB]
                dqs[i]=piece if dqs[i] is None else dqs[i]+piece
        res.append((dqs,dks,dvs))
    lk=lane((KB,128))<64
    for i in range(T//KB):
        sl=slice(i*KB,(i+1)*KB)
        store("q",sl,jnp.where(lk,res[0][0][i],res[1][0][i])*0.125)
        store("k",sl,jnp.where(lk,res[0][1][i],res[1][1][i]))
        store("v",sl,jnp.where(lk,res[0][2][i],res[1][2][i]))
MESH=pl.DeviceIdType.MESH

NU=12; NC=24; LEAD=3; OFFS=(-LEAD,0,2,4); XC=384
class Gather:
    def __init__(self,A,B,l_ref,u_ref,S):
        self.l,self.u,self.S=l_ref,u_ref,S
        self.hr=u_ref.shape[4]//2
        f=lax.axis_index("fsdp"); d=lax.axis_index("dp")
        self.c=f&1; h=f>>1; self.b=h&(B-1); self.a=h>>(B.bit_length()-1)
        par=d&1
        def dev(a,b,c,e): return {"fsdp":(a*B+b)*2+c,"dp":e}
        self.long_a=A>=B; self.L1,self.L2=(A,B) if A>=B else (B,A)
        def along_a(k): return (self.a+k)&(A-1),self.b
        def along_b(k): return self.a,(self.b+k)&(B-1)
        l1,l2=(along_a,along_b) if self.long_a else (along_b,along_a)
        self.p1=[l1(k) for k in range(1,self.L1)]; self.p2=[l2(k) for k in range(1,self.L2)]
        self.d1=[dev(*p,self.c,d) for p in self.p1]; self.d2=[dev(*p,self.c,d) for p in self.p2]
        self.dx=dev(self.a,self.b,self.c,d+1-2*par); self.dc=dev(self.a,self.b,1-self.c,d)
        self.carried=pl.ds(pl.multiple_of(par*XC,128),D-XC)
        self.crossed=pl.ds(pl.multiple_of(par*(D-XC),128),XC)
        self.peers=[self.dc,self.dx]+self.d1+self.d2
    def greet(self):
        self.bar=pltpu.get_barrier_semaphore()
        for p in self.peers: pl.semaphore_signal(self.bar,inc=1,device_id=p,device_id_type=MESH)
    def greeted(self): pl.semaphore_wait(self.bar,len(self.peers))
    def rows(self,g): return g>>1,pl.ds(pl.multiple_of((g&1)*self.hr,8),self.hr)
    def own(self,lo,hi,k): return pltpu.make_async_copy(self.l.at[lo:hi],self.u.at[lo:hi,self.a,self.b,self.c],self.S["loc"].at[k])
    def rc(self,src,dst,name,g,to):
        return pltpu.make_async_remote_copy(src_ref=src,dst_ref=dst,send_sem=self.S[name+"s"],recv_sem=self.S[name+"r"].at[g],device_id=to,device_id_type=MESH)
    def col(self,b,r,cols,u):
        return self.u.at[u,:,b,self.c,r,cols] if self.long_a else self.u.at[u,b,:,self.c,r,cols]
    def zs(self,g):
        u,r=self.rows(g); s=self.l.at[u,r,self.carried]; t=self.u.at[u,self.a,self.b,self.c,r,self.carried]
        return [self.rc(s,t,"z",g,e) for e in self.d1]
    def ys(self,g):
        u,r=self.rows(g); v=self.col(self.b if self.long_a else self.a,r,self.carried,u)
        return [self.rc(v,v,"y",g,e) for e in self.d2]
    def xs(self,g):
        u,r=self.rows(g); out=[]
        for p in self.p1:
            v=self.u.at[u,p[0],p[1],self.c,r,self.crossed]; out.append(self.rc(v,v,"x",g,self.dx))
        return out
    def ws(self,g):
        u,r=self.rows(g); out=[]
        for p in self.p2:
            v=self.col(p[1] if self.long_a else p[0],r,self.crossed,u); out.append(self.rc(v,v,"w",g,self.dx))
        return out
    def cs(self,g):
        u,r=self.rows(g); v=self.u.at[u,:,:,self.c,r]
        return [self.rc(v,v,"c",g,self.dc)]
    def box(self,name,u,r):
        n1=slice(0,self.L1-1); n2=slice(0,self.L2-1); al=slice(None)
        m={"z":(n1,0,self.carried),"y":(al,n2,self.carried),"x":(n1,0,self.crossed),"w":(al,n2,self.crossed),"c":(al,al,al)}[name]
        i1,i2=(m[0],m[1]) if self.long_a else (m[1],m[0])
        return self.u.at[u,i1,i2,0,r,m[2]]
    def got(self,name,g):
        u,r=self.rows(g); v=self.box(name,u,r)
        self.rc(v,v,name,g,self.dc).wait_recv()
    def stage(self,s,g):
        if s==0:
            for cp in self.zs(g): cp.start()
        elif s==1:
            self.got("z",g)
            for cp in self.ys(g)+self.xs(g): cp.start()
        elif s==2:
            self.got("y",g)
            for cp in self.ws(g): cp.start()
        else:
            self.got("x",g); self.got("w",g)
            for cp in self.cs(g): cp.start()
    def tick(self,t,safe=False):
        for s,o in enumerate(OFFS):
            if isinstance(t,int):
                if (2 if s==3 else 0)<=t-o<NC: self.stage(s,jnp.int32(t-o))
            elif safe: self.stage(s,t-o)
            else:
                @pl.when(t-o<NC)
                def _(s=s,o=o): self.stage(s,t-o)
    def ready(self,u):
        self.got("c",2*u); self.got("c",2*u+1)
    def finish(self):
        for n in "zyxwc":
            v=self.box(n,slice(None),slice(None))
            self.rc(v,v,n,0,self.dc).wait_send()
    @staticmethod
    def sems(A,B):
        s={"loc":(2,)}
        for n in "zyxwc": s[n+"s"]=(); s[n+"r"]=(NC,)
        return {n:pltpu.SemaphoreType.DMA(v) for n,v in s.items()}

def attn_fwd_head(q8,k,v,klanes,qlanes,h,put):
    l=lane((T,128))
    hm=(l<64) if h==0 else (l>=64)
    qa=jnp.concatenate([jnp.where(hm,q8,jnp.zeros_like(q8)),qlanes],axis=1)
    ka=jnp.concatenate([k,klanes],axis=1)
    tri=lane((QB,QB))<=row((QB,QB))
    for i in range(T//QB):
        n=(i+1)*QB
        s=nt(qa[i*QB:(i+1)*QB],ka[:n])
        sd=jnp.where(tri,s[:,n-QB:],NEG)
        s=jnp.concatenate([s[:,:n-QB],sd],axis=1) if i else sd
        m=jnp.max(s,axis=1,keepdims=True)
        e=jnp.exp(s-m)
        tot=jnp.sum(e,axis=1,keepdims=True)
        put(i,nn(e.astype(BF),v[:n])*(1.0/tot),m+jnp.log(tot))

def spread(piece,R,put):
    for j in range(4):
        for t in range(8):
            if R==64:
                f=[piece(4*t+j//2),piece(4*t+2+j//2)]
                half=lane(f[0].shape)<64
                v=jnp.where(half,f[0],pltpu.roll(f[1],64,1)) if j%2==0 else jnp.where(half,pltpu.roll(f[0],64,1),f[1])
            else:
                v=None
                for i in range(4):
                    x=piece(4*t+i); sh=(32*i-32*j)%128
                    x=pltpu.roll(x,sh,1) if sh else x
                    ln=lane(x.shape)
                    v=x if v is None else jnp.where((ln>=32*i)&(ln<32*i+32),x,v)
            put(j,t,v)
def forward_kernel(A,B,sem_names,*refs):
    ins=refs[:13]; outs=refs[13:26]; own=refs[26:39]; rest=refs[39:]
    (x_ref,og_ref,sr_ref,gain_ref,shift_ref,ob_ref,bq_ref,bfc_ref,ad_ref,wq_ref,wo_ref,wf_ref,wp_ref)=own
    (u_ref,qkv_out,o_out,lse_out,r_out,kl_out,h1_out,at_out,uu_out,bo_out,dx2_out,do_out,_)=outs
    (l_ref,h1_ref,qkv_ref,o_ref,x2_ref,h2_ref,y_ref,dh_ref,kl_ref,ql_ref,wb_ref,wout_ref,bo_ref,do_ref,lse_ref,r_ref,at_ref,uu_ref,b3_ref,bf_ref,
     isem,wsem,osem)=rest[:23]
    sems=rest[23:]
    G_=Gather(A,B,l_ref,u_ref,dict(zip(sem_names,sems)))
    R=wq_ref.shape[0]
    cin=[pltpu.make_async_copy(a,b,isem.at[i]) for i,(a,b) in enumerate(zip(ins,own))]
    X,OG,SR,GN,SH,OB,BQ,BF_,AD,WQ,WO,WF,WP=range(13)
    for i in (WQ,X,GN,SH,AD,WO,WP,WF,SR,BQ,BF_,OB,OG): cin[i].start()
    G_.greet()
    cin[WQ].wait()
    for p in range(8):
        for i in range(3):
            c0=384*p+128*i
            l_ref[c0//1024,:,c0%1024:c0%1024+128]=wq_ref[:,1024*i+128*p:1024*i+128*p+128]
    G_.greeted()
    for g in range(LEAD): G_.stage(0,jnp.int32(g))
    G_.own(0,3,0).start()
    for i in (X,GN,SH,AD): cin[i].wait()
    a=[ad_ref[i].astype(BF).astype(F32) for i in range(4)]
    z=jnp.zeros((4,D),F32)
    at_ref[...]=jnp.concatenate([a[0],a[0],a[2],a[2]],0).astype(BF)
    uq=jnp.concatenate([8.0*a[1],z,z,z],0).astype(BF); uv=jnp.concatenate([z,z,8.0*a[3],z],0).astype(BF)
    for p in range(8):
        uu_ref[:,384*p:384*p+128]=uq[:,128*p:128*p+128]
        uu_ref[:,384*p+128:384*p+256]=jnp.zeros((16,128),BF)
        uu_ref[:,384*p+256:384*p+384]=uv[:,128*p:128*p+128]
    def ln0(i,_):
        sl=pl.ds(pl.multiple_of(i*256,256),256)
        c,rs=stats(x_ref[sl,:].astype(F32))
        h1_ref[sl,:]=(c*rs*gain_ref[0:1,:]+shift_ref[0:1,:]).astype(BF)
        r_ref[sl,:]=nt(h1_ref[sl,:],at_ref[...]).astype(BF)
        return 0
    lax.fori_loop(0,2,ln0,0)
    G_.own(0,3,0).wait()
    G_.tick(0)
    for i in (WO,WP,WF,SR,BQ,BF_,OB,OG): cin[i].wait()
    l_ref[3]=wo_ref[...]
    for j in range(4): l_ref[5+2*j]=wp_ref[R*j:R*j+R,:]
    def put_w(j,t,v): l_ref[4+2*j,:,128*t:128*t+128]=v.astype(BF)
    spread(lambda k: wf_ref[:,128*k:128*k+128].astype(F32),R,put_w)
    G_.own(3,NU,1).start()
    G_.tick(1)
    lax.fori_loop(2,4,ln0,0)
    G_.tick(2)
    def put_b(j,t,v): bf_ref[j:j+1,128*t:128*t+128]=v[0:1]
    spread(lambda k: jnp.broadcast_to(bfc_ref[k:k+1,:],(8,128)),R,put_b)
    for p in range(8):
        for i in range(3): b3_ref[:,384*p+128*i:384*p+128*i+128]=bq_ref[8*i+p:8*i+p+1,:]
    e8=lane((8,128))==row((8,128))
    s_row=jnp.sum(jnp.where(e8,jnp.broadcast_to(sr_ref[:,0:1],(8,128)),0),axis=0,keepdims=True)
    kl_ref[...]=key_lanes(s_row)
    ql_ref[...]=query_lanes(None)
    lse_ref[...]=jnp.zeros((T,128),F32)
    G_.own(3,NU,1).wait()
    G_.tick(3); G_.stage(3,jnp.int32(0)); G_.tick(4); G_.stage(3,jnp.int32(1))
    def load(u,slot): return pltpu.make_async_copy(u_ref.at[u],wb_ref.at[slot],wsem.at[slot])
    def w(slot): return wb_ref[slot].reshape(D,D)
    def out(src,dst,k):
        cp=pltpu.make_async_copy(src,dst,osem.at[k]); cp.start(); return cp
    pend=[out(r_ref,r_out,14),out(kl_ref,kl_out,15),out(h1_ref,h1_out,16),out(at_ref,at_out,17),out(uu_ref,uu_out,18)]
    G_.ready(0); load(0,0).start()
    t=5
    wo_cp=pltpu.make_async_copy(u_ref.at[3],wout_ref,wsem.at[4])
    first=(0,2,5,8)
    for u in range(3):
        load(u,u).wait()
        def mix(i,_,u=u):
            sl=pl.ds(pl.multiple_of(i*256,256),256)
            cs=slice(u*1024,u*1024+1024)
            qkv_ref[sl,cs]=(nn(h1_ref[sl,:],w(u))+(nn(r_ref[sl,:],uu_ref[:,cs])+b3_ref[:,cs])).astype(BF)
            return 0
        lax.fori_loop(0,4,mix,0)
        G_.tick(t); t+=1
        def pair(p,_,u=u,base=t):
            qs=pl.ds(pl.multiple_of(p*384,128),128); ks=pl.ds(pl.multiple_of(p*384+128,128),128); vs=pl.ds(pl.multiple_of(p*384+256,128),128)
            oc=pl.ds(pl.multiple_of(p*128,128),128)
            lq=lane((QB,128))
            for h in range(2):
                q8=qkv_ref[:,qs]*jnp.asarray(0.125,BF)
                def put(i,o,ls,h=h):
                    sl=slice(i*QB,(i+1)*QB)
                    if h==0: o_ref[sl,oc]=o.astype(BF)
                    else: o_ref[sl,oc]=jnp.where(lq<64,o_ref[sl,oc],o.astype(BF))
                    lse_ref[sl,:]=jnp.where(lq==2*p+h,ls,lse_ref[sl,:])
                attn_fwd_head(q8,qkv_ref[:,ks],qkv_ref[:,vs],kl_ref[...],ql_ref[...],h,put)
            G_.tick(base+p-first[u],True)
            return 0
        lax.fori_loop(first[u],first[u+1]-1,pair,0)
        if u==1: G_.ready(2); load(2,2).start()
        elif u==2: G_.ready(3); wo_cp.start()
        lax.fori_loop(first[u+1]-1,first[u+1],pair,0)
        if u==0: G_.ready(1); load(1,1).start()
        t+=first[u+1]-first[u]
    pend+=[out(qkv_ref,qkv_out,0),out(o_ref,o_out,1),out(lse_ref,lse_out,19)]
    wo_cp.wait()
    RB=256
    def mid0(i,_):
        sl=pl.ds(pl.multiple_of(i*RB,RB),RB)
        x2=x_ref[sl,:].astype(F32)+nn(o_ref[sl,:],wout_ref[...].reshape(D,D))+ob_ref[0:1,:]
        x2_ref[sl,:]=x2
        c,rs=stats(x2)
        h2_ref[sl,:]=(c*rs*gain_ref[1:2,:]+shift_ref[1:2,:]).astype(BF)
        y_ref[sl,:]=x2+ob_ref[1:2,:]
        dh_ref[sl,:]=jnp.zeros((RB,D),F32)
        return 0
    lax.fori_loop(0,T//RB-1,mid0,0)
    G_.ready(4); load(4,0).start()
    lax.fori_loop(T//RB-1,T//RB,mid0,0)
    G_.tick(t); t+=1
    G_.ready(5); load(5,1).start()
    base=t
    def chunk(j,_):
        s0=2*lax.rem(j,2); s1=s0+1
        load(4+2*j,s0).wait(); load(5+2*j,s1).wait()
        def blk(i,_):
            sl=pl.ds(pl.multiple_of(i*RB,RB),RB)
            wf=wb_ref[s0].reshape(D,D); wp=wb_ref[s1].reshape(D,D)
            f=nn(h2_ref[sl,:],wf)+bf_ref[pl.ds(j,1),:]
            f2=f*f
            th=jnp.tanh(C0*(f+C1*(f2*f)))
            hp=0.5*(1.0+th)
            g=(f*hp).astype(BF)
            gp=hp+(0.5*C0)*f*(1.0-th*th)*(1.0+(3*C1)*f2)
            y_ref[sl,:]+=nn(g,wp)
            dg=nt(og_ref[sl,:],wp)
            df=(dg*gp).astype(BF)
            dh_ref[sl,:]+=nt(df,wf)
            G_.tick(base+4*j+i)
            @pl.when((i==2)&(j<3))
            def _():
                G_.ready(6+2*j); load(6+2*j,2-s0).start(); G_.ready(7+2*j); load(7+2*j,3-s0).start()
            return 0
        lax.fori_loop(0,T//RB,blk,0)
        return 0
    lax.fori_loop(0,4,chunk,0)
    for i in range(T//RB):
        sl=slice(i*RB,(i+1)*RB)
        bo_ref[sl,:]=y_ref[sl,:].astype(BF)
        pend.append(out(bo_ref.at[sl],bo_out.at[sl],2+3*i))
        c,rs=stats(x2_ref[sl,:])
        xh=c*rs
        dy=dh_ref[sl,:]*gain_ref[1:2,:]
        dx2=og_ref[sl,:].astype(F32)+rs*(dy-jnp.mean(dy,axis=-1,keepdims=True)-xh*jnp.mean(dy*xh,axis=-1,keepdims=True))
        x2_ref[sl,:]=dx2
        pend.append(out(x2_ref.at[sl],dx2_out.at[sl],3+3*i))
        do_ref[sl,:]=nt(dx2.astype(BF),wout_ref[...].reshape(D,D)).astype(BF)
        pend.append(out(do_ref.at[sl],do_out.at[sl],4+3*i))
    G_.finish()
    for cp in pend: cp.wait()
def forward_call(A,B,*ins):
    R=ins[9].shape[0]
    sems=Gather.sems(A,B)
    hbm=pl.BlockSpec(memory_space=pl.ANY)
    sd=jax.ShapeDtypeStruct; V=pltpu.VMEM
    outs=[sd((NU,A,B,2,R,D),BF),sd((T,3*D),BF),sd((T,D),BF),sd((T,128),F32),sd((T,16),BF),sd((T,128),BF),sd((T,D),BF),sd((16,D),BF),sd((16,3*D),BF),
          sd((T,D),BF),sd((T,D),F32),sd((T,D),BF)]
    def kernel(*refs):
        forward_kernel(A,B,list(sems),*refs[:25],None,*refs[25:])
    return pl.pallas_call(kernel,in_specs=[hbm]*13,out_specs=[hbm]*12,out_shape=outs,
      scratch_shapes=[V(v.shape,v.dtype) for v in ins]+[V((NU,R,D),BF),V((T,D),BF),V((T,3*D),BF),V((T,D),BF),V((T,D),F32),V((T,D),BF),
        V((T,D),F32),V((T,D),F32),V((T,128),BF),V((T,128),BF),V((4,A,B,2,R,D),BF),V((A,B,2,R,D),BF),V((T,D),BF),V((T,D),BF),V((T,128),F32),V((T,16),BF),
        V((16,D),BF),V((16,3*D),BF),V((1,3*D),F32),V((4,D),F32),
        pltpu.SemaphoreType.DMA((13,)),pltpu.SemaphoreType.DMA((5,)),pltpu.SemaphoreType.DMA((20,))]+list(sems.values()),
      compiler_params=pltpu.CompilerParams(collective_id=0,has_side_effects=True,vmem_limit_bytes=61*2**20),name="front")(*ins)

def back_kernel(x_in,gain_in,shift_in,u_in,kl_in,at_in,uu_in,r_in,lse_in,h1_in,dx2_in,qkv_ref,do_ref,o_ref,bo_in,ig_out,ga_ref,bo_ref,
                x_ref,gain_ref,shift_ref,w_ref,kl_ref,at_ref,uu_ref,r_ref,lse_ref,h1_ref,dx2_ref,dm_ref,dr_ref,sem,osem):
    p=pl.program_id(0)
    ins=(x_in,gain_in,shift_in,u_in.at[0:3],kl_in,at_in,uu_in,r_in,lse_in,h1_in,dx2_in)
    own=(x_ref,gain_ref,shift_ref,w_ref,kl_ref,at_ref,uu_ref,r_ref,lse_ref,h1_ref,dx2_ref)
    cps=[pltpu.make_async_copy(a,b,sem.at[i]) for i,(a,b) in enumerate(zip(ins,own))]
    soon=(8,4,6,7)
    @pl.when(p==0)
    def _():
        for i in soon: cps[i].start()
        for i in range(11):
            if i not in soon: cps[i].start()
        for i in soon: cps[i].wait()
        dr_ref[...]=jnp.zeros((T,16),F32)
    bo_ref[...]=bo_in[...]
    l=lane((T,128))
    lse=lse_ref[...]
    lc=[jnp.sum(jnp.where(l==2*p+h,lse,0.0),axis=1,keepdims=True) for h in range(2)]
    cb=pl.multiple_of(p*384,128)
    def store(kind,sl,val):
        dm_ref[sl,pl.ds(pl.multiple_of(p*384+{"q":0,"k":128,"v":256}[kind],128),128)]=val.astype(BF)
    attn_bwd_pair(qkv_ref[:,0:128],qkv_ref[:,128:256],qkv_ref[:,256:384],do_ref[...],o_ref[...],lc,kl_ref[...],store)
    dmp=dm_ref[:,pl.ds(cb,384)]
    dr_ref[...]+=nt(dmp,uu_ref[:,pl.ds(cb,384)])
    gu=tn(r_ref[...],dmp)*8.0
    oc=pl.ds(pl.multiple_of(p*128,128),128)
    ga_ref[1,:,oc]=gu[4:8,0:128]
    ga_ref[3,:,oc]=gu[12:16,256:384]
    @pl.when(p==7)
    def _():
        for i in range(11):
            if i not in soon: cps[i].wait()
        ga=jnp.zeros((16,D),F32); oc=[]
        for b in range(4):
            sl=slice(b*256,b*256+256)
            dm=dm_ref[sl,:]
            drb=dr_ref[sl,:].astype(BF)
            dh=nn(drb,at_ref[...])
            for u in range(3): dh=dh+nt(dm[:,u*1024:u*1024+1024],w_ref[u].reshape(D,D))
            c,rs=stats(x_ref[sl,:].astype(F32))
            xh=c*rs
            dy=dh*gain_ref[0:1,:]
            dx2_ref[sl,:]=dx2_ref[sl,:]+rs*(dy-jnp.mean(dy,axis=-1,keepdims=True)-xh*jnp.mean(dy*xh,axis=-1,keepdims=True))
            cp=pltpu.make_async_copy(dx2_ref.at[sl],ig_out.at[sl],osem.at[b]); cp.start(); oc.append(cp)
            ga=ga+tn(drb,h1_ref[sl,:])
        ga_ref[0]=ga[0:4]
        ga_ref[2]=ga[8:12]
        for cp in oc: cp.wait()
def back_call(x,gain,shift,u,kl,at,uu,r,lse,h1,dx2,qkv,do,o,bo):
    pb=lambda wd: pl.BlockSpec((T,wd),lambda p:(0,p))
    sd=jax.ShapeDtypeStruct; V=pltpu.VMEM
    hbm=pl.BlockSpec(memory_space=pl.ANY)
    first=(x,gain,shift,u,kl,at,uu,r,lse,h1,dx2)
    return pl.pallas_call(back_kernel,grid=(8,),
      in_specs=[hbm]*11+[pb(384),pb(128),pb(128),pb(128)],
      out_specs=[hbm,VM,pb(128)],
      out_shape=[sd((T,D),F32),sd((4,4,D),F32),sd((T,D),BF)],
      scratch_shapes=[V((3,)+v.shape[1:],v.dtype) if v is u else V(v.shape,v.dtype) for v in first]+[V((T,3*D),BF),V((T,16),F32),
        pltpu.SemaphoreType.DMA((11,)),pltpu.SemaphoreType.DMA((4,))],
      compiler_params=pltpu.CompilerParams(vmem_limit_bytes=60*2**20),name="back")(*first,qkv,do,o,bo)

def sum_kernel(F,DP,g_ref,o_ref,acc_ref,rcv_ref,ss,rs):
    f=lax.axis_index("fsdp"); d=lax.axis_index("dp")
    partners=[]
    for ax,size,me in (("fsdp",F,f),("dp",DP,d)):
        bit=1
        while bit<size:
            other=me+bit-2*bit*lax.rem(lax.div(me,bit),2)
            partners.append({"fsdp":other,"dp":d} if ax=="fsdp" else {"fsdp":f,"dp":other})
            bit*=2
    bar=pltpu.get_barrier_semaphore()
    for p in partners: pl.semaphore_signal(bar,inc=1,device_id=p,device_id_type=MESH)
    pl.semaphore_wait(bar,len(partners))
    acc_ref[0]=g_ref[...]
    cps=[]
    for s,p in enumerate(partners):
        cp=pltpu.make_async_remote_copy(src_ref=acc_ref.at[s],dst_ref=rcv_ref.at[s],send_sem=ss.at[s],recv_sem=rs.at[s],device_id=p,device_id_type=MESH)
        cp.start(); cps.append(cp)
        cp.wait_recv()
        tot=acc_ref[s]+rcv_ref[s]
        if s+1<len(partners): acc_ref[s+1]=tot
        else: o_ref[...]=tot
    for cp in cps: cp.wait_send()
def sum_call(F,DP,g):
    n=(F.bit_length()-1)+(DP.bit_length()-1)
    return pl.pallas_call(functools.partial(sum_kernel,F,DP),in_specs=[VM],out_specs=VM,out_shape=jax.ShapeDtypeStruct(g.shape,F32),
      scratch_shapes=[pltpu.VMEM((n,)+g.shape,F32),pltpu.VMEM((n,)+g.shape,F32),pltpu.SemaphoreType.DMA((n,)),pltpu.SemaphoreType.DMA((n,))],
      compiler_params=pltpu.CompilerParams(collective_id=1,has_side_effects=True),name="total")(g)

def solution(mesh):
    F=mesh.shape["fsdp"]; DP=mesh.shape["dp"]
    A,B=(F//4,2) if F<=16 else (2,F//4)
    def per_device(tokens,item_start,og,gains,shifts,wqkv,bqkv,wout,wfc,bfc,wproj,ob,adapters,momentum,average):
        u,qkv,o,lse,r,kl,h1,at,uu,bo,dx2,do=forward_call(A,B,tokens,og,item_start.reshape(8,128),gains,shifts,ob,bqkv.reshape(24,128),bfc.reshape(32,128),
            adapters.transpose(0,2,1),wqkv,wout,wfc,wproj)
        ig,ga,bo=back_call(tokens,gains,shifts,u,kl,at,uu,r,lse,h1,dx2,qkv,do,o,bo)
        grad=sum_call(F,DP,ga).transpose(0,2,1)
        rate=0.01/jnp.sqrt(jnp.float32(tokens.shape[0]*F*DP))
        mom=0.9*momentum+grad
        new=adapters-rate*(grad+0.9*mom)
        avg=0.9*average+0.1*new
        return bo,ig,grad,mom,new,avg,new.astype(BF)
    rows=P(("fsdp","dp"),None); w=P("fsdp",None); n=P()
    return jax.shard_map(per_device,mesh=mesh,
      in_specs=(rows,P(("fsdp","dp")),rows,n,n,w,n,w,w,n,w,n,n,n,n),out_specs=(rows,rows,n,n,n,n,n),check_vma=False)
```

```python
import functools
import math
import jax, jax.numpy as jnp
from jax import lax
from jax.experimental import pallas as pl
from jax.experimental.pallas import tpu as pltpu
from jax.sharding import PartitionSpec as P
F32=jnp.float32; BF=jnp.bfloat16
T=1024; D=1024; H=16; G=4; GW=256
NEG=-1e30
def nn(a,b): return lax.dot_general(a,b,(((1,),(0,)),((),())),preferred_element_type=F32)
def nt(a,b): return lax.dot_general(a,b,(((1,),(1,)),((),())),preferred_element_type=F32)
def tn(a,b): return lax.dot_general(a,b,(((0,),(0,)),((),())),preferred_element_type=F32)
def lane(shape): return lax.broadcasted_iota(jnp.int32,shape,1)
def row(shape): return lax.broadcasted_iota(jnp.int32,shape,0)
def stats(v):
    mu=jnp.mean(v,axis=-1,keepdims=True); c=v-mu
    rs=lax.rsqrt(jnp.mean(c*c,axis=-1,keepdims=True)+1e-5)
    return c,rs
def parts(x):
    hi=x.astype(BF); r1=x-hi.astype(F32); mid=r1.astype(BF); lo=(r1-mid.astype(F32)).astype(BF)
    return hi.astype(F32),mid.astype(F32),lo.astype(F32)
def key_lanes(starts_row):
    l=lane((T,128)); r=row((T,128))
    return jnp.where(l<8, jnp.where(r>=starts_row,0.0,NEG), jnp.where(l<11,-1.0,0.0)).astype(BF)
def query_lanes(cols):
    l=lane((T,128)); r=row((T,128))
    base=jnp.where(l==lax.shift_right_logical(r,7),1.0,0.0)
    if cols is not None:
        hi,mid,lo=cols
        base=jnp.where(l==8,hi,jnp.where(l==9,mid,jnp.where(l==10,lo,base)))
    return base.astype(BF)
QB=256
VM=pl.BlockSpec(memory_space=pltpu.VMEM)
C0=0.7978845608; C1=0.044715
def attn_bwd_pair(q,k,v,do,o,lcols,klanes,store,KB=256):
    l=lane((T,128))
    q8=q*jnp.asarray(0.125,BF)
    ka=jnp.concatenate([k,klanes],axis=1)
    vl=jnp.where((l>=8)&(l<11),-1.0,0.0).astype(BF)
    va=jnp.concatenate([v,vl],axis=1)
    prod=do.astype(F32)*o.astype(F32)
    causal=row((KB,KB))<=lane((KB,KB))
    res=[]
    for h in range(2):
        hm=(l<64) if h==0 else (l>=64)
        dcol=jnp.sum(jnp.where(hm,prod,0.0),axis=1,keepdims=True)
        qa=jnp.concatenate([jnp.where(hm,q8,jnp.zeros_like(q8)),query_lanes(parts(lcols[h]))],axis=1)
        hi,mid,lo=parts(dcol)
        dl=jnp.where(l==8,hi,jnp.where(l==9,mid,jnp.where(l==10,lo,0.0))).astype(BF)
        da=jnp.concatenate([jnp.where(hm,do,jnp.zeros_like(do)),dl],axis=1)
        dqs=[None]*(T//KB); dks=[];dvs=[]
        for j in range(T//KB):
            r0=j*KB
            t=nt(ka[r0:r0+KB],qa[r0:])
            td=jnp.where(causal,t[:,:KB],NEG)
            t=jnp.concatenate([td,t[:,KB:]],axis=1) if r0+KB<T else td
            p=jnp.exp(t)
            dvs.append(nn(p.astype(BF),do[r0:]))
            u=nt(va[r0:r0+KB],da[r0:])
            ds=(p*u).astype(BF)
            dks.append(nn(ds,q8[r0:]))
            dq=tn(ds,k[r0:r0+KB])
            for i in range(j,T//KB):
                piece=dq[(i-j)*KB:(i-j+1)*KB]
                dqs[i]=piece if dqs[i] is None else dqs[i]+piece
        res.append((dqs,dks,dvs))
    lk=lane((KB,128))<64
    for i in range(T//KB):
        sl=slice(i*KB,(i+1)*KB)
        store("q",sl,jnp.where(lk,res[0][0][i],res[1][0][i])*0.125)
        store("k",sl,jnp.where(lk,res[0][1][i],res[1][1][i]))
        store("v",sl,jnp.where(lk,res[0][2][i],res[1][2][i]))
MESH=pl.DeviceIdType.MESH

NU=12; NC=24; LEAD=3; OFFS=(-LEAD,0,2,4); XC=384
class Gather:
    def __init__(self,A,B,l_ref,u_ref,S):
        self.l,self.u,self.S=l_ref,u_ref,S
        self.hr=u_ref.shape[4]//2
        f=lax.axis_index("fsdp"); d=lax.axis_index("dp")
        self.c=f&1; h=f>>1; self.b=h&(B-1); self.a=h>>(B.bit_length()-1)
        par=d&1
        def dev(a,b,c,e): return {"fsdp":(a*B+b)*2+c,"dp":e}
        self.long_a=A>=B; self.L1,self.L2=(A,B) if A>=B else (B,A)
        def along_a(k): return (self.a+k)&(A-1),self.b
        def along_b(k): return self.a,(self.b+k)&(B-1)
        l1,l2=(along_a,along_b) if self.long_a else (along_b,along_a)
        self.p1=[l1(k) for k in range(1,self.L1)]; self.p2=[l2(k) for k in range(1,self.L2)]
        self.d1=[dev(*p,self.c,d) for p in self.p1]; self.d2=[dev(*p,self.c,d) for p in self.p2]
        self.dx=dev(self.a,self.b,self.c,d+1-2*par); self.dc=dev(self.a,self.b,1-self.c,d)
        self.carried=pl.ds(pl.multiple_of(par*XC,128),D-XC)
        self.crossed=pl.ds(pl.multiple_of(par*(D-XC),128),XC)
        self.peers=[self.dc,self.dx]+self.d1+self.d2
    def greet(self):
        self.bar=pltpu.get_barrier_semaphore()
        for p in self.peers: pl.semaphore_signal(self.bar,inc=1,device_id=p,device_id_type=MESH)
    def greeted(self): pl.semaphore_wait(self.bar,len(self.peers))
    def rows(self,g): return g>>1,pl.ds(pl.multiple_of((g&1)*self.hr,8),self.hr)
    def own(self,lo,hi,k): return pltpu.make_async_copy(self.l.at[lo:hi],self.u.at[lo:hi,self.a,self.b,self.c],self.S["loc"].at[k])
    def rc(self,src,dst,name,g,to):
        return pltpu.make_async_remote_copy(src_ref=src,dst_ref=dst,send_sem=self.S[name+"s"],recv_sem=self.S[name+"r"].at[g],device_id=to,device_id_type=MESH)
    def col(self,b,r,cols,u):
        return self.u.at[u,:,b,self.c,r,cols] if self.long_a else self.u.at[u,b,:,self.c,r,cols]
    def zs(self,g):
        u,r=self.rows(g); s=self.l.at[u,r,self.carried]; t=self.u.at[u,self.a,self.b,self.c,r,self.carried]
        return [self.rc(s,t,"z",g,e) for e in self.d1]
    def ys(self,g):
        u,r=self.rows(g); v=self.col(self.b if self.long_a else self.a,r,self.carried,u)
        return [self.rc(v,v,"y",g,e) for e in self.d2]
    def xs(self,g):
        u,r=self.rows(g); out=[]
        for p in self.p1:
            v=self.u.at[u,p[0],p[1],self.c,r,self.crossed]; out.append(self.rc(v,v,"x",g,self.dx))
        return out
    def ws(self,g):
        u,r=self.rows(g); out=[]
        for p in self.p2:
            v=self.col(p[1] if self.long_a else p[0],r,self.crossed,u); out.append(self.rc(v,v,"w",g,self.dx))
        return out
    def cs(self,g):
        u,r=self.rows(g); v=self.u.at[u,:,:,self.c,r]
        return [self.rc(v,v,"c",g,self.dc)]
    def box(self,name,u,r):
        n1=slice(0,self.L1-1); n2=slice(0,self.L2-1); al=slice(None)
        m={"z":(n1,0,self.carried),"y":(al,n2,self.carried),"x":(n1,0,self.crossed),"w":(al,n2,self.crossed),"c":(al,al,al)}[name]
        i1,i2=(m[0],m[1]) if self.long_a else (m[1],m[0])
        return self.u.at[u,i1,i2,0,r,m[2]]
    def got(self,name,g):
        u,r=self.rows(g); v=self.box(name,u,r)
        self.rc(v,v,name,g,self.dc).wait_recv()
    def stage(self,s,g):
        if s==0:
            for cp in self.zs(g): cp.start()
        elif s==1:
            self.got("z",g)
            for cp in self.ys(g)+self.xs(g): cp.start()
        elif s==2:
            self.got("y",g)
            for cp in self.ws(g): cp.start()
        else:
            self.got("x",g); self.got("w",g)
            for cp in self.cs(g): cp.start()
    def tick(self,t,safe=False,least=0):
        for s,o in enumerate(OFFS):
            if isinstance(t,int):
                if (2 if s==3 else 0)<=t-o<NC: self.stage(s,jnp.int32(t-o))
            elif safe and s<3: self.stage(s,t-o)
            elif safe:
                @pl.when(t-o>=least)
                def _(s=s,o=o): self.stage(s,t-o)
            else:
                @pl.when(t-o<NC)
                def _(s=s,o=o): self.stage(s,t-o)
    def ready(self,u):
        self.got("c",2*u); self.got("c",2*u+1)
    def finish(self):
        for n in "zyxwc":
            v=self.box(n,slice(None),slice(None))
            self.rc(v,v,n,0,self.dc).wait_send()
    @staticmethod
    def sems(A,B):
        s={"loc":(2,)}
        for n in "zyxwc": s[n+"s"]=(); s[n+"r"]=(NC,)
        return {n:pltpu.SemaphoreType.DMA(v) for n,v in s.items()}

def attn_fwd_head(q8,k,v,klanes,qlanes,h,put):
    l=lane((T,128))
    hm=(l<64) if h==0 else (l>=64)
    qa=jnp.concatenate([jnp.where(hm,q8,jnp.zeros_like(q8)),qlanes],axis=1)
    ka=jnp.concatenate([k,klanes],axis=1)
    tri=lane((QB,QB))<=row((QB,QB))
    for i in range(T//QB):
        n=(i+1)*QB
        s=nt(qa[i*QB:(i+1)*QB],ka[:n])
        sd=jnp.where(tri,s[:,n-QB:],NEG)
        s=jnp.concatenate([s[:,:n-QB],sd],axis=1) if i else sd
        m=jnp.max(s,axis=1,keepdims=True)
        e=jnp.exp(s-m)
        tot=jnp.sum(e,axis=1,keepdims=True)
        put(i,nn(e.astype(BF),v[:n])*(1.0/tot),m+jnp.log(tot))

def spread(piece,R,put):
    for j in range(4):
        for t in range(8):
            if R==64:
                f=[piece(4*t+j//2),piece(4*t+2+j//2)]
                half=lane(f[0].shape)<64
                v=jnp.where(half,f[0],pltpu.roll(f[1],64,1)) if j%2==0 else jnp.where(half,pltpu.roll(f[0],64,1),f[1])
            else:
                v=None
                for i in range(4):
                    x=piece(4*t+i); sh=(32*i-32*j)%128
                    x=pltpu.roll(x,sh,1) if sh else x
                    ln=lane(x.shape)
                    v=x if v is None else jnp.where((ln>=32*i)&(ln<32*i+32),x,v)
            put(j,t,v)
def forward_kernel(A,B,sem_names,*refs):
    ins=refs[:13]; outs=refs[13:26]; own=refs[26:39]; rest=refs[39:]
    (x_ref,og_ref,sr_ref,gain_ref,shift_ref,ob_ref,bq_ref,bfc_ref,ad_ref,wq_ref,wo_ref,wf_ref,wp_ref)=own
    (u_ref,qkv_out,o_out,lse_out,r_out,kl_out,h1_out,at_out,uu_out,bo_out,dx2_out,do_out,_)=outs
    (l_ref,h1_ref,qkv_ref,o_ref,x2_ref,h2_ref,y_ref,dh_ref,kl_ref,ql_ref,wb_ref,wout_ref,bo_ref,do_ref,lse_ref,r_ref,at_ref,uu_ref,b3_ref,bf_ref,
     isem,wsem,osem)=rest[:23]
    sems=rest[23:]
    G_=Gather(A,B,l_ref,u_ref,dict(zip(sem_names,sems)))
    R=wq_ref.shape[0]
    cin=[pltpu.make_async_copy(a,b,isem.at[i]) for i,(a,b) in enumerate(zip(ins,own))]
    X,OG,SR,GN,SH,OB,BQ,BF_,AD,WQ,WO,WF,WP=range(13)
    for i in (WQ,X,GN,SH,AD,WO,WP,WF,SR,BQ,BF_,OB,OG): cin[i].start()
    G_.greet()
    cin[WQ].wait()
    for p in range(8):
        for i in range(3):
            c0=384*p+128*i
            l_ref[c0//1024,:,c0%1024:c0%1024+128]=wq_ref[:,1024*i+128*p:1024*i+128*p+128]
    G_.greeted()
    for g in range(LEAD): G_.stage(0,jnp.int32(g))
    G_.own(0,3,0).start()
    for i in (X,GN,SH,AD): cin[i].wait()
    a=[ad_ref[i].astype(BF).astype(F32) for i in range(4)]
    z=jnp.zeros((4,D),F32)
    at_ref[...]=jnp.concatenate([a[0],a[0],a[2],a[2]],0).astype(BF)
    uq=jnp.concatenate([8.0*a[1],z,z,z],0).astype(BF); uv=jnp.concatenate([z,z,8.0*a[3],z],0).astype(BF)
    for p in range(8):
        uu_ref[:,384*p:384*p+128]=uq[:,128*p:128*p+128]
        uu_ref[:,384*p+128:384*p+256]=jnp.zeros((16,128),BF)
        uu_ref[:,384*p+256:384*p+384]=uv[:,128*p:128*p+128]
    def ln0(i,_):
        sl=pl.ds(pl.multiple_of(i*256,256),256)
        c,rs=stats(x_ref[sl,:].astype(F32))
        h1_ref[sl,:]=(c*rs*gain_ref[0:1,:]+shift_ref[0:1,:]).astype(BF)
        r_ref[sl,:]=nt(h1_ref[sl,:],at_ref[...]).astype(BF)
        return 0
    lax.fori_loop(0,2,ln0,0)
    G_.own(0,3,0).wait()
    G_.tick(0)
    for i in (WO,WP,WF,SR,BQ,BF_,OB,OG): cin[i].wait()
    l_ref[3]=wo_ref[...]
    for j in range(4): l_ref[5+2*j]=wp_ref[R*j:R*j+R,:]
    def put_w(j,t,v): l_ref[4+2*j,:,128*t:128*t+128]=v.astype(BF)
    spread(lambda k: wf_ref[:,128*k:128*k+128].astype(F32),R,put_w)
    G_.own(3,NU,1).start()
    G_.tick(1)
    lax.fori_loop(2,4,ln0,0)
    G_.tick(2)
    def put_b(j,t,v): bf_ref[j:j+1,128*t:128*t+128]=v[0:1]
    spread(lambda k: jnp.broadcast_to(bfc_ref[k:k+1,:],(8,128)),R,put_b)
    for p in range(8):
        for i in range(3): b3_ref[:,384*p+128*i:384*p+128*i+128]=bq_ref[8*i+p:8*i+p+1,:]
    e8=lane((8,128))==row((8,128))
    s_row=jnp.sum(jnp.where(e8,jnp.broadcast_to(sr_ref[:,0:1],(8,128)),0),axis=0,keepdims=True)
    kl_ref[...]=key_lanes(s_row)
    ql_ref[...]=query_lanes(None)
    lse_ref[...]=jnp.zeros((T,128),F32)
    G_.own(3,NU,1).wait()
    G_.tick(3); G_.stage(3,jnp.int32(0)); G_.tick(4); G_.stage(3,jnp.int32(1))
    def load(u,slot): return pltpu.make_async_copy(u_ref.at[u],wb_ref.at[slot],wsem.at[slot])
    def w(slot): return wb_ref[slot].reshape(D,D)
    def out(src,dst,k):
        cp=pltpu.make_async_copy(src,dst,osem.at[k]); cp.start(); return cp
    pend=[out(r_ref,r_out,14),out(kl_ref,kl_out,15),out(h1_ref,h1_out,16),out(at_ref,at_out,17),out(uu_ref,uu_out,18)]
    G_.ready(0); load(0,0).start()
    wo_cp=pltpu.make_async_copy(u_ref.at[3],wout_ref,wsem.at[4])
    def pair(p,_):
        nu=jnp.where(p>=5,2,jnp.where(p>=2,1,0))
        @pl.when((p==0)|(p==2)|(p==5))
        def _():
            load(nu,nu).wait()
            cs=pl.ds(pl.multiple_of(nu*1024,1024),1024)
            def mix(i,_):
                sl=pl.ds(pl.multiple_of(i*256,256),256)
                qkv_ref[sl,cs]=(nn(h1_ref[sl,:],w(nu))+(nn(r_ref[sl,:],uu_ref[:,cs])+b3_ref[:,cs])).astype(BF)
                return 0
            lax.fori_loop(0,4,mix,0)
            G_.tick(5+p+nu,True,2)
        qs=pl.ds(pl.multiple_of(p*384,128),128); ks=pl.ds(pl.multiple_of(p*384+128,128),128); vs=pl.ds(pl.multiple_of(p*384+256,128),128)
        oc=pl.ds(pl.multiple_of(p*128,128),128)
        lq=lane((QB,128))
        for h in range(2):
            q8=qkv_ref[:,qs]*jnp.asarray(0.125,BF)
            def put(i,o,ls,h=h):
                sl=slice(i*QB,(i+1)*QB)
                if h==0: o_ref[sl,oc]=o.astype(BF)
                else: o_ref[sl,oc]=jnp.where(lq<64,o_ref[sl,oc],o.astype(BF))
                lse_ref[sl,:]=jnp.where(lq==2*p+h,ls,lse_ref[sl,:])
            attn_fwd_head(q8,qkv_ref[:,ks],qkv_ref[:,vs],kl_ref[...],ql_ref[...],h,put)
        G_.tick(6+p+nu,True,2)
        @pl.when((p==1)|(p==3))
        def _(): G_.ready(nu+1); load(nu+1,nu+1).start()
        @pl.when(p==6)
        def _(): G_.ready(3); wo_cp.start()
        return 0
    lax.fori_loop(0,8,pair,0)
    t=16
    pend+=[out(qkv_ref,qkv_out,0),out(o_ref,o_out,1),out(lse_ref,lse_out,19)]
    wo_cp.wait()
    RB=256
    def mid0(i,_):
        sl=pl.ds(pl.multiple_of(i*RB,RB),RB)
        x2=x_ref[sl,:].astype(F32)+nn(o_ref[sl,:],wout_ref[...].reshape(D,D))+ob_ref[0:1,:]
        x2_ref[sl,:]=x2
        c,rs=stats(x2)
        h2_ref[sl,:]=(c*rs*gain_ref[1:2,:]+shift_ref[1:2,:]).astype(BF)
        y_ref[sl,:]=x2+ob_ref[1:2,:]
        dh_ref[sl,:]=jnp.zeros((RB,D),F32)
        return 0
    lax.fori_loop(0,T//RB-1,mid0,0)
    G_.ready(4); load(4,0).start()
    lax.fori_loop(T//RB-1,T//RB,mid0,0)
    G_.tick(t); t+=1
    G_.ready(5); load(5,1).start()
    base=t
    def chunk(j,_):
        s0=2*lax.rem(j,2); s1=s0+1
        load(4+2*j,s0).wait(); load(5+2*j,s1).wait()
        def blk(i,_):
            sl=pl.ds(pl.multiple_of(i*RB,RB),RB)
            wf=wb_ref[s0].reshape(D,D); wp=wb_ref[s1].reshape(D,D)
            f=nn(h2_ref[sl,:],wf)+bf_ref[pl.ds(j,1),:]
            f2=f*f
            th=jnp.tanh(C0*(f+C1*(f2*f)))
            hp=0.5*(1.0+th)
            g=(f*hp).astype(BF)
            gp=hp+(0.5*C0)*f*(1.0-th*th)*(1.0+(3*C1)*f2)
            y_ref[sl,:]+=nn(g,wp)
            dg=nt(og_ref[sl,:],wp)
            df=(dg*gp).astype(BF)
            dh_ref[sl,:]+=nt(df,wf)
            G_.tick(base+4*j+i)
            @pl.when((i==2)&(j<3))
            def _():
                G_.ready(6+2*j); load(6+2*j,2-s0).start(); G_.ready(7+2*j); load(7+2*j,3-s0).start()
            return 0
        lax.fori_loop(0,T//RB,blk,0)
        return 0
    lax.fori_loop(0,4,chunk,0)
    def last(i,_):
        sl=pl.ds(pl.multiple_of(i*RB,RB),RB)
        bo_ref[sl,:]=y_ref[sl,:].astype(BF)
        c,rs=stats(x2_ref[sl,:])
        xh=c*rs
        dy=dh_ref[sl,:]*gain_ref[1:2,:]
        dx2=og_ref[sl,:].astype(F32)+rs*(dy-jnp.mean(dy,axis=-1,keepdims=True)-xh*jnp.mean(dy*xh,axis=-1,keepdims=True))
        x2_ref[sl,:]=dx2
        do_ref[sl,:]=nt(dx2.astype(BF),wout_ref[...].reshape(D,D)).astype(BF)
        for k,(a,b) in enumerate(((bo_ref,bo_out),(x2_ref,dx2_out),(do_ref,do_out))):
            pltpu.make_async_copy(a.at[sl],b.at[sl],osem.at[2+3*i+k]).start()
        return 0
    lax.fori_loop(0,T//RB,last,0)
    for i in range(T//RB):
        sl=slice(i*RB,(i+1)*RB)
        for k,(a,b) in enumerate(((bo_ref,bo_out),(x2_ref,dx2_out),(do_ref,do_out))):
            pend.append(pltpu.make_async_copy(a.at[sl],b.at[sl],osem.at[2+3*i+k]))
    G_.finish()
    for cp in pend: cp.wait()
def forward_call(A,B,*ins):
    R=ins[9].shape[0]
    sems=Gather.sems(A,B)
    hbm=pl.BlockSpec(memory_space=pl.ANY)
    sd=jax.ShapeDtypeStruct; V=pltpu.VMEM
    outs=[sd((NU,A,B,2,R,D),BF),sd((T,3*D),BF),sd((T,D),BF),sd((T,128),F32),sd((T,16),BF),sd((T,128),BF),sd((T,D),BF),sd((16,D),BF),sd((16,3*D),BF),
          sd((T,D),BF),sd((T,D),F32),sd((T,D),BF)]
    def kernel(*refs):
        forward_kernel(A,B,list(sems),*refs[:25],None,*refs[25:])
    return pl.pallas_call(kernel,in_specs=[hbm]*13,out_specs=[hbm]*12,out_shape=outs,
      scratch_shapes=[V(v.shape,v.dtype) for v in ins]+[V((NU,R,D),BF),V((T,D),BF),V((T,3*D),BF),V((T,D),BF),V((T,D),F32),V((T,D),BF),
        V((T,D),F32),V((T,D),F32),V((T,128),BF),V((T,128),BF),V((4,A,B,2,R,D),BF),V((A,B,2,R,D),BF),V((T,D),BF),V((T,D),BF),V((T,128),F32),V((T,16),BF),
        V((16,D),BF),V((16,3*D),BF),V((1,3*D),F32),V((4,D),F32),
        pltpu.SemaphoreType.DMA((13,)),pltpu.SemaphoreType.DMA((5,)),pltpu.SemaphoreType.DMA((20,))]+list(sems.values()),
      compiler_params=pltpu.CompilerParams(collective_id=0,has_side_effects=True,vmem_limit_bytes=61*2**20),name="front")(*ins)

def back_kernel(kl_in,uu_in,r_in,lse_in,h1_in,qkv_ref,do_ref,o_ref,bo_in,dm_ref,drb_ref,ga_ref,bo_ref,
                kl_ref,uu_ref,r_ref,lse_ref,h1_ref,dr_ref,gs_ref,sem):
    p=pl.program_id(0)
    cps=[pltpu.make_async_copy(a,b,sem.at[i]) for i,(a,b) in enumerate(zip((lse_in,kl_in,uu_in,r_in,h1_in),(lse_ref,kl_ref,uu_ref,r_ref,h1_ref)))]
    @pl.when(p==0)
    def _():
        for cp in cps: cp.start()
        for cp in cps[:4]: cp.wait()
        dr_ref[...]=jnp.zeros((T,16),F32)
    bo_ref[...]=bo_in[...]
    l=lane((T,128))
    lse=lse_ref[...]
    lc=[jnp.sum(jnp.where(l==2*p+h,lse,0.0),axis=1,keepdims=True) for h in range(2)]
    def store(kind,sl,val):
        o={"q":0,"k":128,"v":256}[kind]
        dm_ref[sl,o:o+128]=val.astype(BF)
    attn_bwd_pair(qkv_ref[:,0:128],qkv_ref[:,128:256],qkv_ref[:,256:384],do_ref[...],o_ref[...],lc,kl_ref[...],store)
    dmp=dm_ref[...]
    dr_ref[...]+=nt(dmp,uu_ref[:,pl.ds(pl.multiple_of(p*384,128),384)])
    gu=tn(r_ref[...],dmp)*8.0
    oc=pl.ds(pl.multiple_of(p*128,128),128)
    ga_ref[1,:,oc]=gu[4:8,0:128]
    ga_ref[3,:,oc]=gu[12:16,256:384]
    @pl.when(p==7)
    def _():
        cps[4].wait()
        drb=dr_ref[...].astype(BF)
        drb_ref[...]=drb
        gs_ref[...]=tn(drb,h1_ref[...])
        ga_ref[0]=gs_ref[0:4,:]
        ga_ref[2]=gs_ref[8:12,:]
def back_call(kl,uu,r,lse,h1,qkv,do,o,bo):
    pb=lambda wd: pl.BlockSpec((T,wd),lambda p:(0,p))
    sd=jax.ShapeDtypeStruct; V=pltpu.VMEM
    hbm=pl.BlockSpec(memory_space=pl.ANY)
    first=(kl,uu,r,lse,h1)
    return pl.pallas_call(back_kernel,grid=(8,),
      in_specs=[hbm]*5+[pb(384),pb(128),pb(128),pb(128)],
      out_specs=[pb(384),VM,VM,pb(128)],
      out_shape=[sd((T,3*D),BF),sd((T,16),BF),sd((4,4,D),F32),sd((T,D),BF)],
      scratch_shapes=[V(v.shape,v.dtype) for v in first]+[V((T,16),F32),V((16,D),F32),pltpu.SemaphoreType.DMA((5,))],
      compiler_params=pltpu.CompilerParams(vmem_limit_bytes=60*2**20),name="back")(*first,qkv,do,o,bo)

def sum_kernel(A,B,DP,ga_in,x_in,gain_in,u_in,at_in,drb_in,dx2_in,dm_in,o_ref,ig_out,
               g_ref,x_ref,gain_ref,w_ref,at_ref,drb_ref,dx2_ref,dm_ref,c_ref,h_ref,b_ref,z_ref,t_ref,ss,rs,sem,osem):
    ins=(ga_in,gain_in,at_in,drb_in,u_in.at[0:3],dm_in,x_in,dx2_in)
    own=(g_ref,gain_ref,at_ref,drb_ref,w_ref,dm_ref,x_ref,dx2_ref)
    cin=[pltpu.make_async_copy(p,q,sem.at[i]) for i,(p,q) in enumerate(zip(ins[:5],own[:5]))]
    def part(k,i):
        sl=pl.ds(pl.multiple_of(i*256,256),256)
        return pltpu.make_async_copy(ins[k].at[sl],own[k].at[sl],sem.at[5+3*i+k-5])
    for cp in cin: cp.start()
    for i in range(4):
        for k in (5,6,7): part(k,i).start()
    def block(i):
        for k in (5,6,7): part(k,i).wait()
        sl=pl.ds(pl.multiple_of(i*256,256),256)
        dm=dm_ref[sl,:]
        dh=nn(drb_ref[sl,:],at_ref[...])
        for u in range(3): dh=dh+nt(dm[:,u*1024:u*1024+1024],w_ref[u].reshape(D,D))
        v,s=stats(x_ref[sl,:].astype(F32))
        xh=v*s
        dy=dh*gain_ref[0:1,:]
        dx2_ref[sl,:]=dx2_ref[sl,:]+s*(dy-jnp.mean(dy,axis=-1,keepdims=True)-xh*jnp.mean(dy*xh,axis=-1,keepdims=True))
        pltpu.make_async_copy(dx2_ref.at[sl],ig_out.at[sl],osem.at[i]).start()
    f=lax.axis_index("fsdp"); d=lax.axis_index("dp")
    c=f&1; h=f>>1; b=h&(B-1); a=h>>(B.bit_length()-1)
    def dev(a,b,c,e): return {"fsdp":(a*B+b)*2+c,"dp":e}
    L1,L2=(A,B) if A>=B else (B,A)
    m1,m2=(a,b) if A>=B else (b,a)
    at=(lambda p,q: (p,q)) if A>=B else (lambda p,q: (q,p))
    nb=DP*L2
    me=d*L2+m2
    sib=dev(a,b,1-c,d)
    near=[]
    for k in range(1,nb):
        o=(me+k)&(nb-1)
        near.append(dev(*at(m1,o&(L2-1)),c,o>>(L2.bit_length()-1)))
    far=[dev(*at((m1+k)&(L1-1),m2),c,d) for k in range(1,L1)]
    bar=pltpu.get_barrier_semaphore()
    for p in [sib]+near+far: pl.semaphore_signal(bar,inc=1,device_id=p,device_id_type=MESH)
    pl.semaphore_wait(bar,1+len(near)+len(far))
    def rc(src,dst,k,to): return pltpu.make_async_remote_copy(src_ref=src,dst_ref=dst,send_sem=ss.at[k],recv_sem=rs.at[k],device_id=to,device_id_type=MESH)
    cin[0].wait()
    cps=[rc(g_ref.at[pl.ds(2*(1-c),2)],c_ref,0,sib)]
    cps[0].start()
    for cp in cin[1:]: cp.wait()
    cps[0].wait_recv()
    h_ref[...]=g_ref[pl.ds(2*c,2)]+c_ref[...]
    b_ref[me]=h_ref[...]
    first=[rc(h_ref,b_ref.at[me],k,to) for k,to in enumerate(near,1)]
    for cp in first: cp.start()
    lax.fori_loop(0,1,lambda i,_: (block(i),0)[1],0)
    for cp in first: cp.wait_recv()
    v=b_ref[0]
    for k in range(1,nb): v=v+b_ref[k]
    t_ref[...]=v
    z_ref[m1]=v
    second=[rc(t_ref,z_ref.at[m1],k,to) for k,to in enumerate(far,nb)]
    for cp in second: cp.start()
    lax.fori_loop(1,3,lambda i,_: (block(i),0)[1],0)
    for cp in second: cp.wait_recv()
    v=z_ref[0]
    for k in range(1,L1): v=v+z_ref[k]
    half=o_ref.at[pl.ds(2*c,2)]
    o_ref[pl.ds(2*c,2)]=v
    back=rc(half,half,nb+L1-1,sib)
    back.start()
    lax.fori_loop(3,4,lambda i,_: (block(i),0)[1],0)
    back.wait_recv()
    for cp in cps+first+second+[back]: cp.wait_send()
    for i in range(4):
        sl=slice(i*256,i*256+256)
        pltpu.make_async_copy(dx2_ref.at[sl],ig_out.at[sl],osem.at[i]).wait()
def sum_call(A,B,DP,*ins):
    g=ins[0]
    L1,L2=max(A,B),min(A,B); nb=DP*L2; n=nb+L1
    V=pltpu.VMEM; hs=(2,)+g.shape[1:]
    hbm=pl.BlockSpec(memory_space=pl.ANY)
    sems=pltpu.SemaphoreType.DMA
    return pl.pallas_call(functools.partial(sum_kernel,A,B,DP),in_specs=[hbm]*8,out_specs=[VM,hbm],
      out_shape=[jax.ShapeDtypeStruct(g.shape,F32),jax.ShapeDtypeStruct((T,D),F32)],
      scratch_shapes=[V((3,)+v.shape[1:],v.dtype) if k==3 else V(v.shape,v.dtype) for k,v in enumerate(ins)]+[V(hs,F32),V(hs,F32),V((nb,)+hs,F32),V((L1,)+hs,F32),V(hs,F32),
        sems((n,)),sems((n,)),sems((17,)),sems((4,))],
      compiler_params=pltpu.CompilerParams(collective_id=1,has_side_effects=True,vmem_limit_bytes=61*2**20),name="total")(*ins)

def update_kernel(rate,g_in,m_in,a_in,v_in,ig_in,g_out,m_out,a_out,v_out,c_out,ig_out,g_ref,m_ref,a_ref,v_ref,c_ref,ig_ref,isem,osem):
    small=[pltpu.make_async_copy(p,q,isem.at[i]) for i,(p,q) in enumerate(((g_in,g_ref),(m_in,m_ref),(a_in,a_ref),(v_in,v_ref)))]
    for cp in small: cp.start()
    n=ig_ref.shape[0]//4
    rin=[pltpu.make_async_copy(ig_in.at[i*n:i*n+n],ig_ref.at[i*n:i*n+n],isem.at[4+i]) for i in range(4)]
    rout=[pltpu.make_async_copy(ig_ref.at[i*n:i*n+n],ig_out.at[i*n:i*n+n],osem.at[5+i]) for i in range(4)]
    for cp in rin: cp.start()
    for cp in small: cp.wait()
    g=g_ref[...]
    mom=0.9*m_ref[...]+g
    new=a_ref[...]-rate*(g+0.9*mom)
    m_ref[...]=mom
    a_ref[...]=new
    v_ref[...]=0.9*v_ref[...]+0.1*new
    c_ref[...]=new.astype(BF)
    outs=[pltpu.make_async_copy(p,q,osem.at[i]) for i,(p,q) in enumerate(((g_ref,g_out),(m_ref,m_out),(a_ref,a_out),(v_ref,v_out),(c_ref,c_out)))]
    for cp in outs: cp.start()
    for i in range(4): rin[i].wait(); rout[i].start()
    for cp in outs+rout: cp.wait()
def update_call(rate,g,m,a,v,ig):
    hbm=pl.BlockSpec(memory_space=pl.ANY)
    sd=jax.ShapeDtypeStruct; V=pltpu.VMEM
    return pl.pallas_call(functools.partial(update_kernel,rate),in_specs=[hbm]*5,out_specs=[hbm]*6,
      out_shape=[sd(g.shape,F32)]*4+[sd(g.shape,BF),sd(ig.shape,F32)],
      scratch_shapes=[V(g.shape,F32)]*4+[V(g.shape,BF),V(ig.shape,F32),pltpu.SemaphoreType.DMA((8,)),pltpu.SemaphoreType.DMA((9,))],
      compiler_params=pltpu.CompilerParams(vmem_limit_bytes=61*2**20),name="update")(g,m,a,v,ig)
def solution(mesh):
    F=mesh.shape["fsdp"]; DP=mesh.shape["dp"]
    A,B=(F//4,2) if F<=16 else (2,F//4)
    def per_device(tokens,item_start,og,gains,shifts,wqkv,bqkv,wout,wfc,bfc,wproj,ob,adapters,momentum,average):
        u,qkv,o,lse,r,kl,h1,at,uu,bo,dx2,do=forward_call(A,B,tokens,og,item_start.reshape(8,128),gains,shifts,ob,bqkv.reshape(24,128),bfc.reshape(32,128),
            adapters.transpose(0,2,1),wqkv,wout,wfc,wproj)
        dm,drb,ga,bo=back_call(kl,uu,r,lse,h1,qkv,do,o,bo)
        grad,ig=sum_call(A,B,DP,ga,tokens,gains,u,at,drb,dx2,dm)
        t=lambda v: v.transpose(0,2,1)
        rate=0.01/math.sqrt(tokens.shape[0]*F*DP)
        grad,mom,new,avg,low,ig=update_call(rate,grad,t(momentum),t(adapters),t(average),ig)
        return bo,ig,t(grad),t(mom),t(new),t(avg),t(low)
    rows=P(("fsdp","dp"),None); w=P("fsdp",None); n=P()
    return jax.shard_map(per_device,mesh=mesh,
      in_specs=(rows,P(("fsdp","dp")),rows,n,n,w,n,w,w,n,w,n,n,n,n),out_specs=(rows,rows,n,n,n,n,n),check_vma=False)
```

```python
import functools
import math
import jax, jax.numpy as jnp
from jax import lax
from jax.experimental import pallas as pl
from jax.experimental.pallas import tpu as pltpu
from jax.sharding import PartitionSpec as P
F32=jnp.float32; BF=jnp.bfloat16
T=1024; D=1024; H=16; G=4; GW=256
NEG=-1e30
def nn(a,b): return lax.dot_general(a,b,(((1,),(0,)),((),())),preferred_element_type=F32)
def nt(a,b): return lax.dot_general(a,b,(((1,),(1,)),((),())),preferred_element_type=F32)
def tn(a,b): return lax.dot_general(a,b,(((0,),(0,)),((),())),preferred_element_type=F32)
def lane(shape): return lax.broadcasted_iota(jnp.int32,shape,1)
def row(shape): return lax.broadcasted_iota(jnp.int32,shape,0)
def stats(v):
    mu=jnp.mean(v,axis=-1,keepdims=True); c=v-mu
    rs=lax.rsqrt(jnp.mean(c*c,axis=-1,keepdims=True)+1e-5)
    return c,rs
def parts(x):
    hi=x.astype(BF); r1=x-hi.astype(F32); mid=r1.astype(BF); lo=(r1-mid.astype(F32)).astype(BF)
    return hi.astype(F32),mid.astype(F32),lo.astype(F32)
def key_lanes(starts_row):
    l=lane((T,128)); r=row((T,128))
    return jnp.where(l<8, jnp.where(r>=starts_row,0.0,NEG), jnp.where(l<11,-1.0,0.0)).astype(BF)
def query_lanes(cols):
    l=lane((T,128)); r=row((T,128))
    base=jnp.where(l==lax.shift_right_logical(r,7),1.0,0.0)
    if cols is not None:
        hi,mid,lo=cols
        base=jnp.where(l==8,hi,jnp.where(l==9,mid,jnp.where(l==10,lo,base)))
    return base.astype(BF)
QB=256
VM=pl.BlockSpec(memory_space=pltpu.VMEM)
C0=0.7978845608; C1=0.044715
def attn_bwd_pair(q,k,v,do,o,lcols,klanes,store,KB=256):
    l=lane((T,128))
    q8=q*jnp.asarray(0.125,BF)
    ka=jnp.concatenate([k,klanes],axis=1)
    vl=jnp.where((l>=8)&(l<11),-1.0,0.0).astype(BF)
    va=jnp.concatenate([v,vl],axis=1)
    prod=do.astype(F32)*o.astype(F32)
    causal=row((KB,KB))<=lane((KB,KB))
    res=[]
    for h in range(2):
        hm=(l<64) if h==0 else (l>=64)
        dcol=jnp.sum(jnp.where(hm,prod,0.0),axis=1,keepdims=True)
        qa=jnp.concatenate([jnp.where(hm,q8,jnp.zeros_like(q8)),query_lanes(parts(lcols[h]))],axis=1)
        hi,mid,lo=parts(dcol)
        dl=jnp.where(l==8,hi,jnp.where(l==9,mid,jnp.where(l==10,lo,0.0))).astype(BF)
        da=jnp.concatenate([jnp.where(hm,do,jnp.zeros_like(do)),dl],axis=1)
        dqs=[None]*(T//KB); dks=[];dvs=[]
        for j in range(T//KB):
            r0=j*KB
            t=nt(ka[r0:r0+KB],qa[r0:])
            td=jnp.where(causal,t[:,:KB],NEG)
            t=jnp.concatenate([td,t[:,KB:]],axis=1) if r0+KB<T else td
            p=jnp.exp(t)
            dvs.append(nn(p.astype(BF),do[r0:]))
            u=nt(va[r0:r0+KB],da[r0:])
            ds=(p*u).astype(BF)
            dks.append(nn(ds,q8[r0:]))
            dq=tn(ds,k[r0:r0+KB])
            for i in range(j,T//KB):
                piece=dq[(i-j)*KB:(i-j+1)*KB]
                dqs[i]=piece if dqs[i] is None else dqs[i]+piece
        res.append((dqs,dks,dvs))
    lk=lane((KB,128))<64
    for i in range(T//KB):
        sl=slice(i*KB,(i+1)*KB)
        store("q",sl,jnp.where(lk,res[0][0][i],res[1][0][i])*0.125)
        store("k",sl,jnp.where(lk,res[0][1][i],res[1][1][i]))
        store("v",sl,jnp.where(lk,res[0][2][i],res[1][2][i]))
MESH=pl.DeviceIdType.MESH

NU=12; NC=24; LEAD=4; OFFS=(-LEAD,0,2,4,-1); XC=384
class Gather:
    def __init__(self,A,B,l_ref,u_ref,S):
        self.l,self.u,self.S=l_ref,u_ref,S
        self.hr=u_ref.shape[4]//2
        f=lax.axis_index("fsdp"); d=lax.axis_index("dp")
        self.c=f&1; h=f>>1; self.b=h&(B-1); self.a=h>>(B.bit_length()-1)
        par=d&1
        def dev(a,b,c,e): return {"fsdp":(a*B+b)*2+c,"dp":e}
        self.long_a=A>=B; self.L1,self.L2=(A,B) if A>=B else (B,A)
        def along_a(k): return (self.a+k)&(A-1),self.b
        def along_b(k): return self.a,(self.b+k)&(B-1)
        l1,l2=(along_a,along_b) if self.long_a else (along_b,along_a)
        self.relay=self.L1==4
        q=self.a if self.long_a else self.b
        self.end=(q==0)|(q==3); self.mid=(q==1)|(q==2); self.q=q
        self.p1=[l1(k) for k in range(1,self.L1)]; self.p2=[l2(k) for k in range(1,self.L2)]
        self.d1=[dev(*p,self.c,d) for p in self.p1]; self.d2=[dev(*p,self.c,d) for p in self.p2]
        hop=jnp.where(q==1,0,jnp.where(q==2,3,q)) if self.relay else q
        self.dq=dev(hop,self.b,self.c,d) if self.long_a else dev(self.a,hop,self.c,d)
        self.far=self.p1[1] if self.relay else None
        self.dx=dev(self.a,self.b,self.c,d+1-2*par); self.dc=dev(self.a,self.b,1-self.c,d)
        self.carried=pl.ds(pl.multiple_of(par*XC,128),D-XC)
        self.crossed=pl.ds(pl.multiple_of(par*(D-XC),128),XC)
        self.peers=[self.dc,self.dx]+self.d1+self.d2
    def greet(self):
        self.bar=pltpu.get_barrier_semaphore()
        for p in self.peers: pl.semaphore_signal(self.bar,inc=1,device_id=p,device_id_type=MESH)
    def greeted(self): pl.semaphore_wait(self.bar,len(self.peers))
    def rows(self,g): return g>>1,pl.ds(pl.multiple_of((g&1)*self.hr,8),self.hr)
    def own(self,lo,hi,k): return pltpu.make_async_copy(self.l.at[lo:hi],self.u.at[lo:hi,self.a,self.b,self.c],self.S["loc"].at[k])
    def rc(self,src,dst,name,g,to):
        return pltpu.make_async_remote_copy(src_ref=src,dst_ref=dst,send_sem=self.S[name+"s"],recv_sem=self.S[name+"r"].at[g],device_id=to,device_id_type=MESH)
    def col(self,b,r,cols,u):
        return self.u.at[u,:,b,self.c,r,cols] if self.long_a else self.u.at[u,b,:,self.c,r,cols]
    def zs(self,g):
        u,r=self.rows(g); s=self.l.at[u,r,self.carried]; t=self.u.at[u,self.a,self.b,self.c,r,self.carried]
        return [self.rc(s,t,"z",g,e) for e in self.d1]
    def ys(self,g):
        u,r=self.rows(g); v=self.col(self.b if self.long_a else self.a,r,self.carried,u)
        return [self.rc(v,v,"y",g,e) for e in self.d2]
    def xs(self,g):
        u,r=self.rows(g); out=[]
        for p in self.p1:
            v=self.u.at[u,p[0],p[1],self.c,r,self.crossed]; out.append(self.rc(v,v,"x",g,self.dx))
        return out
    def ws(self,g):
        u,r=self.rows(g); out=[]
        for p in self.p2:
            v=self.col(p[1] if self.long_a else p[0],r,self.crossed,u); out.append(self.rc(v,v,"w",g,self.dx))
        return out
    def cs(self,g):
        u,r=self.rows(g); v=self.u.at[u,:,:,self.c,r]
        return [self.rc(v,v,"c",g,self.dc)]
    def qs(self,g):
        u,r=self.rows(g); v=self.u.at[u,self.far[0],self.far[1],self.c,r,self.carried]
        return self.rc(v,v,"q",g,self.dq)
    def box(self,name,u,r,n=None):
        n1=slice(0,n or self.L1-1); n2=slice(0,self.L2-1); al=slice(None)
        m={"z":(n1,0,self.carried),"y":(al,n2,self.carried),"x":(n1,0,self.crossed),"w":(al,n2,self.crossed),"c":(al,al,al),"q":(slice(0,1),0,self.carried)}[name]
        i1,i2=(m[0],m[1]) if self.long_a else (m[1],m[0])
        return self.u.at[u,i1,i2,0,r,m[2]]
    def got(self,name,g,n=None):
        u,r=self.rows(g); v=self.box(name,u,r,n)
        self.rc(v,v,name,g,self.dc).wait_recv()
    def stage(self,s,g):
        if s==0:
            for k,cp in enumerate(self.zs(g),1):
                if self.relay and k!=2:
                    @pl.when(self.q!=(3 if k==1 else 0))
                    def _(cp=cp): cp.start()
                else: cp.start()
        elif s==4:
            if not self.relay: self.got("z",g)
            else:
                @pl.when(self.end)
                def _(): self.got("z",g,2)
                @pl.when(self.mid)
                def _(): self.got("z",g); self.qs(g).start()
        elif s==1:
            if self.relay:
                @pl.when(self.end)
                def _(): self.got("q",g)
            for cp in self.ys(g)+self.xs(g): cp.start()
        elif s==2:
            self.got("y",g)
            for cp in self.ws(g): cp.start()
        else:
            self.got("x",g); self.got("w",g)
            for cp in self.cs(g): cp.start()
    def tick(self,t,safe=False,least=0):
        for s in (0,3,2,4,1):
            o=OFFS[s]
            if isinstance(t,int):
                if (2 if s==3 else 0)<=t-o<NC: self.stage(s,jnp.int32(t-o))
            elif safe and s!=3: self.stage(s,t-o)
            elif safe:
                @pl.when(t-o>=least)
                def _(s=s,o=o): self.stage(s,t-o)
            else:
                @pl.when(t-o<NC)
                def _(s=s,o=o): self.stage(s,t-o)
    def ready(self,u):
        self.got("c",2*u); self.got("c",2*u+1)
    def finish(self):
        def sent(n,k=None):
            v=self.box(n,slice(None),slice(None),k)
            self.rc(v,v,n,0,self.dc).wait_send()
        for n in "yxwc": sent(n)
        if not self.relay: sent("z")
        else:
            @pl.when(self.end)
            def _(): sent("z",2)
            @pl.when(self.mid)
            def _(): sent("z"); sent("q")
    @staticmethod
    def sems(A,B):
        s={"loc":(2,)}
        for n in "zqyxwc": s[n+"s"]=(); s[n+"r"]=(NC,)
        return {n:pltpu.SemaphoreType.DMA(v) for n,v in s.items()}

def attn_fwd_head(q8,k,v,klanes,qlanes,h,put):
    l=lane((T,128))
    hm=(l<64) if h==0 else (l>=64)
    qa=jnp.concatenate([jnp.where(hm,q8,jnp.zeros_like(q8)),qlanes],axis=1)
    ka=jnp.concatenate([k,klanes],axis=1)
    tri=lane((QB,QB))<=row((QB,QB))
    for i in range(T//QB):
        n=(i+1)*QB
        s=nt(qa[i*QB:(i+1)*QB],ka[:n])
        sd=jnp.where(tri,s[:,n-QB:],NEG)
        s=jnp.concatenate([s[:,:n-QB],sd],axis=1) if i else sd
        m=jnp.max(s,axis=1,keepdims=True)
        e=jnp.exp(s-m)
        tot=jnp.sum(e,axis=1,keepdims=True)
        put(i,nn(e.astype(BF),v[:n])*(1.0/tot),m+jnp.log(tot))

def spread(piece,R,put):
    for j in range(4):
        for t in range(8):
            if R==64:
                f=[piece(4*t+j//2),piece(4*t+2+j//2)]
                half=lane(f[0].shape)<64
                v=jnp.where(half,f[0],pltpu.roll(f[1],64,1)) if j%2==0 else jnp.where(half,pltpu.roll(f[0],64,1),f[1])
            else:
                v=None
                for i in range(4):
                    x=piece(4*t+i); sh=(32*i-32*j)%128
                    x=pltpu.roll(x,sh,1) if sh else x
                    ln=lane(x.shape)
                    v=x if v is None else jnp.where((ln>=32*i)&(ln<32*i+32),x,v)
            put(j,t,v)
def forward_kernel(A,B,sem_names,*refs):
    ins=refs[:13]; outs=refs[13:26]; own=refs[26:39]; rest=refs[39:]
    (x_ref,og_ref,sr_ref,gain_ref,shift_ref,ob_ref,bq_ref,bfc_ref,ad_ref,wq_ref,wo_ref,wf_ref,wp_ref)=own
    (u_ref,qkv_out,o_out,lse_out,r_out,kl_out,h1_out,at_out,uu_out,bo_out,dx2_out,do_out,_)=outs
    (l_ref,h1_ref,qkv_ref,o_ref,x2_ref,h2_ref,y_ref,dh_ref,kl_ref,ql_ref,wb_ref,wout_ref,bo_ref,do_ref,lse_ref,r_ref,at_ref,uu_ref,b3_ref,bf_ref,
     isem,wsem,osem)=rest[:23]
    sems=rest[23:]
    G_=Gather(A,B,l_ref,u_ref,dict(zip(sem_names,sems)))
    R=wq_ref.shape[0]
    cin=[pltpu.make_async_copy(a,b,isem.at[i]) for i,(a,b) in enumerate(zip(ins,own))]
    X,OG,SR,GN,SH,OB,BQ,BF_,AD,WQ,WO,WF,WP=range(13)
    for i in (WQ,X,GN,SH,AD,WO,WP,WF,SR,BQ,BF_,OB,OG): cin[i].start()
    G_.greet()
    cin[WQ].wait()
    for p in range(8):
        for i in range(3):
            c0=384*p+128*i
            l_ref[c0//1024,:,c0%1024:c0%1024+128]=wq_ref[:,1024*i+128*p:1024*i+128*p+128]
    G_.greeted()
    for g in range(LEAD): G_.stage(0,jnp.int32(g))
    G_.own(0,3,0).start()
    for i in (X,GN,SH,AD): cin[i].wait()
    a=[ad_ref[i].astype(BF).astype(F32) for i in range(4)]
    z=jnp.zeros((4,D),F32)
    at_ref[...]=jnp.concatenate([a[0],a[0],a[2],a[2]],0).astype(BF)
    uq=jnp.concatenate([8.0*a[1],z,z,z],0).astype(BF); uv=jnp.concatenate([z,z,8.0*a[3],z],0).astype(BF)
    for p in range(8):
        uu_ref[:,384*p:384*p+128]=uq[:,128*p:128*p+128]
        uu_ref[:,384*p+128:384*p+256]=jnp.zeros((16,128),BF)
        uu_ref[:,384*p+256:384*p+384]=uv[:,128*p:128*p+128]
    def ln0(i,_):
        sl=pl.ds(pl.multiple_of(i*256,256),256)
        c,rs=stats(x_ref[sl,:].astype(F32))
        h1_ref[sl,:]=(c*rs*gain_ref[0:1,:]+shift_ref[0:1,:]).astype(BF)
        r_ref[sl,:]=nt(h1_ref[sl,:],at_ref[...]).astype(BF)
        return 0
    lax.fori_loop(0,2,ln0,0)
    G_.own(0,3,0).wait()
    G_.stage(4,jnp.int32(0))
    G_.tick(0)
    for i in (WO,WP,WF,SR,BQ,BF_,OB,OG): cin[i].wait()
    l_ref[3]=wo_ref[...]
    for j in range(4): l_ref[5+2*j]=wp_ref[R*j:R*j+R,:]
    def put_w(j,t,v): l_ref[4+2*j,:,128*t:128*t+128]=v.astype(BF)
    spread(lambda k: wf_ref[:,128*k:128*k+128].astype(F32),R,put_w)
    G_.own(3,NU,1).start()
    G_.tick(1)
    lax.fori_loop(2,4,ln0,0)
    G_.tick(2)
    def put_b(j,t,v): bf_ref[j:j+1,128*t:128*t+128]=v[0:1]
    spread(lambda k: jnp.broadcast_to(bfc_ref[k:k+1,:],(8,128)),R,put_b)
    for p in range(8):
        for i in range(3): b3_ref[:,384*p+128*i:384*p+128*i+128]=bq_ref[8*i+p:8*i+p+1,:]
    e8=lane((8,128))==row((8,128))
    s_row=jnp.sum(jnp.where(e8,jnp.broadcast_to(sr_ref[:,0:1],(8,128)),0),axis=0,keepdims=True)
    kl_ref[...]=key_lanes(s_row)
    ql_ref[...]=query_lanes(None)
    lse_ref[...]=jnp.zeros((T,128),F32)
    G_.own(3,NU,1).wait()
    G_.tick(3); G_.stage(3,jnp.int32(0)); G_.tick(4); G_.stage(3,jnp.int32(1))
    def load(u,slot): return pltpu.make_async_copy(u_ref.at[u],wb_ref.at[slot],wsem.at[slot])
    def w(slot): return wb_ref[slot].reshape(D,D)
    def out(src,dst,k):
        cp=pltpu.make_async_copy(src,dst,osem.at[k]); cp.start(); return cp
    pend=[out(r_ref,r_out,14),out(kl_ref,kl_out,15),out(h1_ref,h1_out,16),out(at_ref,at_out,17),out(uu_ref,uu_out,18)]
    G_.ready(0); load(0,0).start()
    wo_cp=pltpu.make_async_copy(u_ref.at[3],wout_ref,wsem.at[4])
    def pair(p,_):
        nu=jnp.where(p>=5,2,jnp.where(p>=2,1,0))
        @pl.when((p==0)|(p==2)|(p==5))
        def _():
            load(nu,nu).wait()
            cs=pl.ds(pl.multiple_of(nu*1024,1024),1024)
            def mix(i,_):
                sl=pl.ds(pl.multiple_of(i*256,256),256)
                qkv_ref[sl,cs]=(nn(h1_ref[sl,:],w(nu))+(nn(r_ref[sl,:],uu_ref[:,cs])+b3_ref[:,cs])).astype(BF)
                return 0
            lax.fori_loop(0,4,mix,0)
            G_.tick(5+p+nu,True,2)
        qs=pl.ds(pl.multiple_of(p*384,128),128); ks=pl.ds(pl.multiple_of(p*384+128,128),128); vs=pl.ds(pl.multiple_of(p*384+256,128),128)
        oc=pl.ds(pl.multiple_of(p*128,128),128)
        lq=lane((QB,128))
        for h in range(2):
            q8=qkv_ref[:,qs]*jnp.asarray(0.125,BF)
            def put(i,o,ls,h=h):
                sl=slice(i*QB,(i+1)*QB)
                if h==0: o_ref[sl,oc]=o.astype(BF)
                else: o_ref[sl,oc]=jnp.where(lq<64,o_ref[sl,oc],o.astype(BF))
                lse_ref[sl,:]=jnp.where(lq==2*p+h,ls,lse_ref[sl,:])
            attn_fwd_head(q8,qkv_ref[:,ks],qkv_ref[:,vs],kl_ref[...],ql_ref[...],h,put)
        G_.tick(6+p+nu,True,2)
        @pl.when((p==1)|(p==3))
        def _(): G_.ready(nu+1); load(nu+1,nu+1).start()
        @pl.when(p==6)
        def _(): G_.ready(3); wo_cp.start()
        return 0
    lax.fori_loop(0,8,pair,0)
    t=16
    pend+=[out(qkv_ref,qkv_out,0),out(o_ref,o_out,1),out(lse_ref,lse_out,19)]
    wo_cp.wait()
    RB=256
    def mid0(i,_):
        sl=pl.ds(pl.multiple_of(i*RB,RB),RB)
        x2=x_ref[sl,:].astype(F32)+nn(o_ref[sl,:],wout_ref[...].reshape(D,D))+ob_ref[0:1,:]
        x2_ref[sl,:]=x2
        c,rs=stats(x2)
        h2_ref[sl,:]=(c*rs*gain_ref[1:2,:]+shift_ref[1:2,:]).astype(BF)
        y_ref[sl,:]=x2+ob_ref[1:2,:]
        dh_ref[sl,:]=jnp.zeros((RB,D),F32)
        return 0
    lax.fori_loop(0,T//RB-1,mid0,0)
    G_.ready(4); load(4,0).start()
    lax.fori_loop(T//RB-1,T//RB,mid0,0)
    G_.tick(t); t+=1
    G_.ready(5); load(5,1).start()
    base=t
    def chunk(j,_):
        s0=2*lax.rem(j,2); s1=s0+1
        load(4+2*j,s0).wait(); load(5+2*j,s1).wait()
        def blk(i,_):
            sl=pl.ds(pl.multiple_of(i*RB,RB),RB)
            wf=wb_ref[s0].reshape(D,D); wp=wb_ref[s1].reshape(D,D)
            f=nn(h2_ref[sl,:],wf)+bf_ref[pl.ds(j,1),:]
            f2=f*f
            th=jnp.tanh(C0*(f+C1*(f2*f)))
            hp=0.5*(1.0+th)
            g=(f*hp).astype(BF)
            gp=hp+(0.5*C0)*f*(1.0-th*th)*(1.0+(3*C1)*f2)
            y_ref[sl,:]+=nn(g,wp)
            dg=nt(og_ref[sl,:],wp)
            df=(dg*gp).astype(BF)
            dh_ref[sl,:]+=nt(df,wf)
            G_.tick(base+4*j+i)
            @pl.when((i==1)&(j<3))
            def _(): G_.ready(6+2*j); load(6+2*j,2-s0).start()
            @pl.when((i==2)&(j<3))
            def _(): G_.ready(7+2*j); load(7+2*j,3-s0).start()
            return 0
        lax.fori_loop(0,T//RB,blk,0)
        return 0
    lax.fori_loop(0,4,chunk,0)
    def last(i,_):
        sl=pl.ds(pl.multiple_of(i*RB,RB),RB)
        bo_ref[sl,:]=y_ref[sl,:].astype(BF)
        c,rs=stats(x2_ref[sl,:])
        xh=c*rs
        dy=dh_ref[sl,:]*gain_ref[1:2,:]
        dx2=og_ref[sl,:].astype(F32)+rs*(dy-jnp.mean(dy,axis=-1,keepdims=True)-xh*jnp.mean(dy*xh,axis=-1,keepdims=True))
        x2_ref[sl,:]=dx2
        do_ref[sl,:]=nt(dx2.astype(BF),wout_ref[...].reshape(D,D)).astype(BF)
        for k,(a,b) in enumerate(((bo_ref,bo_out),(x2_ref,dx2_out),(do_ref,do_out))):
            pltpu.make_async_copy(a.at[sl],b.at[sl],osem.at[2+3*i+k]).start()
        return 0
    lax.fori_loop(0,T//RB,last,0,unroll=2)
    for i in range(T//RB):
        sl=slice(i*RB,(i+1)*RB)
        for k,(a,b) in enumerate(((bo_ref,bo_out),(x2_ref,dx2_out),(do_ref,do_out))):
            pend.append(pltpu.make_async_copy(a.at[sl],b.at[sl],osem.at[2+3*i+k]))
    G_.finish()
    for cp in pend: cp.wait()
def forward_call(A,B,*ins):
    R=ins[9].shape[0]
    sems=Gather.sems(A,B)
    hbm=pl.BlockSpec(memory_space=pl.ANY)
    sd=jax.ShapeDtypeStruct; V=pltpu.VMEM
    outs=[sd((NU,A,B,2,R,D),BF),sd((T,3*D),BF),sd((T,D),BF),sd((T,128),F32),sd((T,16),BF),sd((T,128),BF),sd((T,D),BF),sd((16,D),BF),sd((16,3*D),BF),
          sd((T,D),BF),sd((T,D),F32),sd((T,D),BF)]
    def kernel(*refs):
        forward_kernel(A,B,list(sems),*refs[:25],None,*refs[25:])
    return pl.pallas_call(kernel,in_specs=[hbm]*13,out_specs=[hbm]*12,out_shape=outs,
      scratch_shapes=[V(v.shape,v.dtype) for v in ins]+[V((NU,R,D),BF),V((T,D),BF),V((T,3*D),BF),V((T,D),BF),V((T,D),F32),V((T,D),BF),
        V((T,D),F32),V((T,D),F32),V((T,128),BF),V((T,128),BF),V((4,A,B,2,R,D),BF),V((A,B,2,R,D),BF),V((T,D),BF),V((T,D),BF),V((T,128),F32),V((T,16),BF),
        V((16,D),BF),V((16,3*D),BF),V((1,3*D),F32),V((4,D),F32),
        pltpu.SemaphoreType.DMA((13,)),pltpu.SemaphoreType.DMA((5,)),pltpu.SemaphoreType.DMA((20,))]+list(sems.values()),
      compiler_params=pltpu.CompilerParams(collective_id=0,has_side_effects=True,vmem_limit_bytes=61*2**20),name="front")(*ins)

def back_kernel(kl_in,uu_in,r_in,lse_in,h1_in,qkv_ref,do_ref,o_ref,bo_in,dm_ref,drb_ref,ga_ref,bo_ref,
                kl_ref,uu_ref,r_ref,lse_ref,h1_ref,dr_ref,gs_ref,sem):
    p=pl.program_id(0)
    cps=[pltpu.make_async_copy(a,b,sem.at[i]) for i,(a,b) in enumerate(zip((lse_in,kl_in,uu_in,r_in,h1_in),(lse_ref,kl_ref,uu_ref,r_ref,h1_ref)))]
    @pl.when(p==0)
    def _():
        for cp in cps: cp.start()
        for cp in cps[:4]: cp.wait()
        dr_ref[...]=jnp.zeros((T,16),F32)
    bo_ref[...]=bo_in[...]
    l=lane((T,128))
    lse=lse_ref[...]
    lc=[jnp.sum(jnp.where(l==2*p+h,lse,0.0),axis=1,keepdims=True) for h in range(2)]
    def store(kind,sl,val):
        o={"q":0,"k":128,"v":256}[kind]
        dm_ref[sl,o:o+128]=val.astype(BF)
    attn_bwd_pair(qkv_ref[:,0:128],qkv_ref[:,128:256],qkv_ref[:,256:384],do_ref[...],o_ref[...],lc,kl_ref[...],store)
    dmp=dm_ref[...]
    dr_ref[...]+=nt(dmp,uu_ref[:,pl.ds(pl.multiple_of(p*384,128),384)])
    gu=tn(r_ref[...],dmp)*8.0
    oc=pl.ds(pl.multiple_of(p*128,128),128)
    ga_ref[1,:,oc]=gu[4:8,0:128]
    ga_ref[3,:,oc]=gu[12:16,256:384]
    @pl.when(p==7)
    def _():
        cps[4].wait()
        drb=dr_ref[...].astype(BF)
        drb_ref[...]=drb
        gs_ref[...]=tn(drb,h1_ref[...])
        ga_ref[0]=gs_ref[0:4,:]
        ga_ref[2]=gs_ref[8:12,:]
def back_call(kl,uu,r,lse,h1,qkv,do,o,bo):
    pb=lambda wd: pl.BlockSpec((T,wd),lambda p:(0,p))
    sd=jax.ShapeDtypeStruct; V=pltpu.VMEM
    hbm=pl.BlockSpec(memory_space=pl.ANY)
    first=(kl,uu,r,lse,h1)
    return pl.pallas_call(back_kernel,grid=(8,),
      in_specs=[hbm]*5+[pb(384),pb(128),pb(128),pb(128)],
      out_specs=[pb(384),VM,VM,pb(128)],
      out_shape=[sd((T,3*D),BF),sd((T,16),BF),sd((4,4,D),F32),sd((T,D),BF)],
      scratch_shapes=[V(v.shape,v.dtype) for v in first]+[V((T,16),F32),V((16,D),F32),pltpu.SemaphoreType.DMA((5,))],
      compiler_params=pltpu.CompilerParams(vmem_limit_bytes=60*2**20),name="back")(*first,qkv,do,o,bo)

def sum_kernel(A,B,DP,ga_in,x_in,gain_in,u_in,at_in,drb_in,dx2_in,dm_in,o_ref,ig_out,
               g_ref,x_ref,gain_ref,w_ref,at_ref,drb_ref,dx2_ref,dm_ref,c_ref,h_ref,b_ref,z_ref,t_ref,ss,rs,sem,osem):
    ins=(ga_in,gain_in,at_in,drb_in,u_in.at[0:3],dm_in,x_in,dx2_in)
    own=(g_ref,gain_ref,at_ref,drb_ref,w_ref,dm_ref,x_ref,dx2_ref)
    cin=[pltpu.make_async_copy(p,q,sem.at[i]) for i,(p,q) in enumerate(zip(ins[:5],own[:5]))]
    def part(k,i):
        sl=pl.ds(pl.multiple_of(i*256,256),256)
        return pltpu.make_async_copy(ins[k].at[sl],own[k].at[sl],sem.at[5+3*i+k-5])
    for cp in cin: cp.start()
    for i in range(4):
        for k in (5,6,7): part(k,i).start()
    def block(i):
        for k in (5,6,7): part(k,i).wait()
        sl=pl.ds(pl.multiple_of(i*256,256),256)
        dm=dm_ref[sl,:]
        dh=nn(drb_ref[sl,:],at_ref[...])
        for u in range(3): dh=dh+nt(dm[:,u*1024:u*1024+1024],w_ref[u].reshape(D,D))
        v,s=stats(x_ref[sl,:].astype(F32))
        xh=v*s
        dy=dh*gain_ref[0:1,:]
        dx2_ref[sl,:]=dx2_ref[sl,:]+s*(dy-jnp.mean(dy,axis=-1,keepdims=True)-xh*jnp.mean(dy*xh,axis=-1,keepdims=True))
        pltpu.make_async_copy(dx2_ref.at[sl],ig_out.at[sl],osem.at[i]).start()
    f=lax.axis_index("fsdp"); d=lax.axis_index("dp")
    c=f&1; h=f>>1; b=h&(B-1); a=h>>(B.bit_length()-1)
    def dev(a,b,c,e): return {"fsdp":(a*B+b)*2+c,"dp":e}
    L1,L2=(A,B) if A>=B else (B,A)
    m1,m2=(a,b) if A>=B else (b,a)
    at=(lambda p,q: (p,q)) if A>=B else (lambda p,q: (q,p))
    nb=DP*L2
    me=d*L2+m2
    sib=dev(a,b,1-c,d)
    near=[]
    for k in range(1,nb):
        o=(me+k)&(nb-1)
        near.append(dev(*at(m1,o&(L2-1)),c,o>>(L2.bit_length()-1)))
    far=[dev(*at((m1+k)&(L1-1),m2),c,d) for k in range(1,L1)]
    bar=pltpu.get_barrier_semaphore()
    for p in [sib]+near+far: pl.semaphore_signal(bar,inc=1,device_id=p,device_id_type=MESH)
    pl.semaphore_wait(bar,1+len(near)+len(far))
    def rc(src,dst,k,to): return pltpu.make_async_remote_copy(src_ref=src,dst_ref=dst,send_sem=ss.at[k],recv_sem=rs.at[k],device_id=to,device_id_type=MESH)
    cin[0].wait()
    cps=[rc(g_ref.at[pl.ds(2*(1-c),2)],c_ref,0,sib)]
    cps[0].start()
    for cp in cin[1:]: cp.wait()
    cps[0].wait_recv()
    h_ref[...]=g_ref[pl.ds(2*c,2)]+c_ref[...]
    b_ref[me]=h_ref[...]
    first=[rc(h_ref,b_ref.at[me],k,to) for k,to in enumerate(near,1)]
    for cp in first: cp.start()
    lax.fori_loop(0,1,lambda i,_: (block(i),0)[1],0)
    for cp in first: cp.wait_recv()
    v=b_ref[0]
    for k in range(1,nb): v=v+b_ref[k]
    t_ref[...]=v
    z_ref[m1]=v
    second=[rc(t_ref,z_ref.at[m1],k,to) for k,to in enumerate(far,nb)]
    for cp in second: cp.start()
    lax.fori_loop(1,3,lambda i,_: (block(i),0)[1],0)
    for cp in second: cp.wait_recv()
    v=z_ref[0]
    for k in range(1,L1): v=v+z_ref[k]
    half=o_ref.at[pl.ds(2*c,2)]
    o_ref[pl.ds(2*c,2)]=v
    back=rc(half,half,nb+L1-1,sib)
    back.start()
    lax.fori_loop(3,4,lambda i,_: (block(i),0)[1],0)
    back.wait_recv()
    for cp in cps+first+second+[back]: cp.wait_send()
    for i in range(4):
        sl=slice(i*256,i*256+256)
        pltpu.make_async_copy(dx2_ref.at[sl],ig_out.at[sl],osem.at[i]).wait()
def sum_call(A,B,DP,*ins):
    g=ins[0]
    L1,L2=max(A,B),min(A,B); nb=DP*L2; n=nb+L1
    V=pltpu.VMEM; hs=(2,)+g.shape[1:]
    hbm=pl.BlockSpec(memory_space=pl.ANY)
    sems=pltpu.SemaphoreType.DMA
    return pl.pallas_call(functools.partial(sum_kernel,A,B,DP),in_specs=[hbm]*8,out_specs=[VM,hbm],
      out_shape=[jax.ShapeDtypeStruct(g.shape,F32),jax.ShapeDtypeStruct((T,D),F32)],
      scratch_shapes=[V((3,)+v.shape[1:],v.dtype) if k==3 else V(v.shape,v.dtype) for k,v in enumerate(ins)]+[V(hs,F32),V(hs,F32),V((nb,)+hs,F32),V((L1,)+hs,F32),V(hs,F32),
        sems((n,)),sems((n,)),sems((17,)),sems((4,))],
      compiler_params=pltpu.CompilerParams(collective_id=1,has_side_effects=True,vmem_limit_bytes=61*2**20),name="total")(*ins)

def update_kernel(rate,g_in,m_in,a_in,v_in,ig_in,g_out,m_out,a_out,v_out,c_out,ig_out,g_ref,m_ref,a_ref,v_ref,c_ref,ig_ref,isem,osem):
    small=[pltpu.make_async_copy(p,q,isem.at[i]) for i,(p,q) in enumerate(((g_in,g_ref),(m_in,m_ref),(a_in,a_ref),(v_in,v_ref)))]
    for cp in small: cp.start()
    n=ig_ref.shape[0]//4
    rin=[pltpu.make_async_copy(ig_in.at[i*n:i*n+n],ig_ref.at[i*n:i*n+n],isem.at[4+i]) for i in range(4)]
    rout=[pltpu.make_async_copy(ig_ref.at[i*n:i*n+n],ig_out.at[i*n:i*n+n],osem.at[5+i]) for i in range(4)]
    for cp in rin: cp.start()
    for cp in small: cp.wait()
    g=g_ref[...]
    mom=0.9*m_ref[...]+g
    new=a_ref[...]-rate*(g+0.9*mom)
    m_ref[...]=mom
    a_ref[...]=new
    v_ref[...]=0.9*v_ref[...]+0.1*new
    c_ref[...]=new.astype(BF)
    outs=[pltpu.make_async_copy(p,q,osem.at[i]) for i,(p,q) in enumerate(((g_ref,g_out),(m_ref,m_out),(a_ref,a_out),(v_ref,v_out),(c_ref,c_out)))]
    for cp in outs: cp.start()
    for i in range(4): rin[i].wait(); rout[i].start()
    for cp in outs+rout: cp.wait()
def update_call(rate,g,m,a,v,ig):
    hbm=pl.BlockSpec(memory_space=pl.ANY)
    sd=jax.ShapeDtypeStruct; V=pltpu.VMEM
    return pl.pallas_call(functools.partial(update_kernel,rate),in_specs=[hbm]*5,out_specs=[hbm]*6,
      out_shape=[sd(g.shape,F32)]*4+[sd(g.shape,BF),sd(ig.shape,F32)],
      scratch_shapes=[V(g.shape,F32)]*4+[V(g.shape,BF),V(ig.shape,F32),pltpu.SemaphoreType.DMA((8,)),pltpu.SemaphoreType.DMA((9,))],
      compiler_params=pltpu.CompilerParams(vmem_limit_bytes=61*2**20),name="update")(g,m,a,v,ig)
def solution(mesh):
    F=mesh.shape["fsdp"]; DP=mesh.shape["dp"]
    A,B=(F//4,2) if F<=16 else (2,F//4)
    def per_device(tokens,item_start,og,gains,shifts,wqkv,bqkv,wout,wfc,bfc,wproj,ob,adapters,momentum,average):
        u,qkv,o,lse,r,kl,h1,at,uu,bo,dx2,do=forward_call(A,B,tokens,og,item_start.reshape(8,128),gains,shifts,ob,bqkv.reshape(24,128),bfc.reshape(32,128),
            adapters.transpose(0,2,1),wqkv,wout,wfc,wproj)
        dm,drb,ga,bo=back_call(kl,uu,r,lse,h1,qkv,do,o,bo)
        grad,ig=sum_call(A,B,DP,ga,tokens,gains,u,at,drb,dx2,dm)
        t=lambda v: v.transpose(0,2,1)
        rate=0.01/math.sqrt(tokens.shape[0]*F*DP)
        grad,mom,new,avg,low,ig=update_call(rate,grad,t(momentum),t(adapters),t(average),ig)
        return bo,ig,t(grad),t(mom),t(new),t(avg),t(low)
    rows=P(("fsdp","dp"),None); w=P("fsdp",None); n=P()
    return jax.shard_map(per_device,mesh=mesh,
      in_specs=(rows,P(("fsdp","dp")),rows,n,n,w,n,w,w,n,w,n,n,n,n),out_specs=(rows,rows,n,n,n,n,n),check_vma=False)
```

```python
import functools
import math
import jax, jax.numpy as jnp
from jax import lax
from jax.experimental import pallas as pl
from jax.experimental.pallas import tpu as pltpu
from jax.sharding import PartitionSpec as P
F32=jnp.float32; BF=jnp.bfloat16
T=1024; D=1024; H=16; G=4; GW=256
NEG=-1e30
def nn(a,b): return lax.dot_general(a,b,(((1,),(0,)),((),())),preferred_element_type=F32)
def nt(a,b): return lax.dot_general(a,b,(((1,),(1,)),((),())),preferred_element_type=F32)
def tn(a,b): return lax.dot_general(a,b,(((0,),(0,)),((),())),preferred_element_type=F32)
def lane(shape): return lax.broadcasted_iota(jnp.int32,shape,1)
def row(shape): return lax.broadcasted_iota(jnp.int32,shape,0)
def stats(v):
    mu=jnp.mean(v,axis=-1,keepdims=True); c=v-mu
    rs=lax.rsqrt(jnp.mean(c*c,axis=-1,keepdims=True)+1e-5)
    return c,rs
def parts(x):
    hi=x.astype(BF); r1=x-hi.astype(F32); mid=r1.astype(BF); lo=(r1-mid.astype(F32)).astype(BF)
    return hi.astype(F32),mid.astype(F32),lo.astype(F32)
def key_lanes(starts_row):
    l=lane((T,128)); r=row((T,128))
    return jnp.where(l<8, jnp.where(r>=starts_row,0.0,NEG), jnp.where(l<11,-1.0,0.0)).astype(BF)
def query_lanes(cols):
    l=lane((T,128)); r=row((T,128))
    base=jnp.where(l==lax.shift_right_logical(r,7),1.0,0.0)
    if cols is not None:
        hi,mid,lo=cols
        base=jnp.where(l==8,hi,jnp.where(l==9,mid,jnp.where(l==10,lo,base)))
    return base.astype(BF)
QB=512
VM=pl.BlockSpec(memory_space=pltpu.VMEM)
C0=0.7978845608; C1=0.044715
def attn_bwd_pair(q,k,v,do,o,lcols,klanes,store,KB=512):
    l=lane((T,128))
    q8=q*jnp.asarray(0.125,BF)
    ka=jnp.concatenate([k,klanes],axis=1)
    vl=jnp.where((l>=8)&(l<11),-1.0,0.0).astype(BF)
    va=jnp.concatenate([v,vl],axis=1)
    prod=do.astype(F32)*o.astype(F32)
    causal=row((KB,KB))<=lane((KB,KB))
    res=[]
    for h in range(2):
        hm=(l<64) if h==0 else (l>=64)
        dcol=jnp.sum(jnp.where(hm,prod,0.0),axis=1,keepdims=True)
        qa=jnp.concatenate([jnp.where(hm,q8,jnp.zeros_like(q8)),query_lanes(parts(lcols[h]))],axis=1)
        hi,mid,lo=parts(dcol)
        dl=jnp.where(l==8,hi,jnp.where(l==9,mid,jnp.where(l==10,lo,0.0))).astype(BF)
        da=jnp.concatenate([jnp.where(hm,do,jnp.zeros_like(do)),dl],axis=1)
        dqs=[None]*(T//KB); dks=[];dvs=[]
        for j in range(T//KB):
            r0=j*KB
            t=nt(ka[r0:r0+KB],qa[r0:])
            td=jnp.where(causal,t[:,:KB],NEG)
            t=jnp.concatenate([td,t[:,KB:]],axis=1) if r0+KB<T else td
            p=jnp.exp(t)
            dvs.append(nn(p.astype(BF),do[r0:]))
            u=nt(va[r0:r0+KB],da[r0:])
            ds=(p*u).astype(BF)
            dks.append(nn(ds,q8[r0:]))
            dq=tn(ds,k[r0:r0+KB])
            for i in range(j,T//KB):
                piece=dq[(i-j)*KB:(i-j+1)*KB]
                dqs[i]=piece if dqs[i] is None else dqs[i]+piece
        res.append((dqs,dks,dvs))
    lk=lane((KB,128))<64
    for i in range(T//KB):
        sl=slice(i*KB,(i+1)*KB)
        store("q",sl,jnp.where(lk,res[0][0][i],res[1][0][i])*0.125)
        store("k",sl,jnp.where(lk,res[0][1][i],res[1][1][i]))
        store("v",sl,jnp.where(lk,res[0][2][i],res[1][2][i]))
MESH=pl.DeviceIdType.MESH

NU=12; NC=24; LEAD=4; OFFS=(-LEAD,0,2,4,-1); XC=384
class Gather:
    def __init__(self,A,B,l_ref,u_ref,S):
        self.l,self.u,self.S=l_ref,u_ref,S
        self.hr=u_ref.shape[4]//2
        f=lax.axis_index("fsdp"); d=lax.axis_index("dp")
        self.c=f&1; h=f>>1; self.b=h&(B-1); self.a=h>>(B.bit_length()-1)
        par=d&1
        def dev(a,b,c,e): return {"fsdp":(a*B+b)*2+c,"dp":e}
        self.long_a=A>=B; self.L1,self.L2=(A,B) if A>=B else (B,A)
        def along_a(k): return (self.a+k)&(A-1),self.b
        def along_b(k): return self.a,(self.b+k)&(B-1)
        l1,l2=(along_a,along_b) if self.long_a else (along_b,along_a)
        self.relay=self.L1==4
        q=self.a if self.long_a else self.b
        self.end=(q==0)|(q==3); self.mid=(q==1)|(q==2); self.q=q
        self.p1=[l1(k) for k in range(1,self.L1)]; self.p2=[l2(k) for k in range(1,self.L2)]
        self.d1=[dev(*p,self.c,d) for p in self.p1]; self.d2=[dev(*p,self.c,d) for p in self.p2]
        hop=jnp.where(q==1,0,jnp.where(q==2,3,q)) if self.relay else q
        self.dq=dev(hop,self.b,self.c,d) if self.long_a else dev(self.a,hop,self.c,d)
        self.far=self.p1[1] if self.relay else None
        self.dx=dev(self.a,self.b,self.c,d+1-2*par); self.dc=dev(self.a,self.b,1-self.c,d)
        self.carried=pl.ds(pl.multiple_of(par*XC,128),D-XC)
        self.crossed=pl.ds(pl.multiple_of(par*(D-XC),128),XC)
        self.peers=[self.dc,self.dx]+self.d1+self.d2
    def greet(self):
        self.bar=pltpu.get_barrier_semaphore()
        for p in self.peers: pl.semaphore_signal(self.bar,inc=1,device_id=p,device_id_type=MESH)
    def greeted(self): pl.semaphore_wait(self.bar,len(self.peers))
    def rows(self,g): return g>>1,pl.ds(pl.multiple_of((g&1)*self.hr,8),self.hr)
    def own(self,lo,hi,k): return pltpu.make_async_copy(self.l.at[lo:hi],self.u.at[lo:hi,self.a,self.b,self.c],self.S["loc"].at[k])
    def rc(self,src,dst,name,g,to):
        return pltpu.make_async_remote_copy(src_ref=src,dst_ref=dst,send_sem=self.S[name+"s"],recv_sem=self.S[name+"r"].at[g],device_id=to,device_id_type=MESH)
    def col(self,b,r,cols,u):
        return self.u.at[u,:,b,self.c,r,cols] if self.long_a else self.u.at[u,b,:,self.c,r,cols]
    def zs(self,g):
        u,r=self.rows(g); s=self.l.at[u,r,self.carried]; t=self.u.at[u,self.a,self.b,self.c,r,self.carried]
        return [self.rc(s,t,"z",g,e) for e in self.d1]
    def ys(self,g):
        u,r=self.rows(g); v=self.col(self.b if self.long_a else self.a,r,self.carried,u)
        return [self.rc(v,v,"y",g,e) for e in self.d2]
    def xs(self,g):
        u,r=self.rows(g); out=[]
        for p in self.p1:
            v=self.u.at[u,p[0],p[1],self.c,r,self.crossed]; out.append(self.rc(v,v,"x",g,self.dx))
        return out
    def ws(self,g):
        u,r=self.rows(g); out=[]
        for p in self.p2:
            v=self.col(p[1] if self.long_a else p[0],r,self.crossed,u); out.append(self.rc(v,v,"w",g,self.dx))
        return out
    def cs(self,g):
        u,r=self.rows(g); v=self.u.at[u,:,:,self.c,r]
        return [self.rc(v,v,"c",g,self.dc)]
    def qs(self,g):
        u,r=self.rows(g); v=self.u.at[u,self.far[0],self.far[1],self.c,r,self.carried]
        return self.rc(v,v,"q",g,self.dq)
    def box(self,name,u,r,n=None):
        n1=slice(0,n or self.L1-1); n2=slice(0,self.L2-1); al=slice(None)
        m={"z":(n1,0,self.carried),"y":(al,n2,self.carried),"x":(n1,0,self.crossed),"w":(al,n2,self.crossed),"c":(al,al,al),"q":(slice(0,1),0,self.carried)}[name]
        i1,i2=(m[0],m[1]) if self.long_a else (m[1],m[0])
        return self.u.at[u,i1,i2,0,r,m[2]]
    def got(self,name,g,n=None):
        u,r=self.rows(g); v=self.box(name,u,r,n)
        self.rc(v,v,name,g,self.dc).wait_recv()
    def stage(self,s,g):
        if s==0:
            for k,cp in enumerate(self.zs(g),1):
                if self.relay and k!=2:
                    @pl.when(self.q!=(3 if k==1 else 0))
                    def _(cp=cp): cp.start()
                else: cp.start()
        elif s==4:
            if not self.relay: self.got("z",g)
            else:
                @pl.when(self.end)
                def _(): self.got("z",g,2)
                @pl.when(self.mid)
                def _(): self.got("z",g); self.qs(g).start()
        elif s==1:
            if self.relay:
                @pl.when(self.end)
                def _(): self.got("q",g)
            for cp in self.ys(g)+self.xs(g): cp.start()
        elif s==2:
            self.got("y",g)
            for cp in self.ws(g): cp.start()
        else:
            self.got("x",g); self.got("w",g)
            for cp in self.cs(g): cp.start()
    def tick(self,t,safe=False,least=0):
        for s in (0,3,2,4,1):
            o=OFFS[s]
            if isinstance(t,int):
                if (2 if s==3 else 0)<=t-o<NC: self.stage(s,jnp.int32(t-o))
            elif safe and s!=3: self.stage(s,t-o)
            elif safe:
                @pl.when(t-o>=least)
                def _(s=s,o=o): self.stage(s,t-o)
            else:
                @pl.when(t-o<NC)
                def _(s=s,o=o): self.stage(s,t-o)
    def ready(self,u):
        self.got("c",2*u); self.got("c",2*u+1)
    def finish(self):
        def sent(n,k=None):
            v=self.box(n,slice(None),slice(None),k)
            self.rc(v,v,n,0,self.dc).wait_send()
        for n in "yxwc": sent(n)
        if not self.relay: sent("z")
        else:
            @pl.when(self.end)
            def _(): sent("z",2)
            @pl.when(self.mid)
            def _(): sent("z"); sent("q")
    @staticmethod
    def sems(A,B):
        s={"loc":(2,)}
        for n in "zqyxwc": s[n+"s"]=(); s[n+"r"]=(NC,)
        return {n:pltpu.SemaphoreType.DMA(v) for n,v in s.items()}

def attn_fwd_head(q8,k,v,klanes,qlanes,h,put):
    l=lane((T,128))
    hm=(l<64) if h==0 else (l>=64)
    qa=jnp.concatenate([jnp.where(hm,q8,jnp.zeros_like(q8)),qlanes],axis=1)
    ka=jnp.concatenate([k,klanes],axis=1)
    tri=lane((QB,QB))<=row((QB,QB))
    for i in range(T//QB):
        n=(i+1)*QB
        s=nt(qa[i*QB:(i+1)*QB],ka[:n])
        sd=jnp.where(tri,s[:,n-QB:],NEG)
        s=jnp.concatenate([s[:,:n-QB],sd],axis=1) if i else sd
        m=jnp.max(s,axis=1,keepdims=True)
        e=jnp.exp(s-m)
        tot=jnp.sum(e,axis=1,keepdims=True)
        put(i,nn(e.astype(BF),v[:n])*(1.0/tot),m+jnp.log(tot))

def spread(piece,R,put):
    for j in range(4):
        for t in range(8):
            if R==64:
                f=[piece(4*t+j//2),piece(4*t+2+j//2)]
                half=lane(f[0].shape)<64
                v=jnp.where(half,f[0],pltpu.roll(f[1],64,1)) if j%2==0 else jnp.where(half,pltpu.roll(f[0],64,1),f[1])
            else:
                v=None
                for i in range(4):
                    x=piece(4*t+i); sh=(32*i-32*j)%128
                    x=pltpu.roll(x,sh,1) if sh else x
                    ln=lane(x.shape)
                    v=x if v is None else jnp.where((ln>=32*i)&(ln<32*i+32),x,v)
            put(j,t,v)
def forward_kernel(A,B,sem_names,*refs):
    ins=refs[:13]; outs=refs[13:26]; own=refs[26:39]; rest=refs[39:]
    (x_ref,og_ref,sr_ref,gain_ref,shift_ref,ob_ref,bq_ref,bfc_ref,ad_ref,wq_ref,wo_ref,wf_ref,wp_ref)=own
    (u_ref,qkv_out,o_out,lse_out,r_out,kl_out,h1_out,at_out,uu_out,bo_out,dx2_out,do_out,_)=outs
    (l_ref,h1_ref,qkv_ref,o_ref,x2_ref,h2_ref,y_ref,dh_ref,kl_ref,ql_ref,wb_ref,wout_ref,bo_ref,do_ref,lse_ref,r_ref,at_ref,uu_ref,b3_ref,bf_ref,
     isem,wsem,osem)=rest[:23]
    sems=rest[23:]
    G_=Gather(A,B,l_ref,u_ref,dict(zip(sem_names,sems)))
    R=wq_ref.shape[0]
    cin=[pltpu.make_async_copy(a,b,isem.at[i]) for i,(a,b) in enumerate(zip(ins,own))]
    X,OG,SR,GN,SH,OB,BQ,BF_,AD,WQ,WO,WF,WP=range(13)
    for i in (WQ,X,GN,SH,AD,WO,WP,WF,SR,BQ,BF_,OB,OG): cin[i].start()
    G_.greet()
    cin[WQ].wait()
    for p in range(8):
        for i in range(3):
            c0=384*p+128*i
            l_ref[c0//1024,:,c0%1024:c0%1024+128]=wq_ref[:,1024*i+128*p:1024*i+128*p+128]
    G_.greeted()
    for g in range(LEAD): G_.stage(0,jnp.int32(g))
    G_.own(0,3,0).start()
    for i in (X,GN,SH,AD): cin[i].wait()
    a=[ad_ref[i].astype(BF).astype(F32) for i in range(4)]
    z=jnp.zeros((4,D),F32)
    at_ref[...]=jnp.concatenate([a[0],a[0],a[2],a[2]],0).astype(BF)
    uq=jnp.concatenate([8.0*a[1],z,z,z],0).astype(BF); uv=jnp.concatenate([z,z,8.0*a[3],z],0).astype(BF)
    for p in range(8):
        uu_ref[:,384*p:384*p+128]=uq[:,128*p:128*p+128]
        uu_ref[:,384*p+128:384*p+256]=jnp.zeros((16,128),BF)
        uu_ref[:,384*p+256:384*p+384]=uv[:,128*p:128*p+128]
    def ln0(i,_):
        sl=pl.ds(pl.multiple_of(i*256,256),256)
        c,rs=stats(x_ref[sl,:].astype(F32))
        h1_ref[sl,:]=(c*rs*gain_ref[0:1,:]+shift_ref[0:1,:]).astype(BF)
        r_ref[sl,:]=nt(h1_ref[sl,:],at_ref[...]).astype(BF)
        return 0
    lax.fori_loop(0,2,ln0,0)
    G_.own(0,3,0).wait()
    G_.stage(4,jnp.int32(0))
    G_.tick(0)
    for i in (WO,WP,WF,SR,BQ,BF_,OB,OG): cin[i].wait()
    l_ref[3]=wo_ref[...]
    for j in range(4): l_ref[5+2*j]=wp_ref[R*j:R*j+R,:]
    def put_w(j,t,v): l_ref[4+2*j,:,128*t:128*t+128]=v.astype(BF)
    spread(lambda k: wf_ref[:,128*k:128*k+128].astype(F32),R,put_w)
    G_.own(3,NU,1).start()
    G_.tick(1)
    lax.fori_loop(2,4,ln0,0)
    G_.tick(2)
    def put_b(j,t,v): bf_ref[j:j+1,128*t:128*t+128]=v[0:1]
    spread(lambda k: jnp.broadcast_to(bfc_ref[k:k+1,:],(8,128)),R,put_b)
    for p in range(8):
        for i in range(3): b3_ref[:,384*p+128*i:384*p+128*i+128]=bq_ref[8*i+p:8*i+p+1,:]
    e8=lane((8,128))==row((8,128))
    s_row=jnp.sum(jnp.where(e8,jnp.broadcast_to(sr_ref[:,0:1],(8,128)),0),axis=0,keepdims=True)
    kl_ref[...]=key_lanes(s_row)
    ql_ref[...]=query_lanes(None)
    lse_ref[...]=jnp.zeros((T,128),F32)
    G_.own(3,NU,1).wait()
    G_.tick(3); G_.stage(3,jnp.int32(0)); G_.tick(4); G_.stage(3,jnp.int32(1))
    def load(u,slot): return pltpu.make_async_copy(u_ref.at[u],wb_ref.at[slot],wsem.at[slot])
    def w(slot): return wb_ref[slot].reshape(D,D)
    def out(src,dst,k):
        cp=pltpu.make_async_copy(src,dst,osem.at[k]); cp.start(); return cp
    pend=[out(r_ref,r_out,14),out(kl_ref,kl_out,15),out(h1_ref,h1_out,16),out(at_ref,at_out,17),out(uu_ref,uu_out,18)]
    G_.ready(0); load(0,0).start()
    wo_cp=pltpu.make_async_copy(u_ref.at[3],wout_ref,wsem.at[4])
    def pair(p,_):
        nu=jnp.where(p>=5,2,jnp.where(p>=2,1,0))
        @pl.when((p==0)|(p==2)|(p==5))
        def _():
            load(nu,nu).wait()
            cs=pl.ds(pl.multiple_of(nu*1024,1024),1024)
            def mix(i,_):
                sl=pl.ds(pl.multiple_of(i*256,256),256)
                qkv_ref[sl,cs]=(nn(h1_ref[sl,:],w(nu))+(nn(r_ref[sl,:],uu_ref[:,cs])+b3_ref[:,cs])).astype(BF)
                return 0
            lax.fori_loop(0,4,mix,0)
            G_.tick(5+p+nu,True,2)
        qs=pl.ds(pl.multiple_of(p*384,128),128); ks=pl.ds(pl.multiple_of(p*384+128,128),128); vs=pl.ds(pl.multiple_of(p*384+256,128),128)
        oc=pl.ds(pl.multiple_of(p*128,128),128)
        lq=lane((QB,128))
        for h in range(2):
            q8=qkv_ref[:,qs]*jnp.asarray(0.125,BF)
            def put(i,o,ls,h=h):
                sl=slice(i*QB,(i+1)*QB)
                if h==0: o_ref[sl,oc]=o.astype(BF)
                else: o_ref[sl,oc]=jnp.where(lq<64,o_ref[sl,oc],o.astype(BF))
                lse_ref[sl,:]=jnp.where(lq==2*p+h,ls,lse_ref[sl,:])
            attn_fwd_head(q8,qkv_ref[:,ks],qkv_ref[:,vs],kl_ref[...],ql_ref[...],h,put)
        G_.tick(6+p+nu,True,2)
        @pl.when((p==1)|(p==3))
        def _(): G_.ready(nu+1); load(nu+1,nu+1).start()
        @pl.when(p==6)
        def _(): G_.ready(3); wo_cp.start()
        return 0
    lax.fori_loop(0,8,pair,0)
    t=16
    pend+=[out(qkv_ref,qkv_out,0),out(o_ref,o_out,1),out(lse_ref,lse_out,19)]
    wo_cp.wait()
    RB=256
    def mid0(i,_):
        sl=pl.ds(pl.multiple_of(i*RB,RB),RB)
        x2=x_ref[sl,:].astype(F32)+nn(o_ref[sl,:],wout_ref[...].reshape(D,D))+ob_ref[0:1,:]
        x2_ref[sl,:]=x2
        c,rs=stats(x2)
        h2_ref[sl,:]=(c*rs*gain_ref[1:2,:]+shift_ref[1:2,:]).astype(BF)
        y_ref[sl,:]=x2+ob_ref[1:2,:]
        dh_ref[sl,:]=jnp.zeros((RB,D),F32)
        return 0
    lax.fori_loop(0,T//RB-1,mid0,0)
    G_.ready(4); load(4,0).start()
    lax.fori_loop(T//RB-1,T//RB,mid0,0)
    G_.tick(t); t+=1
    G_.ready(5); load(5,1).start()
    base=t
    def chunk(j,_):
        s0=2*lax.rem(j,2); s1=s0+1
        load(4+2*j,s0).wait(); load(5+2*j,s1).wait()
        def blk(i,_):
            sl=pl.ds(pl.multiple_of(i*RB,RB),RB)
            wf=wb_ref[s0].reshape(D,D); wp=wb_ref[s1].reshape(D,D)
            f=nn(h2_ref[sl,:],wf)+bf_ref[pl.ds(j,1),:]
            f2=f*f
            th=jnp.tanh(C0*(f+C1*(f2*f)))
            hp=0.5*(1.0+th)
            g=(f*hp).astype(BF)
            gp=hp+(0.5*C0)*f*(1.0-th*th)*(1.0+(3*C1)*f2)
            y_ref[sl,:]+=nn(g,wp)
            dg=nt(og_ref[sl,:],wp)
            df=(dg*gp).astype(BF)
            dh_ref[sl,:]+=nt(df,wf)
            G_.tick(base+4*j+i)
            @pl.when((i==1)&(j<3))
            def _(): G_.ready(6+2*j); load(6+2*j,2-s0).start()
            @pl.when((i==2)&(j<3))
            def _(): G_.ready(7+2*j); load(7+2*j,3-s0).start()
            return 0
        lax.fori_loop(0,T//RB,blk,0)
        return 0
    lax.fori_loop(0,4,chunk,0)
    def last(i,_):
        sl=pl.ds(pl.multiple_of(i*RB,RB),RB)
        bo_ref[sl,:]=y_ref[sl,:].astype(BF)
        c,rs=stats(x2_ref[sl,:])
        xh=c*rs
        dy=dh_ref[sl,:]*gain_ref[1:2,:]
        dx2=og_ref[sl,:].astype(F32)+rs*(dy-jnp.mean(dy,axis=-1,keepdims=True)-xh*jnp.mean(dy*xh,axis=-1,keepdims=True))
        x2_ref[sl,:]=dx2
        do_ref[sl,:]=nt(dx2.astype(BF),wout_ref[...].reshape(D,D)).astype(BF)
        for k,(a,b) in enumerate(((bo_ref,bo_out),(x2_ref,dx2_out),(do_ref,do_out))):
            pltpu.make_async_copy(a.at[sl],b.at[sl],osem.at[2+3*i+k]).start()
        return 0
    lax.fori_loop(0,T//RB,last,0,unroll=2)
    for i in range(T//RB):
        sl=slice(i*RB,(i+1)*RB)
        for k,(a,b) in enumerate(((bo_ref,bo_out),(x2_ref,dx2_out),(do_ref,do_out))):
            pend.append(pltpu.make_async_copy(a.at[sl],b.at[sl],osem.at[2+3*i+k]))
    G_.finish()
    for cp in pend: cp.wait()
def forward_call(A,B,*ins):
    R=ins[9].shape[0]
    sems=Gather.sems(A,B)
    hbm=pl.BlockSpec(memory_space=pl.ANY)
    sd=jax.ShapeDtypeStruct; V=pltpu.VMEM
    outs=[sd((NU,A,B,2,R,D),BF),sd((T,3*D),BF),sd((T,D),BF),sd((T,128),F32),sd((T,16),BF),sd((T,128),BF),sd((T,D),BF),sd((16,D),BF),sd((16,3*D),BF),
          sd((T,D),BF),sd((T,D),F32),sd((T,D),BF)]
    def kernel(*refs):
        forward_kernel(A,B,list(sems),*refs[:25],None,*refs[25:])
    return pl.pallas_call(kernel,in_specs=[hbm]*13,out_specs=[hbm]*12,out_shape=outs,
      scratch_shapes=[V(v.shape,v.dtype) for v in ins]+[V((NU,R,D),BF),V((T,D),BF),V((T,3*D),BF),V((T,D),BF),V((T,D),F32),V((T,D),BF),
        V((T,D),F32),V((T,D),F32),V((T,128),BF),V((T,128),BF),V((4,A,B,2,R,D),BF),V((A,B,2,R,D),BF),V((T,D),BF),V((T,D),BF),V((T,128),F32),V((T,16),BF),
        V((16,D),BF),V((16,3*D),BF),V((1,3*D),F32),V((4,D),F32),
        pltpu.SemaphoreType.DMA((13,)),pltpu.SemaphoreType.DMA((5,)),pltpu.SemaphoreType.DMA((20,))]+list(sems.values()),
      compiler_params=pltpu.CompilerParams(collective_id=0,has_side_effects=True,vmem_limit_bytes=61*2**20),name="front")(*ins)

def back_kernel(kl_in,uu_in,r_in,lse_in,h1_in,qkv_ref,do_ref,o_ref,bo_in,dm_ref,drb_ref,ga_ref,bo_ref,
                kl_ref,uu_ref,r_ref,lse_ref,h1_ref,dr_ref,gs_ref,sem):
    p=pl.program_id(0)
    cps=[pltpu.make_async_copy(a,b,sem.at[i]) for i,(a,b) in enumerate(zip((lse_in,kl_in,uu_in,r_in,h1_in),(lse_ref,kl_ref,uu_ref,r_ref,h1_ref)))]
    @pl.when(p==0)
    def _():
        for cp in cps: cp.start()
        for cp in cps[:4]: cp.wait()
        dr_ref[...]=jnp.zeros((T,16),F32)
    bo_ref[...]=bo_in[...]
    l=lane((T,128))
    lse=lse_ref[...]
    lc=[jnp.sum(jnp.where(l==2*p+h,lse,0.0),axis=1,keepdims=True) for h in range(2)]
    def store(kind,sl,val):
        o={"q":0,"k":128,"v":256}[kind]
        dm_ref[sl,o:o+128]=val.astype(BF)
    attn_bwd_pair(qkv_ref[:,0:128],qkv_ref[:,128:256],qkv_ref[:,256:384],do_ref[...],o_ref[...],lc,kl_ref[...],store)
    dmp=dm_ref[...]
    dr_ref[...]+=nt(dmp,uu_ref[:,pl.ds(pl.multiple_of(p*384,128),384)])
    gu=tn(r_ref[...],dmp)*8.0
    oc=pl.ds(pl.multiple_of(p*128,128),128)
    ga_ref[1,:,oc]=gu[4:8,0:128]
    ga_ref[3,:,oc]=gu[12:16,256:384]
    @pl.when(p==7)
    def _():
        cps[4].wait()
        drb=dr_ref[...].astype(BF)
        drb_ref[...]=drb
        gs_ref[...]=tn(drb,h1_ref[...])
        ga_ref[0]=gs_ref[0:4,:]
        ga_ref[2]=gs_ref[8:12,:]
def back_call(kl,uu,r,lse,h1,qkv,do,o,bo):
    pb=lambda wd: pl.BlockSpec((T,wd),lambda p:(0,p))
    sd=jax.ShapeDtypeStruct; V=pltpu.VMEM
    hbm=pl.BlockSpec(memory_space=pl.ANY)
    first=(kl,uu,r,lse,h1)
    return pl.pallas_call(back_kernel,grid=(8,),
      in_specs=[hbm]*5+[pb(384),pb(128),pb(128),pb(128)],
      out_specs=[pb(384),VM,VM,pb(128)],
      out_shape=[sd((T,3*D),BF),sd((T,16),BF),sd((4,4,D),F32),sd((T,D),BF)],
      scratch_shapes=[V(v.shape,v.dtype) for v in first]+[V((T,16),F32),V((16,D),F32),pltpu.SemaphoreType.DMA((5,))],
      compiler_params=pltpu.CompilerParams(vmem_limit_bytes=60*2**20),name="back")(*first,qkv,do,o,bo)

def sum_kernel(A,B,DP,ga_in,x_in,gain_in,u_in,at_in,drb_in,dx2_in,dm_in,o_ref,ig_out,
               g_ref,x_ref,gain_ref,w_ref,at_ref,drb_ref,dx2_ref,dm_ref,c_ref,h_ref,b_ref,z_ref,t_ref,ss,rs,sem,osem):
    ins=(ga_in,gain_in,at_in,drb_in,u_in.at[0:3],dm_in,x_in,dx2_in)
    own=(g_ref,gain_ref,at_ref,drb_ref,w_ref,dm_ref,x_ref,dx2_ref)
    cin=[pltpu.make_async_copy(p,q,sem.at[i]) for i,(p,q) in enumerate(zip(ins[:5],own[:5]))]
    def part(k,i):
        sl=pl.ds(pl.multiple_of(i*256,256),256)
        return pltpu.make_async_copy(ins[k].at[sl],own[k].at[sl],sem.at[5+3*i+k-5])
    for cp in cin: cp.start()
    for i in range(4):
        for k in (5,6,7): part(k,i).start()
    def block(i):
        for k in (5,6,7): part(k,i).wait()
        sl=pl.ds(pl.multiple_of(i*256,256),256)
        dm=dm_ref[sl,:]
        dh=nn(drb_ref[sl,:],at_ref[...])
        for u in range(3): dh=dh+nt(dm[:,u*1024:u*1024+1024],w_ref[u].reshape(D,D))
        v,s=stats(x_ref[sl,:].astype(F32))
        xh=v*s
        dy=dh*gain_ref[0:1,:]
        dx2_ref[sl,:]=dx2_ref[sl,:]+s*(dy-jnp.mean(dy,axis=-1,keepdims=True)-xh*jnp.mean(dy*xh,axis=-1,keepdims=True))
        pltpu.make_async_copy(dx2_ref.at[sl],ig_out.at[sl],osem.at[i]).start()
    f=lax.axis_index("fsdp"); d=lax.axis_index("dp")
    c=f&1; h=f>>1; b=h&(B-1); a=h>>(B.bit_length()-1)
    def dev(a,b,c,e): return {"fsdp":(a*B+b)*2+c,"dp":e}
    L1,L2=(A,B) if A>=B else (B,A)
    m1,m2=(a,b) if A>=B else (b,a)
    at=(lambda p,q: (p,q)) if A>=B else (lambda p,q: (q,p))
    nb=DP*L2
    me=d*L2+m2
    sib=dev(a,b,1-c,d)
    near=[]
    for k in range(1,nb):
        o=(me+k)&(nb-1)
        near.append(dev(*at(m1,o&(L2-1)),c,o>>(L2.bit_length()-1)))
    far=[dev(*at((m1+k)&(L1-1),m2),c,d) for k in range(1,L1)]
    bar=pltpu.get_barrier_semaphore()
    for p in [sib]+near+far: pl.semaphore_signal(bar,inc=1,device_id=p,device_id_type=MESH)
    pl.semaphore_wait(bar,1+len(near)+len(far))
    def rc(src,dst,k,to): return pltpu.make_async_remote_copy(src_ref=src,dst_ref=dst,send_sem=ss.at[k],recv_sem=rs.at[k],device_id=to,device_id_type=MESH)
    cin[0].wait()
    cps=[rc(g_ref.at[pl.ds(2*(1-c),2)],c_ref,0,sib)]
    cps[0].start()
    for cp in cin[1:]: cp.wait()
    cps[0].wait_recv()
    h_ref[...]=g_ref[pl.ds(2*c,2)]+c_ref[...]
    b_ref[me]=h_ref[...]
    first=[rc(h_ref,b_ref.at[me],k,to) for k,to in enumerate(near,1)]
    for cp in first: cp.start()
    lax.fori_loop(0,1,lambda i,_: (block(i),0)[1],0)
    for cp in first: cp.wait_recv()
    v=b_ref[0]
    for k in range(1,nb): v=v+b_ref[k]
    t_ref[...]=v
    z_ref[m1]=v
    second=[rc(t_ref,z_ref.at[m1],k,to) for k,to in enumerate(far,nb)]
    for cp in second: cp.start()
    lax.fori_loop(1,3,lambda i,_: (block(i),0)[1],0)
    for cp in second: cp.wait_recv()
    v=z_ref[0]
    for k in range(1,L1): v=v+z_ref[k]
    half=o_ref.at[pl.ds(2*c,2)]
    o_ref[pl.ds(2*c,2)]=v
    back=rc(half,half,nb+L1-1,sib)
    back.start()
    lax.fori_loop(3,4,lambda i,_: (block(i),0)[1],0)
    back.wait_recv()
    for cp in cps+first+second+[back]: cp.wait_send()
    for i in range(4):
        sl=slice(i*256,i*256+256)
        pltpu.make_async_copy(dx2_ref.at[sl],ig_out.at[sl],osem.at[i]).wait()
def sum_call(A,B,DP,*ins):
    g=ins[0]
    L1,L2=max(A,B),min(A,B); nb=DP*L2; n=nb+L1
    V=pltpu.VMEM; hs=(2,)+g.shape[1:]
    hbm=pl.BlockSpec(memory_space=pl.ANY)
    sems=pltpu.SemaphoreType.DMA
    return pl.pallas_call(functools.partial(sum_kernel,A,B,DP),in_specs=[hbm]*8,out_specs=[VM,hbm],
      out_shape=[jax.ShapeDtypeStruct(g.shape,F32),jax.ShapeDtypeStruct((T,D),F32)],
      scratch_shapes=[V((3,)+v.shape[1:],v.dtype) if k==3 else V(v.shape,v.dtype) for k,v in enumerate(ins)]+[V(hs,F32),V(hs,F32),V((nb,)+hs,F32),V((L1,)+hs,F32),V(hs,F32),
        sems((n,)),sems((n,)),sems((17,)),sems((4,))],
      compiler_params=pltpu.CompilerParams(collective_id=1,has_side_effects=True,vmem_limit_bytes=61*2**20),name="total")(*ins)

def update_kernel(rate,g_in,m_in,a_in,v_in,ig_in,g_out,m_out,a_out,v_out,c_out,ig_out,g_ref,m_ref,a_ref,v_ref,c_ref,ig_ref,isem,osem):
    small=[pltpu.make_async_copy(p,q,isem.at[i]) for i,(p,q) in enumerate(((g_in,g_ref),(m_in,m_ref),(a_in,a_ref),(v_in,v_ref)))]
    for cp in small: cp.start()
    n=ig_ref.shape[0]//4
    rin=[pltpu.make_async_copy(ig_in.at[i*n:i*n+n],ig_ref.at[i*n:i*n+n],isem.at[4+i]) for i in range(4)]
    rout=[pltpu.make_async_copy(ig_ref.at[i*n:i*n+n],ig_out.at[i*n:i*n+n],osem.at[5+i]) for i in range(4)]
    for cp in rin: cp.start()
    for cp in small: cp.wait()
    g=g_ref[...]
    mom=0.9*m_ref[...]+g
    new=a_ref[...]-rate*(g+0.9*mom)
    m_ref[...]=mom
    a_ref[...]=new
    v_ref[...]=0.9*v_ref[...]+0.1*new
    c_ref[...]=new.astype(BF)
    outs=[pltpu.make_async_copy(p,q,osem.at[i]) for i,(p,q) in enumerate(((g_ref,g_out),(m_ref,m_out),(a_ref,a_out),(v_ref,v_out),(c_ref,c_out)))]
    for cp in outs: cp.start()
    for i in range(4): rin[i].wait(); rout[i].start()
    for cp in outs+rout: cp.wait()
def update_call(rate,g,m,a,v,ig):
    hbm=pl.BlockSpec(memory_space=pl.ANY)
    sd=jax.ShapeDtypeStruct; V=pltpu.VMEM
    return pl.pallas_call(functools.partial(update_kernel,rate),in_specs=[hbm]*5,out_specs=[hbm]*6,
      out_shape=[sd(g.shape,F32)]*4+[sd(g.shape,BF),sd(ig.shape,F32)],
      scratch_shapes=[V(g.shape,F32)]*4+[V(g.shape,BF),V(ig.shape,F32),pltpu.SemaphoreType.DMA((8,)),pltpu.SemaphoreType.DMA((9,))],
      compiler_params=pltpu.CompilerParams(vmem_limit_bytes=61*2**20),name="update")(g,m,a,v,ig)
def solution(mesh):
    F=mesh.shape["fsdp"]; DP=mesh.shape["dp"]
    A,B=(F//4,2) if F<=16 else (2,F//4)
    def per_device(tokens,item_start,og,gains,shifts,wqkv,bqkv,wout,wfc,bfc,wproj,ob,adapters,momentum,average):
        u,qkv,o,lse,r,kl,h1,at,uu,bo,dx2,do=forward_call(A,B,tokens,og,item_start.reshape(8,128),gains,shifts,ob,bqkv.reshape(24,128),bfc.reshape(32,128),
            adapters.transpose(0,2,1),wqkv,wout,wfc,wproj)
        dm,drb,ga,bo=back_call(kl,uu,r,lse,h1,qkv,do,o,bo)
        grad,ig=sum_call(A,B,DP,ga,tokens,gains,u,at,drb,dx2,dm)
        t=lambda v: v.transpose(0,2,1)
        rate=0.01/math.sqrt(tokens.shape[0]*F*DP)
        grad,mom,new,avg,low,ig=update_call(rate,grad,t(momentum),t(adapters),t(average),ig)
        return bo,ig,t(grad),t(mom),t(new),t(avg),t(low)
    rows=P(("fsdp","dp"),None); w=P("fsdp",None); n=P()
    return jax.shard_map(per_device,mesh=mesh,
      in_specs=(rows,P(("fsdp","dp")),rows,n,n,w,n,w,w,n,w,n,n,n,n),out_specs=(rows,rows,n,n,n,n,n),check_vma=False)
```

```python
import functools
import math
import jax, jax.numpy as jnp
from jax import lax
from jax.experimental import pallas as pl
from jax.experimental.pallas import tpu as pltpu
from jax.sharding import PartitionSpec as P
F32=jnp.float32; BF=jnp.bfloat16
T=1024; D=1024; H=16; G=4; GW=256
NEG=-1e30
def nn(a,b): return lax.dot_general(a,b,(((1,),(0,)),((),())),preferred_element_type=F32)
def nt(a,b): return lax.dot_general(a,b,(((1,),(1,)),((),())),preferred_element_type=F32)
def tn(a,b): return lax.dot_general(a,b,(((0,),(0,)),((),())),preferred_element_type=F32)
def lane(shape): return lax.broadcasted_iota(jnp.int32,shape,1)
def row(shape): return lax.broadcasted_iota(jnp.int32,shape,0)
def stats(v):
    mu=jnp.mean(v,axis=-1,keepdims=True); c=v-mu
    rs=lax.rsqrt(jnp.mean(c*c,axis=-1,keepdims=True)+1e-5)
    return c,rs
def parts(x):
    hi=x.astype(BF); r1=x-hi.astype(F32); mid=r1.astype(BF); lo=(r1-mid.astype(F32)).astype(BF)
    return hi.astype(F32),mid.astype(F32),lo.astype(F32)
def key_lanes(starts_row):
    l=lane((T,128)); r=row((T,128))
    return jnp.where(l<8, jnp.where(r>=starts_row,0.0,NEG), jnp.where(l<11,-1.0,0.0)).astype(BF)
def query_lanes(cols):
    l=lane((T,128)); r=row((T,128))
    base=jnp.where(l==lax.shift_right_logical(r,7),1.0,0.0)
    if cols is not None:
        hi,mid,lo=cols
        base=jnp.where(l==8,hi,jnp.where(l==9,mid,jnp.where(l==10,lo,base)))
    return base.astype(BF)
QB=512
VM=pl.BlockSpec(memory_space=pltpu.VMEM)
C0=0.7978845608; C1=0.044715
def attn_bwd_pair(q,k,v,do,o,lcols,klanes,store,KB=512):
    l=lane((T,128))
    q8=q*jnp.asarray(0.125,BF)
    ka=jnp.concatenate([k,klanes],axis=1)
    vl=jnp.where((l>=8)&(l<11),-1.0,0.0).astype(BF)
    va=jnp.concatenate([v,vl],axis=1)
    prod=do.astype(F32)*o.astype(F32)
    causal=row((KB,KB))<=lane((KB,KB))
    res=[]
    for h in range(2):
        hm=(l<64) if h==0 else (l>=64)
        dcol=jnp.sum(jnp.where(hm,prod,0.0),axis=1,keepdims=True)
        qa=jnp.concatenate([jnp.where(hm,q8,jnp.zeros_like(q8)),query_lanes(parts(lcols[h]))],axis=1)
        hi,mid,lo=parts(dcol)
        dl=jnp.where(l==8,hi,jnp.where(l==9,mid,jnp.where(l==10,lo,0.0))).astype(BF)
        da=jnp.concatenate([jnp.where(hm,do,jnp.zeros_like(do)),dl],axis=1)
        dqs=[None]*(T//KB); dks=[];dvs=[]
        for j in range(T//KB):
            r0=j*KB
            t=nt(ka[r0:r0+KB],qa[r0:])
            td=jnp.where(causal,t[:,:KB],NEG)
            t=jnp.concatenate([td,t[:,KB:]],axis=1) if r0+KB<T else td
            p=jnp.exp(t)
            dvs.append(nn(p.astype(BF),do[r0:]))
            u=nt(va[r0:r0+KB],da[r0:])
            ds=(p*u).astype(BF)
            dks.append(nn(ds,q8[r0:]))
            dq=tn(ds,k[r0:r0+KB])
            for i in range(j,T//KB):
                piece=dq[(i-j)*KB:(i-j+1)*KB]
                dqs[i]=piece if dqs[i] is None else dqs[i]+piece
        res.append((dqs,dks,dvs))
    lk=lane((KB,128))<64
    for i in range(T//KB):
        sl=slice(i*KB,(i+1)*KB)
        store("q",sl,jnp.where(lk,res[0][0][i],res[1][0][i])*0.125)
        store("k",sl,jnp.where(lk,res[0][1][i],res[1][1][i]))
        store("v",sl,jnp.where(lk,res[0][2][i],res[1][2][i]))
MESH=pl.DeviceIdType.MESH

NU=12; NC=24; LEAD=4; OFFS=(-LEAD,0,2,4,-1); XC=384
class Gather:
    def __init__(self,A,B,l_ref,u_ref,S):
        self.l,self.u,self.S=l_ref,u_ref,S
        self.hr=u_ref.shape[4]//2
        f=lax.axis_index("fsdp"); d=lax.axis_index("dp")
        self.c=f&1; h=f>>1; self.b=h&(B-1); self.a=h>>(B.bit_length()-1)
        par=d&1
        def dev(a,b,c,e): return {"fsdp":(a*B+b)*2+c,"dp":e}
        self.long_a=A>=B; self.L1,self.L2=(A,B) if A>=B else (B,A)
        def along_a(k): return (self.a+k)&(A-1),self.b
        def along_b(k): return self.a,(self.b+k)&(B-1)
        l1,l2=(along_a,along_b) if self.long_a else (along_b,along_a)
        self.relay=self.L1==4
        q=self.a if self.long_a else self.b
        self.end=(q==0)|(q==3); self.mid=(q==1)|(q==2); self.q=q
        self.p1=[l1(k) for k in range(1,self.L1)]; self.p2=[l2(k) for k in range(1,self.L2)]
        self.d1=[dev(*p,self.c,d) for p in self.p1]; self.d2=[dev(*p,self.c,d) for p in self.p2]
        hop=jnp.where(q==1,0,jnp.where(q==2,3,q)) if self.relay else q
        self.dq=dev(hop,self.b,self.c,d) if self.long_a else dev(self.a,hop,self.c,d)
        self.far=self.p1[1] if self.relay else None
        self.dx=dev(self.a,self.b,self.c,d+1-2*par); self.dc=dev(self.a,self.b,1-self.c,d)
        self.carried=pl.ds(pl.multiple_of(par*XC,128),D-XC)
        self.crossed=pl.ds(pl.multiple_of(par*(D-XC),128),XC)
        self.peers=[self.dc,self.dx]+self.d1+self.d2
    def greet(self):
        self.bar=pltpu.get_barrier_semaphore()
        for p in self.peers: pl.semaphore_signal(self.bar,inc=1,device_id=p,device_id_type=MESH)
    def greeted(self): pl.semaphore_wait(self.bar,len(self.peers))
    def rows(self,g): return g>>1,pl.ds(pl.multiple_of((g&1)*self.hr,8),self.hr)
    def own(self,lo,hi,k): return pltpu.make_async_copy(self.l.at[lo:hi],self.u.at[lo:hi,self.a,self.b,self.c],self.S["loc"].at[k])
    def rc(self,src,dst,name,g,to):
        return pltpu.make_async_remote_copy(src_ref=src,dst_ref=dst,send_sem=self.S[name+"s"],recv_sem=self.S[name+"r"].at[g],device_id=to,device_id_type=MESH)
    def col(self,b,r,cols,u):
        return self.u.at[u,:,b,self.c,r,cols] if self.long_a else self.u.at[u,b,:,self.c,r,cols]
    def zs(self,g):
        u,r=self.rows(g); s=self.l.at[u,r,self.carried]; t=self.u.at[u,self.a,self.b,self.c,r,self.carried]
        return [self.rc(s,t,"z",g,e) for e in self.d1]
    def ys(self,g):
        u,r=self.rows(g); v=self.col(self.b if self.long_a else self.a,r,self.carried,u)
        return [self.rc(v,v,"y",g,e) for e in self.d2]
    def xs(self,g):
        u,r=self.rows(g); out=[]
        for p in self.p1:
            v=self.u.at[u,p[0],p[1],self.c,r,self.crossed]; out.append(self.rc(v,v,"x",g,self.dx))
        return out
    def ws(self,g):
        u,r=self.rows(g); out=[]
        for p in self.p2:
            v=self.col(p[1] if self.long_a else p[0],r,self.crossed,u); out.append(self.rc(v,v,"w",g,self.dx))
        return out
    def cs(self,g):
        u,r=self.rows(g); v=self.u.at[u,:,:,self.c,r]
        return [self.rc(v,v,"c",g,self.dc)]
    def qs(self,g):
        u,r=self.rows(g); v=self.u.at[u,self.far[0],self.far[1],self.c,r,self.carried]
        return self.rc(v,v,"q",g,self.dq)
    def box(self,name,u,r,n=None):
        n1=slice(0,n or self.L1-1); n2=slice(0,self.L2-1); al=slice(None)
        m={"z":(n1,0,self.carried),"y":(al,n2,self.carried),"x":(n1,0,self.crossed),"w":(al,n2,self.crossed),"c":(al,al,al),"q":(slice(0,1),0,self.carried)}[name]
        i1,i2=(m[0],m[1]) if self.long_a else (m[1],m[0])
        return self.u.at[u,i1,i2,0,r,m[2]]
    def got(self,name,g,n=None):
        u,r=self.rows(g); v=self.box(name,u,r,n)
        self.rc(v,v,name,g,self.dc).wait_recv()
    def stage(self,s,g):
        if s==0:
            for k,cp in enumerate(self.zs(g),1):
                if self.relay and k!=2:
                    @pl.when(self.q!=(3 if k==1 else 0))
                    def _(cp=cp): cp.start()
                else: cp.start()
        elif s==4:
            if not self.relay: self.got("z",g)
            else:
                @pl.when(self.end)
                def _(): self.got("z",g,2)
                @pl.when(self.mid)
                def _(): self.got("z",g); self.qs(g).start()
        elif s==1:
            if self.relay:
                @pl.when(self.end)
                def _(): self.got("q",g)
            for cp in self.ys(g)+self.xs(g): cp.start()
        elif s==2:
            self.got("y",g)
            for cp in self.ws(g): cp.start()
        else:
            self.got("x",g); self.got("w",g)
            for cp in self.cs(g): cp.start()
    def tick(self,t,safe=False,least=0):
        for s in (0,3,2,4,1):
            o=OFFS[s]
            if isinstance(t,int):
                if (2 if s==3 else 0)<=t-o<NC: self.stage(s,jnp.int32(t-o))
            elif safe and s!=3: self.stage(s,t-o)
            elif safe:
                @pl.when(t-o>=least)
                def _(s=s,o=o): self.stage(s,t-o)
            else:
                @pl.when(t-o<NC)
                def _(s=s,o=o): self.stage(s,t-o)
    def ready(self,u):
        self.got("c",2*u); self.got("c",2*u+1)
    def finish(self):
        def sent(n,k=None):
            v=self.box(n,slice(None),slice(None),k)
            self.rc(v,v,n,0,self.dc).wait_send()
        for n in "yxwc": sent(n)
        if not self.relay: sent("z")
        else:
            @pl.when(self.end)
            def _(): sent("z",2)
            @pl.when(self.mid)
            def _(): sent("z"); sent("q")
    @staticmethod
    def sems(A,B):
        s={"loc":(2,)}
        for n in "zqyxwc": s[n+"s"]=(); s[n+"r"]=(NC,)
        return {n:pltpu.SemaphoreType.DMA(v) for n,v in s.items()}

def attn_fwd_head(q8,k,v,klanes,qlanes,h,put):
    l=lane((T,128))
    hm=(l<64) if h==0 else (l>=64)
    qa=jnp.concatenate([jnp.where(hm,q8,jnp.zeros_like(q8)),qlanes],axis=1)
    ka=jnp.concatenate([k,klanes],axis=1)
    tri=lane((QB,QB))<=row((QB,QB))
    for i in range(T//QB):
        n=(i+1)*QB
        s=nt(qa[i*QB:(i+1)*QB],ka[:n])
        sd=jnp.where(tri,s[:,n-QB:],NEG)
        s=jnp.concatenate([s[:,:n-QB],sd],axis=1) if i else sd
        m=jnp.max(s,axis=1,keepdims=True)
        e=jnp.exp(s-m)
        tot=jnp.sum(e,axis=1,keepdims=True)
        put(i,nn(e.astype(BF),v[:n])*(1.0/tot),m+jnp.log(tot))

def spread(piece,R,put):
    for j in range(4):
        for t in range(8):
            if R==64:
                f=[piece(4*t+j//2),piece(4*t+2+j//2)]
                half=lane(f[0].shape)<64
                v=jnp.where(half,f[0],pltpu.roll(f[1],64,1)) if j%2==0 else jnp.where(half,pltpu.roll(f[0],64,1),f[1])
            else:
                v=None
                for i in range(4):
                    x=piece(4*t+i); sh=(32*i-32*j)%128
                    x=pltpu.roll(x,sh,1) if sh else x
                    ln=lane(x.shape)
                    v=x if v is None else jnp.where((ln>=32*i)&(ln<32*i+32),x,v)
            put(j,t,v)
def forward_kernel(A,B,sem_names,*refs):
    ins=refs[:13]; outs=refs[13:26]; own=refs[26:39]; rest=refs[39:]
    (x_ref,og_ref,sr_ref,gain_ref,shift_ref,ob_ref,bq_ref,bfc_ref,ad_ref,wq_ref,wo_ref,wf_ref,wp_ref)=own
    (u_ref,qkv_out,o_out,lse_out,r_out,kl_out,h1_out,at_out,uu_out,bo_out,dx2_out,do_out,_)=outs
    (l_ref,h1_ref,qkv_ref,o_ref,x2_ref,h2_ref,y_ref,dh_ref,kl_ref,ql_ref,wb_ref,wout_ref,bo_ref,do_ref,lse_ref,r_ref,at_ref,uu_ref,b3_ref,bf_ref,
     isem,wsem,osem)=rest[:23]
    sems=rest[23:]
    G_=Gather(A,B,l_ref,u_ref,dict(zip(sem_names,sems)))
    R=wq_ref.shape[0]
    cin=[pltpu.make_async_copy(a,b,isem.at[i]) for i,(a,b) in enumerate(zip(ins,own))]
    X,OG,SR,GN,SH,OB,BQ,BF_,AD,WQ,WO,WF,WP=range(13)
    for i in (WQ,X,GN,SH,AD,WO,WP,WF,SR,BQ,BF_,OB,OG): cin[i].start()
    G_.greet()
    cin[WQ].wait()
    for p in range(8):
        for i in range(3):
            c0=384*p+128*i
            l_ref[c0//1024,:,c0%1024:c0%1024+128]=wq_ref[:,1024*i+128*p:1024*i+128*p+128]
    G_.greeted()
    for g in range(LEAD): G_.stage(0,jnp.int32(g))
    G_.own(0,3,0).start()
    for i in (X,GN,SH,AD): cin[i].wait()
    a=[ad_ref[i].astype(BF).astype(F32) for i in range(4)]
    z=jnp.zeros((4,D),F32)
    at_ref[...]=jnp.concatenate([a[0],a[0],a[2],a[2]],0).astype(BF)
    uq=jnp.concatenate([8.0*a[1],z,z,z],0).astype(BF); uv=jnp.concatenate([z,z,8.0*a[3],z],0).astype(BF)
    for p in range(8):
        uu_ref[:,384*p:384*p+128]=uq[:,128*p:128*p+128]
        uu_ref[:,384*p+128:384*p+256]=jnp.zeros((16,128),BF)
        uu_ref[:,384*p+256:384*p+384]=uv[:,128*p:128*p+128]
    def ln0(i,_):
        sl=pl.ds(pl.multiple_of(i*256,256),256)
        c,rs=stats(x_ref[sl,:].astype(F32))
        h1_ref[sl,:]=(c*rs*gain_ref[0:1,:]+shift_ref[0:1,:]).astype(BF)
        r_ref[sl,:]=nt(h1_ref[sl,:],at_ref[...]).astype(BF)
        return 0
    lax.fori_loop(0,2,ln0,0)
    G_.own(0,3,0).wait()
    G_.stage(4,jnp.int32(0))
    G_.tick(0)
    for i in (WO,WP,WF,SR,BQ,BF_,OB,OG): cin[i].wait()
    l_ref[3]=wo_ref[...]
    for j in range(4): l_ref[5+2*j]=wp_ref[R*j:R*j+R,:]
    def put_w(j,t,v): l_ref[4+2*j,:,128*t:128*t+128]=v.astype(BF)
    spread(lambda k: wf_ref[:,128*k:128*k+128].astype(F32),R,put_w)
    G_.own(3,NU,1).start()
    G_.tick(1)
    lax.fori_loop(2,4,ln0,0)
    G_.tick(2)
    def put_b(j,t,v): bf_ref[j:j+1,128*t:128*t+128]=v[0:1]
    spread(lambda k: jnp.broadcast_to(bfc_ref[k:k+1,:],(8,128)),R,put_b)
    for p in range(8):
        for i in range(3): b3_ref[:,384*p+128*i:384*p+128*i+128]=bq_ref[8*i+p:8*i+p+1,:]
    e8=lane((8,128))==row((8,128))
    s_row=jnp.sum(jnp.where(e8,jnp.broadcast_to(sr_ref[:,0:1],(8,128)),0),axis=0,keepdims=True)
    kl_ref[...]=key_lanes(s_row)
    ql_ref[...]=query_lanes(None)
    lse_ref[...]=jnp.zeros((T,128),F32)
    G_.own(3,NU,1).wait()
    G_.tick(3); G_.stage(3,jnp.int32(0)); G_.tick(4); G_.stage(3,jnp.int32(1))
    def load(u,slot): return pltpu.make_async_copy(u_ref.at[u],wb_ref.at[slot],wsem.at[slot])
    def w(slot): return wb_ref[slot].reshape(D,D)
    def out(src,dst,k):
        cp=pltpu.make_async_copy(src,dst,osem.at[k]); cp.start(); return cp
    pend=[out(r_ref,r_out,14),out(kl_ref,kl_out,15),out(h1_ref,h1_out,16),out(at_ref,at_out,17),out(uu_ref,uu_out,18)]
    G_.ready(0); load(0,0).start()
    wo_cp=pltpu.make_async_copy(u_ref.at[3],wout_ref,wsem.at[4])
    def pair(p,_):
        nu=jnp.where(p>=5,2,jnp.where(p>=2,1,0))
        @pl.when((p==0)|(p==2)|(p==5))
        def _():
            load(nu,nu).wait()
            cs=pl.ds(pl.multiple_of(nu*1024,1024),1024)
            def mix(i,_):
                sl=pl.ds(pl.multiple_of(i*256,256),256)
                qkv_ref[sl,cs]=(nn(h1_ref[sl,:],w(nu))+(nn(r_ref[sl,:],uu_ref[:,cs])+b3_ref[:,cs])).astype(BF)
                return 0
            lax.fori_loop(0,4,mix,0,unroll=2)
            G_.tick(5+p+nu,True,2)
        qs=pl.ds(pl.multiple_of(p*384,128),128); ks=pl.ds(pl.multiple_of(p*384+128,128),128); vs=pl.ds(pl.multiple_of(p*384+256,128),128)
        oc=pl.ds(pl.multiple_of(p*128,128),128)
        lq=lane((QB,128))
        for h in range(2):
            q8=qkv_ref[:,qs]*jnp.asarray(0.125,BF)
            def put(i,o,ls,h=h):
                sl=slice(i*QB,(i+1)*QB)
                if h==0: o_ref[sl,oc]=o.astype(BF)
                else: o_ref[sl,oc]=jnp.where(lq<64,o_ref[sl,oc],o.astype(BF))
                lse_ref[sl,:]=jnp.where(lq==2*p+h,ls,lse_ref[sl,:])
            attn_fwd_head(q8,qkv_ref[:,ks],qkv_ref[:,vs],kl_ref[...],ql_ref[...],h,put)
        G_.tick(6+p+nu,True,2)
        @pl.when((p==1)|(p==3))
        def _(): G_.ready(nu+1); load(nu+1,nu+1).start()
        @pl.when(p==6)
        def _(): G_.ready(3); wo_cp.start()
        return 0
    lax.fori_loop(0,8,pair,0)
    t=16
    pend+=[out(qkv_ref,qkv_out,0),out(o_ref,o_out,1),out(lse_ref,lse_out,19)]
    wo_cp.wait()
    RB=256
    def mid0(i,_):
        sl=pl.ds(pl.multiple_of(i*RB,RB),RB)
        x2=x_ref[sl,:].astype(F32)+nn(o_ref[sl,:],wout_ref[...].reshape(D,D))+ob_ref[0:1,:]
        x2_ref[sl,:]=x2
        c,rs=stats(x2)
        h2_ref[sl,:]=(c*rs*gain_ref[1:2,:]+shift_ref[1:2,:]).astype(BF)
        y_ref[sl,:]=x2+ob_ref[1:2,:]
        dh_ref[sl,:]=jnp.zeros((RB,D),F32)
        return 0
    lax.fori_loop(0,T//RB-1,mid0,0)
    G_.ready(4); load(4,0).start()
    lax.fori_loop(T//RB-1,T//RB,mid0,0)
    G_.tick(t); t+=1
    G_.ready(5); load(5,1).start()
    base=t
    def chunk(j,_):
        s0=2*lax.rem(j,2); s1=s0+1
        load(4+2*j,s0).wait(); load(5+2*j,s1).wait()
        def blk(i,_):
            sl=pl.ds(pl.multiple_of(i*RB,RB),RB)
            wf=wb_ref[s0].reshape(D,D); wp=wb_ref[s1].reshape(D,D)
            f=nn(h2_ref[sl,:],wf)+bf_ref[pl.ds(j,1),:]
            f2=f*f
            th=jnp.tanh(C0*(f+C1*(f2*f)))
            hp=0.5*(1.0+th)
            g=(f*hp).astype(BF)
            gp=hp+(0.5*C0)*f*(1.0-th*th)*(1.0+(3*C1)*f2)
            y_ref[sl,:]+=nn(g,wp)
            dg=nt(og_ref[sl,:],wp)
            df=(dg*gp).astype(BF)
            dh_ref[sl,:]+=nt(df,wf)
            G_.tick(base+4*j+i)
            @pl.when((i==1)&(j<3))
            def _(): G_.ready(6+2*j); load(6+2*j,2-s0).start()
            @pl.when((i==2)&(j<3))
            def _(): G_.ready(7+2*j); load(7+2*j,3-s0).start()
            return 0
        lax.fori_loop(0,T//RB,blk,0)
        return 0
    lax.fori_loop(0,4,chunk,0)
    def last(i,_):
        sl=pl.ds(pl.multiple_of(i*RB,RB),RB)
        bo_ref[sl,:]=y_ref[sl,:].astype(BF)
        c,rs=stats(x2_ref[sl,:])
        xh=c*rs
        dy=dh_ref[sl,:]*gain_ref[1:2,:]
        dx2=og_ref[sl,:].astype(F32)+rs*(dy-jnp.mean(dy,axis=-1,keepdims=True)-xh*jnp.mean(dy*xh,axis=-1,keepdims=True))
        x2_ref[sl,:]=dx2
        do_ref[sl,:]=nt(dx2.astype(BF),wout_ref[...].reshape(D,D)).astype(BF)
        for k,(a,b) in enumerate(((bo_ref,bo_out),(x2_ref,dx2_out),(do_ref,do_out))):
            pltpu.make_async_copy(a.at[sl],b.at[sl],osem.at[2+3*i+k]).start()
        return 0
    lax.fori_loop(0,T//RB,last,0,unroll=2)
    for i in range(T//RB):
        sl=slice(i*RB,(i+1)*RB)
        for k,(a,b) in enumerate(((bo_ref,bo_out),(x2_ref,dx2_out),(do_ref,do_out))):
            pend.append(pltpu.make_async_copy(a.at[sl],b.at[sl],osem.at[2+3*i+k]))
    G_.finish()
    for cp in pend: cp.wait()
def forward_call(A,B,*ins):
    R=ins[9].shape[0]
    sems=Gather.sems(A,B)
    hbm=pl.BlockSpec(memory_space=pl.ANY)
    sd=jax.ShapeDtypeStruct; V=pltpu.VMEM
    outs=[sd((NU,A,B,2,R,D),BF),sd((T,3*D),BF),sd((T,D),BF),sd((T,128),F32),sd((T,16),BF),sd((T,128),BF),sd((T,D),BF),sd((16,D),BF),sd((16,3*D),BF),
          sd((T,D),BF),sd((T,D),F32),sd((T,D),BF)]
    def kernel(*refs):
        forward_kernel(A,B,list(sems),*refs[:25],None,*refs[25:])
    return pl.pallas_call(kernel,in_specs=[hbm]*13,out_specs=[hbm]*12,out_shape=outs,
      scratch_shapes=[V(v.shape,v.dtype) for v in ins]+[V((NU,R,D),BF),V((T,D),BF),V((T,3*D),BF),V((T,D),BF),V((T,D),F32),V((T,D),BF),
        V((T,D),F32),V((T,D),F32),V((T,128),BF),V((T,128),BF),V((4,A,B,2,R,D),BF),V((A,B,2,R,D),BF),V((T,D),BF),V((T,D),BF),V((T,128),F32),V((T,16),BF),
        V((16,D),BF),V((16,3*D),BF),V((1,3*D),F32),V((4,D),F32),
        pltpu.SemaphoreType.DMA((13,)),pltpu.SemaphoreType.DMA((5,)),pltpu.SemaphoreType.DMA((20,))]+list(sems.values()),
      compiler_params=pltpu.CompilerParams(collective_id=0,has_side_effects=True,vmem_limit_bytes=61*2**20),name="front")(*ins)

def back_kernel(kl_in,uu_in,r_in,lse_in,h1_in,qkv_ref,do_ref,o_ref,bo_in,dm_ref,drb_ref,ga_ref,bo_ref,
                kl_ref,uu_ref,r_ref,lse_ref,h1_ref,dr_ref,gs_ref,sem):
    p=pl.program_id(0)
    cps=[pltpu.make_async_copy(a,b,sem.at[i]) for i,(a,b) in enumerate(zip((lse_in,kl_in,uu_in,r_in,h1_in),(lse_ref,kl_ref,uu_ref,r_ref,h1_ref)))]
    @pl.when(p==0)
    def _():
        for cp in cps: cp.start()
        for cp in cps[:4]: cp.wait()
        dr_ref[...]=jnp.zeros((T,16),F32)
    bo_ref[...]=bo_in[...]
    l=lane((T,128))
    lse=lse_ref[...]
    lc=[jnp.sum(jnp.where(l==2*p+h,lse,0.0),axis=1,keepdims=True) for h in range(2)]
    def store(kind,sl,val):
        o={"q":0,"k":128,"v":256}[kind]
        dm_ref[sl,o:o+128]=val.astype(BF)
    attn_bwd_pair(qkv_ref[:,0:128],qkv_ref[:,128:256],qkv_ref[:,256:384],do_ref[...],o_ref[...],lc,kl_ref[...],store)
    dmp=dm_ref[...]
    dr_ref[...]+=nt(dmp,uu_ref[:,pl.ds(pl.multiple_of(p*384,128),384)])
    gu=tn(r_ref[...],dmp)*8.0
    oc=pl.ds(pl.multiple_of(p*128,128),128)
    ga_ref[1,:,oc]=gu[4:8,0:128]
    ga_ref[3,:,oc]=gu[12:16,256:384]
    @pl.when(p==7)
    def _():
        cps[4].wait()
        drb=dr_ref[...].astype(BF)
        drb_ref[...]=drb
        gs_ref[...]=tn(drb,h1_ref[...])
        ga_ref[0]=gs_ref[0:4,:]
        ga_ref[2]=gs_ref[8:12,:]
def back_call(kl,uu,r,lse,h1,qkv,do,o,bo):
    pb=lambda wd: pl.BlockSpec((T,wd),lambda p:(0,p))
    sd=jax.ShapeDtypeStruct; V=pltpu.VMEM
    hbm=pl.BlockSpec(memory_space=pl.ANY)
    first=(kl,uu,r,lse,h1)
    return pl.pallas_call(back_kernel,grid=(8,),
      in_specs=[hbm]*5+[pb(384),pb(128),pb(128),pb(128)],
      out_specs=[pb(384),VM,VM,pb(128)],
      out_shape=[sd((T,3*D),BF),sd((T,16),BF),sd((4,4,D),F32),sd((T,D),BF)],
      scratch_shapes=[V(v.shape,v.dtype) for v in first]+[V((T,16),F32),V((16,D),F32),pltpu.SemaphoreType.DMA((5,))],
      compiler_params=pltpu.CompilerParams(vmem_limit_bytes=60*2**20),name="back")(*first,qkv,do,o,bo)

def sum_kernel(A,B,DP,ga_in,x_in,gain_in,u_in,at_in,drb_in,dx2_in,dm_in,o_ref,ig_out,
               g_ref,x_ref,gain_ref,w_ref,at_ref,drb_ref,dx2_ref,dm_ref,c_ref,h_ref,b_ref,z_ref,t_ref,ss,rs,sem,osem):
    ins=(ga_in,gain_in,at_in,drb_in,u_in.at[0:3],dm_in,x_in,dx2_in)
    own=(g_ref,gain_ref,at_ref,drb_ref,w_ref,dm_ref,x_ref,dx2_ref)
    cin=[pltpu.make_async_copy(p,q,sem.at[i]) for i,(p,q) in enumerate(zip(ins[:5],own[:5]))]
    def part(k,i):
        sl=pl.ds(pl.multiple_of(i*256,256),256)
        return pltpu.make_async_copy(ins[k].at[sl],own[k].at[sl],sem.at[5+3*i+k-5])
    for cp in cin: cp.start()
    for i in range(4):
        for k in (5,6,7): part(k,i).start()
    def block(i):
        for k in (5,6,7): part(k,i).wait()
        sl=pl.ds(pl.multiple_of(i*256,256),256)
        dm=dm_ref[sl,:]
        dh=nn(drb_ref[sl,:],at_ref[...])
        for u in range(3): dh=dh+nt(dm[:,u*1024:u*1024+1024],w_ref[u].reshape(D,D))
        v,s=stats(x_ref[sl,:].astype(F32))
        xh=v*s
        dy=dh*gain_ref[0:1,:]
        dx2_ref[sl,:]=dx2_ref[sl,:]+s*(dy-jnp.mean(dy,axis=-1,keepdims=True)-xh*jnp.mean(dy*xh,axis=-1,keepdims=True))
        pltpu.make_async_copy(dx2_ref.at[sl],ig_out.at[sl],osem.at[i]).start()
    f=lax.axis_index("fsdp"); d=lax.axis_index("dp")
    c=f&1; h=f>>1; b=h&(B-1); a=h>>(B.bit_length()-1)
    def dev(a,b,c,e): return {"fsdp":(a*B+b)*2+c,"dp":e}
    L1,L2=(A,B) if A>=B else (B,A)
    m1,m2=(a,b) if A>=B else (b,a)
    at=(lambda p,q: (p,q)) if A>=B else (lambda p,q: (q,p))
    nb=DP*L2
    me=d*L2+m2
    sib=dev(a,b,1-c,d)
    near=[]
    for k in range(1,nb):
        o=(me+k)&(nb-1)
        near.append(dev(*at(m1,o&(L2-1)),c,o>>(L2.bit_length()-1)))
    far=[dev(*at((m1+k)&(L1-1),m2),c,d) for k in range(1,L1)]
    bar=pltpu.get_barrier_semaphore()
    for p in [sib]+near+far: pl.semaphore_signal(bar,inc=1,device_id=p,device_id_type=MESH)
    pl.semaphore_wait(bar,1+len(near)+len(far))
    def rc(src,dst,k,to): return pltpu.make_async_remote_copy(src_ref=src,dst_ref=dst,send_sem=ss.at[k],recv_sem=rs.at[k],device_id=to,device_id_type=MESH)
    cin[0].wait()
    cps=[rc(g_ref.at[pl.ds(2*(1-c),2)],c_ref,0,sib)]
    cps[0].start()
    for cp in cin[1:]: cp.wait()
    cps[0].wait_recv()
    h_ref[...]=g_ref[pl.ds(2*c,2)]+c_ref[...]
    b_ref[me]=h_ref[...]
    first=[rc(h_ref,b_ref.at[me],k,to) for k,to in enumerate(near,1)]
    for cp in first: cp.start()
    lax.fori_loop(0,1,lambda i,_: (block(i),0)[1],0)
    for cp in first: cp.wait_recv()
    v=b_ref[0]
    for k in range(1,nb): v=v+b_ref[k]
    t_ref[...]=v
    z_ref[m1]=v
    second=[rc(t_ref,z_ref.at[m1],k,to) for k,to in enumerate(far,nb)]
    for cp in second: cp.start()
    lax.fori_loop(1,3,lambda i,_: (block(i),0)[1],0)
    for cp in second: cp.wait_recv()
    v=z_ref[0]
    for k in range(1,L1): v=v+z_ref[k]
    half=o_ref.at[pl.ds(2*c,2)]
    o_ref[pl.ds(2*c,2)]=v
    back=rc(half,half,nb+L1-1,sib)
    back.start()
    lax.fori_loop(3,4,lambda i,_: (block(i),0)[1],0)
    back.wait_recv()
    for cp in cps+first+second+[back]: cp.wait_send()
    for i in range(4):
        sl=slice(i*256,i*256+256)
        pltpu.make_async_copy(dx2_ref.at[sl],ig_out.at[sl],osem.at[i]).wait()
def sum_call(A,B,DP,*ins):
    g=ins[0]
    L1,L2=max(A,B),min(A,B); nb=DP*L2; n=nb+L1
    V=pltpu.VMEM; hs=(2,)+g.shape[1:]
    hbm=pl.BlockSpec(memory_space=pl.ANY)
    sems=pltpu.SemaphoreType.DMA
    return pl.pallas_call(functools.partial(sum_kernel,A,B,DP),in_specs=[hbm]*8,out_specs=[VM,hbm],
      out_shape=[jax.ShapeDtypeStruct(g.shape,F32),jax.ShapeDtypeStruct((T,D),F32)],
      scratch_shapes=[V((3,)+v.shape[1:],v.dtype) if k==3 else V(v.shape,v.dtype) for k,v in enumerate(ins)]+[V(hs,F32),V(hs,F32),V((nb,)+hs,F32),V((L1,)+hs,F32),V(hs,F32),
        sems((n,)),sems((n,)),sems((17,)),sems((4,))],
      compiler_params=pltpu.CompilerParams(collective_id=1,has_side_effects=True,vmem_limit_bytes=61*2**20),name="total")(*ins)

def update_kernel(rate,g_in,m_in,a_in,v_in,ig_in,g_out,m_out,a_out,v_out,c_out,ig_out,g_ref,m_ref,a_ref,v_ref,c_ref,ig_ref,isem,osem):
    small=[pltpu.make_async_copy(p,q,isem.at[i]) for i,(p,q) in enumerate(((g_in,g_ref),(m_in,m_ref),(a_in,a_ref),(v_in,v_ref)))]
    for cp in small: cp.start()
    n=ig_ref.shape[0]//4
    rin=[pltpu.make_async_copy(ig_in.at[i*n:i*n+n],ig_ref.at[i*n:i*n+n],isem.at[4+i]) for i in range(4)]
    rout=[pltpu.make_async_copy(ig_ref.at[i*n:i*n+n],ig_out.at[i*n:i*n+n],osem.at[5+i]) for i in range(4)]
    for cp in rin: cp.start()
    for cp in small: cp.wait()
    g=g_ref[...]
    mom=0.9*m_ref[...]+g
    new=a_ref[...]-rate*(g+0.9*mom)
    m_ref[...]=mom
    a_ref[...]=new
    v_ref[...]=0.9*v_ref[...]+0.1*new
    c_ref[...]=new.astype(BF)
    outs=[pltpu.make_async_copy(p,q,osem.at[i]) for i,(p,q) in enumerate(((g_ref,g_out),(m_ref,m_out),(a_ref,a_out),(v_ref,v_out),(c_ref,c_out)))]
    for cp in outs: cp.start()
    for i in range(4): rin[i].wait(); rout[i].start()
    for cp in outs+rout: cp.wait()
def update_call(rate,g,m,a,v,ig):
    hbm=pl.BlockSpec(memory_space=pl.ANY)
    sd=jax.ShapeDtypeStruct; V=pltpu.VMEM
    return pl.pallas_call(functools.partial(update_kernel,rate),in_specs=[hbm]*5,out_specs=[hbm]*6,
      out_shape=[sd(g.shape,F32)]*4+[sd(g.shape,BF),sd(ig.shape,F32)],
      scratch_shapes=[V(g.shape,F32)]*4+[V(g.shape,BF),V(ig.shape,F32),pltpu.SemaphoreType.DMA((8,)),pltpu.SemaphoreType.DMA((9,))],
      compiler_params=pltpu.CompilerParams(vmem_limit_bytes=61*2**20),name="update")(g,m,a,v,ig)
def solution(mesh):
    F=mesh.shape["fsdp"]; DP=mesh.shape["dp"]
    A,B=(F//4,2) if F<=16 else (2,F//4)
    def per_device(tokens,item_start,og,gains,shifts,wqkv,bqkv,wout,wfc,bfc,wproj,ob,adapters,momentum,average):
        u,qkv,o,lse,r,kl,h1,at,uu,bo,dx2,do=forward_call(A,B,tokens,og,item_start.reshape(8,128),gains,shifts,ob,bqkv.reshape(24,128),bfc.reshape(32,128),
            adapters.transpose(0,2,1),wqkv,wout,wfc,wproj)
        dm,drb,ga,bo=back_call(kl,uu,r,lse,h1,qkv,do,o,bo)
        grad,ig=sum_call(A,B,DP,ga,tokens,gains,u,at,drb,dx2,dm)
        t=lambda v: v.transpose(0,2,1)
        rate=0.01/math.sqrt(tokens.shape[0]*F*DP)
        grad,mom,new,avg,low,ig=update_call(rate,grad,t(momentum),t(adapters),t(average),ig)
        return bo,ig,t(grad),t(mom),t(new),t(avg),t(low)
    rows=P(("fsdp","dp"),None); w=P("fsdp",None); n=P()
    return jax.shard_map(per_device,mesh=mesh,
      in_specs=(rows,P(("fsdp","dp")),rows,n,n,w,n,w,w,n,w,n,n,n,n),out_specs=(rows,rows,n,n,n,n,n),check_vma=False)
```
